128 devices in a mesh: ctx: 8 (over x, z_lo), fsdp: 16 (over z_hi, y, core).
Axes of the slice: x: 4, y: 4, z: 4 (z_hi: 2, z_lo: 2; z = z_hi * 2 + z_lo), core: 2. Of those that a mesh axis runs over, the one named last changes fastest.
Arguments:
- inputs: bfloat16 [16, 1024, 1152], P('fsdp', 'ctx'), may hold values from -6 to 6
- out_grad: bfloat16 [16, 1024, 1152], P('fsdp', 'ctx'), may hold values from -6 to 6
- positions: int32 [16, 1024], P('fsdp', 'ctx'), may hold values from 0 to 1023, as said below
- block_order: int32 [8, 2], replicated, may hold values from 0 to 15, as said below
- w_query: bfloat16 [1152, 1024], P('fsdp'), may hold values from -0.1875 to 0.1875
- w_key: bfloat16 [1152, 256], P('fsdp'), may hold values from -0.1875 to 0.1875
- w_value: bfloat16 [1152, 256], P('fsdp'), may hold values from -0.1875 to 0.1875
- w_output: bfloat16 [1024, 1152], P(None, 'fsdp'), may hold values from -0.1875 to 0.1875
- w_gate: bfloat16 [6912, 1152], P('fsdp'), may hold values from -0.1875 to 0.1875
- w_up: bfloat16 [6912, 1152], P('fsdp'), may hold values from -0.1875 to 0.1875
- w_down: bfloat16 [6912, 1152], P('fsdp'), may hold values from -0.078125 to 0.078125
- gain_in: bfloat16 [1152], P('fsdp'), may hold values from 0.099609375 to 1.8984375
- gain_query: bfloat16 [256], P('fsdp'), may hold values from 0.099609375 to 1.8984375
- gain_key: bfloat16 [256], P('fsdp'), may hold values from 0.099609375 to 1.8984375
- gain_attn: bfloat16 [1152], P('fsdp'), may hold values from 0.099609375 to 1.8984375
- gain_pre: bfloat16 [1152], P('fsdp'), may hold values from 0.099609375 to 1.8984375
- gain_post: bfloat16 [1152], P('fsdp'), may hold values from 0.099609375 to 1.8984375
Outputs:
- outputs: bfloat16 [16, 1024, 1152], P('fsdp', 'ctx')
- in_grad: bfloat16 [16, 1024, 1152], P('fsdp', 'ctx')
- grad_w_query: float32 [1152, 1024], P('fsdp')
- grad_w_key: float32 [1152, 256], P('fsdp')
- grad_w_value: float32 [1152, 256], P('fsdp')
- grad_w_output: float32 [1024, 1152], P(None, 'fsdp')
- grad_w_gate: float32 [6912, 1152], P('fsdp')
- grad_w_up: float32 [6912, 1152], P('fsdp')
- grad_w_down: float32 [6912, 1152], P('fsdp')
- grad_gain_in: float32 [1152], P('fsdp')
- grad_gain_query: float32 [256], P('fsdp')
- grad_gain_key: float32 [256], P('fsdp')
- grad_gain_attn: float32 [1152], P('fsdp')
- grad_gain_pre: float32 [1152], P('fsdp')
- grad_gain_post: float32 [1152], P('fsdp')
The draws below stay inside these ranges and needn't reach their ends.
Inputs may be any that keep to these rules, and one draw needn't show every extreme that they name: `block_order`: row c names the two blocks of 64 tokens in device c's rows, in order; every block appears once, and a row holds blocks k and m with k + m one less than the number of blocks. `positions`: each row's offset from the start of its document in the sequence; documents begin at the sequence's first token and at random places; sequence 0 is one document.
All inputs are finite; a program needn't handle non-finite values.
Results may differ from the reference program's by a relative error of at most 0.03.
Values may be sent and summed in bfloat16 or wider, within the bound.
No kernel may reach another device: no remote copies, remote signals or barrier semaphores. Data moves between devices by JAX's collectives and lax.ppermute only.
A program may use at most 128 MiB of HBM per device.

```python
import jax
import jax.numpy as jnp
from jax import lax

D = 1152
FF = 6912
H = 4
HD = 256
LEN = 1024
BLOCK = 64
SEQS = 16
N_CTX = 8


def block_table(key):
    order = jax.random.permutation(jax.random.fold_in(key, 7), N_CTX).astype(jnp.int32)
    flips = jax.random.randint(jax.random.fold_in(key, 8), (N_CTX,), 0, 2, dtype=jnp.int32)
    first = jnp.where(flips == 1, 2 * N_CTX - 1 - order, order)
    second = 2 * N_CTX - 1 - first
    return jnp.stack([first, second], axis=1).astype(jnp.int32)


def draw_block_order(key, part):
    return block_table(key)


def draw_positions(key, part):
    table = block_table(key)
    steps = jnp.arange(LEN, dtype=jnp.int32)
    marks = jax.random.randint(jax.random.fold_in(key, 9), (SEQS, LEN), 0, LEN, dtype=jnp.int32) < 4
    later = jnp.arange(SEQS, dtype=jnp.int32)[:, None] > 0
    marks = marks & later | (steps[None, :] == 0)
    starts = lax.cummax(jnp.where(marks, steps[None, :], 0), axis=1)
    within = steps[None, :] - starts
    seq_rows = table.reshape(-1)[steps // BLOCK] * BLOCK + steps % BLOCK
    return jnp.take(within, seq_rows, axis=1).astype(jnp.int32)


def level_of(stream_key, dims, pieces, least, high):
    level = 1.0
    for position, blocks in pieces:
        heights = jax.random.uniform(jax.random.fold_in(jax.random.fold_in(stream_key, 6), position), (blocks,), jnp.float32, least / len(pieces), high / len(pieces))
        level = level * jnp.repeat(jnp.exp(heights), dims[position] // blocks).reshape((-1,) + (1,) * (len(dims) - 1 - position))
    return level


def scatter_about(stream_key, extent, deviation, most, pieces=(), kind=jnp.bfloat16):
    result = deviation * jax.random.normal(stream_key, extent, jnp.float32)
    if pieces:
        result = result * level_of(stream_key, extent, pieces, -0.22, 0.18)
    return jnp.clip(result, -most, most).astype(kind)


def setup_inputs(seed: int = 0) -> dict:
    splits = jax.random.split(jax.random.key(seed), 18)
    inputs = scatter_about(splits[0], (SEQS, LEN, D), 1.0, 6.0, ((0, 16), (1, 8)))
    out_grad = scatter_about(splits[1], (SEQS, LEN, D), 1.0, 6.0, ((0, 16), (1, 8)))
    positions = draw_positions(jax.random.fold_in(splits[17], 71), 0)
    block_order = draw_block_order(jax.random.fold_in(splits[17], 71), 0)
    w_query = scatter_about(splits[4], (D, H * HD), D ** -0.5, 0.1875, ((0, 16),))
    w_key = scatter_about(splits[5], (D, HD), D ** -0.5, 0.1875, ((0, 16),))
    w_value = scatter_about(splits[6], (D, HD), D ** -0.5, 0.1875, ((0, 16),))
    w_output = scatter_about(splits[7], (H * HD, D), (H * HD) ** -0.5, 0.1875, ((1, 16),))
    w_gate = scatter_about(splits[8], (FF, D), D ** -0.5, 0.1875, ((0, 16),))
    w_up = scatter_about(splits[9], (FF, D), D ** -0.5, 0.1875, ((0, 16),))
    w_down = scatter_about(splits[10], (FF, D), FF ** -0.5, 0.078125, ((0, 16),))
    gain_in = jnp.clip(1.0 + 0.18 * jax.random.normal(splits[11], (D,), jnp.float32), 0.099609375, 1.8984375).astype(jnp.bfloat16)
    gain_query = jnp.clip(1.0 + 0.18 * jax.random.normal(splits[12], (HD,), jnp.float32), 0.099609375, 1.8984375).astype(jnp.bfloat16)
    gain_key = jnp.clip(1.0 + 0.18 * jax.random.normal(splits[13], (HD,), jnp.float32), 0.099609375, 1.8984375).astype(jnp.bfloat16)
    gain_attn = jnp.clip(1.0 + 0.18 * jax.random.normal(splits[14], (D,), jnp.float32), 0.099609375, 1.8984375).astype(jnp.bfloat16)
    gain_pre = jnp.clip(1.0 + 0.18 * jax.random.normal(splits[15], (D,), jnp.float32), 0.099609375, 1.8984375).astype(jnp.bfloat16)
    gain_post = jnp.clip(1.0 + 0.18 * jax.random.normal(splits[16], (D,), jnp.float32), 0.099609375, 1.8984375).astype(jnp.bfloat16)
    return {"inputs": inputs, "out_grad": out_grad, "positions": positions, "block_order": block_order, "w_query": w_query, "w_key": w_key, "w_value": w_value, "w_output": w_output, "w_gate": w_gate, "w_up": w_up, "w_down": w_down, "gain_in": gain_in, "gain_query": gain_query, "gain_key": gain_key, "gain_attn": gain_attn, "gain_pre": gain_pre, "gain_post": gain_post}


EPS = 1e-06
ROPE_BASE = 1000000.0
GELU_C = 0.7978845608028654
GELU_A = 0.044715

def norm_forward(values, gain):
    inverse = lax.rsqrt(lax.optimization_barrier(jnp.mean(values * values, axis=-1, keepdims=True)) + EPS)
    unit = values * inverse
    return (unit * gain, unit, inverse)

def norm_backward(upstream, unit, inverse, gain):
    scaled = upstream * gain
    inner = lax.optimization_barrier(jnp.mean(scaled * unit, axis=-1, keepdims=True))
    leading = tuple(range(upstream.ndim - 1))
    return (inverse * (scaled - unit * inner), lax.optimization_barrier(jnp.sum(upstream * unit, axis=leading)))

def gelu_pair(gate):
    inner = GELU_C * (gate + GELU_A * gate * gate * gate)
    tangent = jnp.tanh(inner)
    value = 0.5 * gate * (1.0 + tangent)
    slope = 0.5 * (1.0 + tangent) + 0.5 * gate * (1.0 - tangent * tangent) * GELU_C * (1.0 + 3.0 * GELU_A * gate * gate)
    return (value, slope)

def rope_tables(positions, width):
    half = width // 2
    freqs = ROPE_BASE ** (-2.0 * jnp.arange(half, dtype=jnp.float32) / width)
    angles = positions.astype(jnp.float32)[:, None] * freqs[None, :]
    return (jnp.cos(angles), jnp.sin(angles))

def rotate(values, cosine, sine):
    half = values.shape[-1] // 2
    first = values[..., :half]
    second = values[..., half:]
    return jnp.concatenate([first * cosine - second * sine, second * cosine + first * sine], axis=-1)

def rotate_back(values, cosine, sine):
    half = values.shape[-1] // 2
    first = values[..., :half]
    second = values[..., half:]
    return jnp.concatenate([first * cosine + second * sine, second * cosine - first * sine], axis=-1)

def layout_sequence(block_order, total, block):
    rows = jnp.arange(total, dtype=jnp.int32)
    return block_order.reshape(-1)[rows // block] * block + rows % block

def one_sequence(inputs, out_grad, positions, seq_rows, weights, gains):
    w_query, w_key, w_value, w_output, w_gate, w_up, w_down = weights
    gain_in, gain_query, gain_key, gain_attn, gain_pre, gain_post = gains
    f32 = jnp.float32
    low = jnp.bfloat16
    rows = inputs.shape[0]
    flat_in = inputs.astype(f32)
    normed_full, unit_in, inv_in = norm_forward(flat_in, gain_in)
    normed_in = normed_full.astype(low)
    queries = jnp.dot(normed_in, w_query, preferred_element_type=f32).reshape(rows, H, HD)
    keys_raw = jnp.dot(normed_in, w_key, preferred_element_type=f32)
    values = jnp.dot(normed_in, w_value, preferred_element_type=f32).astype(low)
    query_normed, query_unit, query_inv = norm_forward(queries, gain_query)
    key_normed, key_unit, key_inv = norm_forward(keys_raw, gain_key)
    cosine, sine = rope_tables(positions, HD)
    scale = HD ** (-0.5)
    query_rot = (rotate(query_normed, cosine[:, None, :], sine[:, None, :]) * scale).astype(low)
    key_rot = rotate(key_normed, cosine, sine).astype(low)
    scores = jnp.einsum('qhd,kd->hqk', query_rot.astype(f32), key_rot.astype(f32))
    allowed = seq_rows[:, None] >= seq_rows[None, :]
    scores = jnp.where(allowed[None], scores, -jnp.inf)
    highest = lax.optimization_barrier(jnp.max(scores, axis=-1, keepdims=True))
    log_total = highest + jnp.log(lax.optimization_barrier(jnp.sum(jnp.exp(scores - highest), axis=-1, keepdims=True)))
    probs_full = jnp.exp(scores - log_total)
    probs = probs_full.astype(low)
    attended = jnp.einsum('hqk,kd->qhd', probs.astype(f32), values.astype(f32)).reshape(rows, H * HD).astype(low)
    branch_attn = jnp.dot(attended, w_output, preferred_element_type=f32)
    attn_normed, attn_unit, attn_inv = norm_forward(branch_attn, gain_attn)
    residual = flat_in + attn_normed
    pre_full, pre_unit, pre_inv = norm_forward(residual, gain_pre)
    normed_pre = pre_full.astype(low)
    gate = jnp.dot(normed_pre, w_gate.T, preferred_element_type=f32)
    upper = jnp.dot(normed_pre, w_up.T, preferred_element_type=f32)
    gelu_value, gelu_slope = gelu_pair(gate)
    hidden = (gelu_value * upper).astype(low)
    branch_ffn = jnp.dot(hidden, w_down, preferred_element_type=f32)
    post_normed, post_unit, post_inv = norm_forward(branch_ffn, gain_post)
    outputs = (residual + post_normed).astype(low)
    grad_out = out_grad.astype(f32)
    grad_ffn_full, grad_gain_post = norm_backward(grad_out, post_unit, post_inv, gain_post)
    grad_ffn = grad_ffn_full.astype(low)
    grad_hidden = jnp.dot(grad_ffn, w_down.T, preferred_element_type=f32)
    grad_gate = (grad_hidden * upper * gelu_slope).astype(low)
    grad_up = (grad_hidden * gelu_value).astype(low)
    grad_w_down = jnp.dot(hidden.T, grad_ffn, preferred_element_type=f32)
    grad_w_gate = jnp.dot(grad_gate.T, normed_pre, preferred_element_type=f32)
    grad_w_up = jnp.dot(grad_up.T, normed_pre, preferred_element_type=f32)
    grad_pre = jnp.dot(grad_gate, w_gate, preferred_element_type=f32) + jnp.dot(grad_up, w_up, preferred_element_type=f32)
    grad_from_pre, grad_gain_pre = norm_backward(grad_pre, pre_unit, pre_inv, gain_pre)
    grad_residual = grad_out + grad_from_pre
    grad_branch_full, grad_gain_attn = norm_backward(grad_residual, attn_unit, attn_inv, gain_attn)
    grad_branch = grad_branch_full.astype(low)
    grad_w_output = jnp.dot(attended.T, grad_branch, preferred_element_type=f32)
    grad_attended = jnp.dot(grad_branch, w_output.T, preferred_element_type=f32).astype(low)
    grad_heads = grad_attended.reshape(rows, H, HD).astype(f32)
    attended_heads = attended.reshape(rows, H, HD).astype(f32)
    delta = jnp.transpose(lax.optimization_barrier(jnp.sum(grad_heads * attended_heads, axis=-1)))[:, :, None]
    grad_probs = jnp.einsum('qhd,kd->hqk', grad_heads, values.astype(f32))
    grad_scores = (probs_full * (grad_probs - delta)).astype(low)
    grad_values_full = jnp.einsum('hqk,qhd->kd', probs.astype(f32), grad_heads)
    grad_key_rot = jnp.einsum('hqk,qhd->kd', grad_scores.astype(f32), query_rot.astype(f32))
    grad_query_rot = jnp.einsum('hqk,kd->qhd', grad_scores.astype(f32), key_rot.astype(f32))
    grad_q_normed = rotate_back(grad_query_rot * scale, cosine[:, None, :], sine[:, None, :])
    grad_q_full, grad_gain_query = norm_backward(grad_q_normed, query_unit, query_inv, gain_query)
    grad_k_normed = rotate_back(grad_key_rot, cosine, sine)
    grad_k_full, grad_gain_key = norm_backward(grad_k_normed, key_unit, key_inv, gain_key)
    grad_q_in = grad_q_full.reshape(rows, H * HD).astype(low)
    grad_k_in = grad_k_full.astype(low)
    grad_values = grad_values_full.astype(low)
    grad_w_query = jnp.dot(normed_in.T, grad_q_in, preferred_element_type=f32)
    grad_w_key = jnp.dot(normed_in.T, grad_k_in, preferred_element_type=f32)
    grad_w_value = jnp.dot(normed_in.T, grad_values, preferred_element_type=f32)
    grad_normed = jnp.dot(grad_q_in, w_query.T, preferred_element_type=f32) + jnp.dot(grad_k_in, w_key.T, preferred_element_type=f32) + jnp.dot(grad_values, w_value.T, preferred_element_type=f32)
    grad_from_in, grad_gain_in = norm_backward(grad_normed, unit_in, inv_in, gain_in)
    in_grad = (grad_residual + grad_from_in).astype(low)
    grads = (grad_w_query, grad_w_key, grad_w_value, grad_w_output, grad_w_gate, grad_w_up, grad_w_down, grad_gain_in, grad_gain_query, grad_gain_key, grad_gain_attn, grad_gain_pre, grad_gain_post)
    return (outputs, in_grad, grads)

def reference(inputs, out_grad, positions, block_order, w_query, w_key, w_value, w_output, w_gate, w_up, w_down, gain_in, gain_query, gain_key, gain_attn, gain_pre, gain_post):
    seq_rows = layout_sequence(block_order, LEN, BLOCK)
    weights = (w_query, w_key, w_value, w_output, w_gate, w_up, w_down)
    gains = tuple((g.astype(jnp.float32) for g in (gain_in, gain_query, gain_key, gain_attn, gain_pre, gain_post)))
    zeros = tuple((jnp.zeros(w.shape, jnp.float32) for w in weights)) + tuple((jnp.zeros(g.shape, jnp.float32) for g in gains))

    def advance(carry, item):
        outputs, in_grad, grads = one_sequence(item[0], item[1], item[2], seq_rows, weights, gains)
        return (tuple((c + g for c, g in zip(carry, grads))), (outputs, in_grad))
    totals, stacked = lax.scan(advance, zeros, (inputs, out_grad, positions))
    return (stacked[0], stacked[1], totals[0], totals[1], totals[2], totals[3], totals[4], totals[5], totals[6], totals[7], totals[8], totals[9], totals[10], totals[11], totals[12])
```

```python
import jax
import jax.numpy as jnp
from jax import lax
from jax.sharding import PartitionSpec as P

H = 4
HD = 256


EPS = 1e-06
ROPE_BASE = 1000000.0
GELU_C = 0.7978845608028654
GELU_A = 0.044715


def norm_forward(values, gain):
    inverse = lax.rsqrt(jnp.mean(values * values, axis=-1, keepdims=True) + EPS)
    unit = values * inverse
    return (unit * gain, unit, inverse)


def norm_backward(upstream, unit, inverse, gain):
    scaled = upstream * gain
    inner = jnp.mean(scaled * unit, axis=-1, keepdims=True)
    leading = tuple(range(upstream.ndim - 1))
    return (inverse * (scaled - unit * inner), jnp.sum(upstream * unit, axis=leading))


def gelu_pair(gate):
    inner = GELU_C * (gate + GELU_A * gate * gate * gate)
    tangent = jnp.tanh(inner)
    value = 0.5 * gate * (1.0 + tangent)
    slope = 0.5 * (1.0 + tangent) + 0.5 * gate * (1.0 - tangent * tangent) * GELU_C * (
        1.0 + 3.0 * GELU_A * gate * gate
    )
    return (value, slope)


def rope_tables(positions, width):
    half = width // 2
    freqs = ROPE_BASE ** (-2.0 * jnp.arange(half, dtype=jnp.float32) / width)
    angles = positions.astype(jnp.float32)[:, None] * freqs[None, :]
    return (jnp.cos(angles), jnp.sin(angles))


def rotate(values, cosine, sine):
    half = values.shape[-1] // 2
    first = values[..., :half]
    second = values[..., half:]
    return jnp.concatenate(
        [first * cosine - second * sine, second * cosine + first * sine], axis=-1
    )


def rotate_back(values, cosine, sine):
    half = values.shape[-1] // 2
    first = values[..., :half]
    second = values[..., half:]
    return jnp.concatenate(
        [first * cosine + second * sine, second * cosine - first * sine], axis=-1
    )


def sequence_rows(order_flat, first_row, count, block):
    rows = first_row + jnp.arange(count, dtype=jnp.int32)
    slots = rows // block
    table = jnp.arange(order_flat.shape[0], dtype=jnp.int32)
    picked = jnp.sum(jnp.where(slots[:, None] == table[None, :], order_flat[None, :], 0), axis=1)
    return picked * block + rows % block


def pad_rows(shard, rows):
    return jnp.pad(shard, (0, rows - shard.shape[0]))


def body(
    inputs,
    out_grad,
    positions,
    block_order,
    w_query,
    w_key,
    w_value,
    w_output,
    w_gate,
    w_up,
    w_down,
    gain_in,
    gain_query,
    gain_key,
    gain_attn,
    gain_pre,
    gain_post,
):
    f32 = jnp.float32
    low = jnp.bfloat16
    tokens = inputs[0]
    local = tokens.shape[0]
    parts = lax.axis_size("ctx")
    groups = lax.axis_size("fsdp")
    total = local * parts
    block = local // 2
    width_shard = w_query.shape[0]
    qw = w_query.shape[1]
    kw = w_key.shape[1]
    gain_cols = jnp.stack(
        [
            gain_in,
            gain_attn,
            gain_pre,
            gain_post,
            pad_rows(gain_query, width_shard),
            pad_rows(gain_key, width_shard),
        ],
        axis=1,
    )
    gain_cols = jnp.pad(gain_cols, ((0, 0), (0, 128 - gain_cols.shape[1])))
    packed = jnp.concatenate([w_query, w_key, w_value, w_output.T, gain_cols], axis=1)
    packed_all = lax.all_gather(packed, "fsdp", axis=0, tiled=True)
    o1 = qw
    o2 = o1 + kw
    o3 = o2 + kw
    o4 = o3 + w_output.shape[0]
    full_query = packed_all[:, :o1]
    full_key = packed_all[:, o1:o2]
    full_value = packed_all[:, o2:o3]
    full_output_t = packed_all[:, o3:o4]
    gains_all = packed_all[:, o4:].astype(f32)
    head_shard = gain_query.shape[0]

    def head_gain(col):
        return col.reshape(groups, width_shard)[:, :head_shard].reshape(-1)

    norm_in = gains_all[:, 0]
    norm_attn = gains_all[:, 1]
    norm_pre = gains_all[:, 2]
    norm_post = gains_all[:, 3]
    norm_query = head_gain(gains_all[:, 4])
    norm_key = head_gain(gains_all[:, 5])
    ctx_index = lax.axis_index("ctx")
    order_flat = block_order.reshape(-1)
    my_seq = sequence_rows(order_flat, ctx_index * local, local, block)
    all_seq = sequence_rows(order_flat, 0, total, block)
    flat_in = tokens.astype(f32)
    normed_full, unit_in, inv_in = norm_forward(flat_in, norm_in)
    normed_in = normed_full.astype(low)
    queries = jnp.dot(normed_in, full_query, preferred_element_type=f32).reshape(local, H, HD)
    keys_raw = jnp.dot(normed_in, full_key, preferred_element_type=f32)
    values = jnp.dot(normed_in, full_value, preferred_element_type=f32).astype(low)
    query_normed, query_unit, query_inv = norm_forward(queries, norm_query)
    key_normed, key_unit, key_inv = norm_forward(keys_raw, norm_key)
    cosine, sine = rope_tables(positions[0], HD)
    scale = HD ** (-0.5)
    query_rot = (rotate(query_normed, cosine[:, None, :], sine[:, None, :]) * scale).astype(low)
    key_rot = rotate(key_normed, cosine, sine).astype(low)
    kv_all = lax.all_gather(
        jnp.concatenate([key_rot, values], axis=1), "ctx", axis=0, tiled=True
    )
    key_all = kv_all[:, :HD]
    value_all = kv_all[:, HD:]
    scores = jnp.einsum("qhd,kd->hqk", query_rot, key_all, preferred_element_type=f32)
    allowed = my_seq[:, None] >= all_seq[None, :]
    scores = jnp.where(allowed[None], scores, -jnp.inf)
    highest = jnp.max(scores, axis=-1, keepdims=True)
    log_total = highest + jnp.log(jnp.sum(jnp.exp(scores - highest), axis=-1, keepdims=True))
    probs_full = jnp.exp(scores - log_total)
    probs = probs_full.astype(low)
    attended = (
        jnp.einsum("hqk,kd->qhd", probs, value_all, preferred_element_type=f32)
        .reshape(local, H * HD)
        .astype(low)
    )
    branch_attn = jnp.einsum("tc,dc->td", attended, full_output_t, preferred_element_type=f32)
    attn_normed, attn_unit, attn_inv = norm_forward(branch_attn, norm_attn)
    residual = flat_in + attn_normed
    pre_full, pre_unit, pre_inv = norm_forward(residual, norm_pre)
    normed_pre = pre_full.astype(low)
    rows_all = lax.all_gather(normed_pre, "fsdp", axis=0, tiled=True)
    gate = jnp.einsum("td,fd->tf", rows_all, w_gate, preferred_element_type=f32)
    upper = jnp.einsum("td,fd->tf", rows_all, w_up, preferred_element_type=f32)
    gelu_value, gelu_slope = gelu_pair(gate)
    hidden = (gelu_value * upper).astype(low)
    branch_ffn = lax.psum_scatter(
        jnp.dot(hidden, w_down, preferred_element_type=f32).astype(jnp.bfloat16),
        "fsdp",
        scatter_dimension=0,
        tiled=True,
    ).astype(jnp.float32)
    post_normed, post_unit, post_inv = norm_forward(branch_ffn, norm_post)
    outputs = (residual + post_normed).astype(low)
    grad_out = out_grad[0].astype(f32)
    grad_ffn_full, grad_gain_post = norm_backward(grad_out, post_unit, post_inv, norm_post)
    grad_ffn = grad_ffn_full.astype(low)
    grad_all = lax.all_gather(grad_ffn, "fsdp", axis=0, tiled=True)
    grad_hidden = jnp.einsum("td,fd->tf", grad_all, w_down, preferred_element_type=f32)
    grad_gate = (grad_hidden * upper * gelu_slope).astype(low)
    grad_up = (grad_hidden * gelu_value).astype(low)
    shard_gate = jnp.einsum("tf,td->fd", grad_gate, rows_all, preferred_element_type=f32)
    shard_up = jnp.einsum("tf,td->fd", grad_up, rows_all, preferred_element_type=f32)
    shard_down = jnp.einsum("tf,td->fd", hidden, grad_all, preferred_element_type=f32)
    grad_pre = lax.psum_scatter(
        (
            jnp.dot(grad_gate, w_gate, preferred_element_type=f32)
            + jnp.dot(grad_up, w_up, preferred_element_type=f32)
        ).astype(jnp.bfloat16),
        "fsdp",
        scatter_dimension=0,
        tiled=True,
    ).astype(jnp.float32)
    grad_from_pre, grad_gain_pre = norm_backward(grad_pre, pre_unit, pre_inv, norm_pre)
    grad_residual = grad_out + grad_from_pre
    grad_branch_full, grad_gain_attn = norm_backward(grad_residual, attn_unit, attn_inv, norm_attn)
    grad_branch = grad_branch_full.astype(low)
    term_output_t = jnp.einsum("td,tc->dc", grad_branch, attended, preferred_element_type=f32)
    grad_attended = jnp.einsum(
        "td,dc->tc", grad_branch, full_output_t, preferred_element_type=f32
    ).astype(low)
    grad_heads = grad_attended.reshape(local, H, HD)
    attended_heads = attended.reshape(local, H, HD)
    delta = jnp.transpose(jnp.sum(grad_heads.astype(f32) * attended_heads.astype(f32), axis=-1))[
        :, :, None
    ]
    grad_probs = jnp.einsum("qhd,kd->hqk", grad_heads, value_all, preferred_element_type=f32)
    grad_scores = (probs_full * (grad_probs - delta)).astype(low)
    value_term = jnp.einsum("hqk,qhd->kd", probs, grad_heads, preferred_element_type=f32)
    key_term = jnp.einsum("hqk,qhd->kd", grad_scores, query_rot, preferred_element_type=f32)
    key_value_terms = jnp.concatenate([key_term, value_term], axis=1)
    grad_query_rot = jnp.einsum("hqk,kd->qhd", grad_scores, key_all, preferred_element_type=f32)
    summed_kv = lax.psum_scatter(
        key_value_terms.astype(jnp.bfloat16), "ctx", scatter_dimension=0, tiled=True
    ).astype(jnp.float32)
    grad_key_rot = summed_kv[:, :HD]
    grad_values = summed_kv[:, HD:].astype(low)
    grad_q_normed = rotate_back(grad_query_rot * scale, cosine[:, None, :], sine[:, None, :])
    grad_q_full, grad_gain_query = norm_backward(grad_q_normed, query_unit, query_inv, norm_query)
    grad_k_normed = rotate_back(grad_key_rot, cosine, sine)
    grad_k_full, grad_gain_key = norm_backward(grad_k_normed, key_unit, key_inv, norm_key)
    grad_q_in = grad_q_full.reshape(local, H * HD).astype(low)
    grad_k_in = grad_k_full.astype(low)
    term_query = jnp.einsum("td,tc->dc", normed_in, grad_q_in, preferred_element_type=f32)
    term_key = jnp.einsum("td,tc->dc", normed_in, grad_k_in, preferred_element_type=f32)
    term_value = jnp.einsum("td,tc->dc", normed_in, grad_values, preferred_element_type=f32)
    grad_normed = (
        jnp.einsum("tc,dc->td", grad_q_in, full_query, preferred_element_type=f32)
        + jnp.einsum("tc,dc->td", grad_k_in, full_key, preferred_element_type=f32)
        + jnp.einsum("tc,dc->td", grad_values, full_value, preferred_element_type=f32)
    )
    grad_from_in, grad_gain_in = norm_backward(grad_normed, unit_in, inv_in, norm_in)
    in_grad = (grad_residual + grad_from_in).astype(low)

    def head_col(g):
        return jnp.pad(g.reshape(groups, head_shard), ((0, 0), (0, width_shard - head_shard))).reshape(-1)

    grad_gain_cols = jnp.stack(
        [
            grad_gain_in,
            grad_gain_attn,
            grad_gain_pre,
            grad_gain_post,
            head_col(grad_gain_query),
            head_col(grad_gain_key),
        ],
        axis=1,
    )
    grad_gain_cols = jnp.pad(grad_gain_cols, ((0, 0), (0, 128 - grad_gain_cols.shape[1])))
    grad_packed = jnp.concatenate(
        [term_query, term_key, term_value, term_output_t, grad_gain_cols], axis=1
    ).astype(low)
    grad_shard = lax.psum_scatter(grad_packed, "fsdp", scatter_dimension=0, tiled=True)
    totals = lax.psum(
        (grad_shard, shard_gate.astype(low), shard_up.astype(low), shard_down.astype(low)), "ctx"
    )
    grad_shard = totals[0].astype(f32)
    gcols = grad_shard[:, o4:]
    return (
        outputs[None],
        in_grad[None],
        grad_shard[:, :o1],
        grad_shard[:, o1:o2],
        grad_shard[:, o2:o3],
        grad_shard[:, o3:o4].T,
        totals[1].astype(f32),
        totals[2].astype(f32),
        totals[3].astype(f32),
        gcols[:, 0],
        gcols[:head_shard, 4],
        gcols[:head_shard, 5],
        gcols[:, 1],
        gcols[:, 2],
        gcols[:, 3],
    )


def solution(mesh):
    placed = (
        P("fsdp", "ctx", None),
        P("fsdp", "ctx", None),
        P("fsdp", "ctx"),
        P(),
        P("fsdp", None),
        P("fsdp", None),
        P("fsdp", None),
        P(None, "fsdp"),
        P("fsdp", None),
        P("fsdp", None),
        P("fsdp", None),
        P("fsdp"),
        P("fsdp"),
        P("fsdp"),
        P("fsdp"),
        P("fsdp"),
        P("fsdp"),
    )
    return jax.shard_map(
        body,
        mesh=mesh,
        in_specs=placed,
        out_specs=(
            P("fsdp", "ctx", None),
            P("fsdp", "ctx", None),
            P("fsdp", None),
            P("fsdp", None),
            P("fsdp", None),
            P(None, "fsdp"),
            P("fsdp", None),
            P("fsdp", None),
            P("fsdp", None),
            P("fsdp"),
            P("fsdp"),
            P("fsdp"),
            P("fsdp"),
            P("fsdp"),
            P("fsdp"),
        ),
        check_vma=False,
    )
```

```python
import jax
import jax.numpy as jnp
from jax import lax
from jax.sharding import PartitionSpec as P

H = 4
HD = 256


EPS = 1e-06
ROPE_BASE = 1000000.0
GELU_C = 0.7978845608028654
GELU_A = 0.044715


def norm_forward(values, gain):
    inverse = lax.rsqrt(jnp.mean(values * values, axis=-1, keepdims=True) + EPS)
    unit = values * inverse
    return (unit * gain, unit, inverse)


def norm_backward(upstream, unit, inverse, gain):
    scaled = upstream * gain
    inner = jnp.mean(scaled * unit, axis=-1, keepdims=True)
    leading = tuple(range(upstream.ndim - 1))
    return (inverse * (scaled - unit * inner), jnp.sum(upstream * unit, axis=leading))


def gelu_pair(gate):
    inner = GELU_C * (gate + GELU_A * gate * gate * gate)
    tangent = jnp.tanh(inner)
    value = 0.5 * gate * (1.0 + tangent)
    slope = 0.5 * (1.0 + tangent) + 0.5 * gate * (1.0 - tangent * tangent) * GELU_C * (
        1.0 + 3.0 * GELU_A * gate * gate
    )
    return (value, slope)


def rope_tables(positions, width):
    half = width // 2
    freqs = ROPE_BASE ** (-2.0 * jnp.arange(half, dtype=jnp.float32) / width)
    angles = positions.astype(jnp.float32)[:, None] * freqs[None, :]
    return (jnp.cos(angles), jnp.sin(angles))


def rotate(values, cosine, sine):
    half = values.shape[-1] // 2
    first = values[..., :half]
    second = values[..., half:]
    return jnp.concatenate(
        [first * cosine - second * sine, second * cosine + first * sine], axis=-1
    )


def rotate_back(values, cosine, sine):
    half = values.shape[-1] // 2
    first = values[..., :half]
    second = values[..., half:]
    return jnp.concatenate(
        [first * cosine + second * sine, second * cosine - first * sine], axis=-1
    )


def sequence_rows(order_flat, first_row, count, block):
    rows = first_row + jnp.arange(count, dtype=jnp.int32)
    slots = rows // block
    table = jnp.arange(order_flat.shape[0], dtype=jnp.int32)
    picked = jnp.sum(jnp.where(slots[:, None] == table[None, :], order_flat[None, :], 0), axis=1)
    return picked * block + rows % block


def pad_rows(shard, rows):
    return jnp.pad(shard, (0, rows - shard.shape[0]))


def body(
    inputs,
    out_grad,
    positions,
    block_order,
    w_query,
    w_key,
    w_value,
    w_output,
    w_gate,
    w_up,
    w_down,
    gain_in,
    gain_query,
    gain_key,
    gain_attn,
    gain_pre,
    gain_post,
):
    f32 = jnp.float32
    low = jnp.bfloat16
    tokens = inputs[0]
    local = tokens.shape[0]
    parts = lax.axis_size("ctx")
    groups = lax.axis_size("fsdp")
    total = local * parts
    block = local // 2
    width_shard = w_query.shape[0]
    qw = w_query.shape[1]
    kw = w_key.shape[1]
    gain_cols = jnp.stack(
        [
            gain_in,
            gain_attn,
            gain_pre,
            gain_post,
            pad_rows(gain_query, width_shard),
            pad_rows(gain_key, width_shard),
        ],
        axis=1,
    )
    gain_cols = jnp.pad(gain_cols, ((0, 0), (0, 128 - gain_cols.shape[1])))
    packed = jnp.concatenate([w_query, w_key, w_value, w_output.T, gain_cols], axis=1)
    packed_all = lax.all_gather(packed, "fsdp", axis=0, tiled=True)
    o1 = qw
    o2 = o1 + kw
    o3 = o2 + kw
    o4 = o3 + w_output.shape[0]
    full_query = packed_all[:, :o1]
    full_key = packed_all[:, o1:o2]
    full_value = packed_all[:, o2:o3]
    full_output_t = packed_all[:, o3:o4]
    gains_all = packed_all[:, o4:].astype(f32)
    head_shard = gain_query.shape[0]

    def head_gain(col):
        return col.reshape(groups, width_shard)[:, :head_shard].reshape(-1)

    norm_in = gains_all[:, 0]
    norm_attn = gains_all[:, 1]
    norm_pre = gains_all[:, 2]
    norm_post = gains_all[:, 3]
    norm_query = head_gain(gains_all[:, 4])
    norm_key = head_gain(gains_all[:, 5])
    ctx_index = lax.axis_index("ctx")
    order_flat = block_order.reshape(-1)
    my_seq = sequence_rows(order_flat, ctx_index * local, local, block)
    all_seq = sequence_rows(order_flat, 0, total, block)
    flat_in = tokens.astype(f32)
    normed_full, unit_in, inv_in = norm_forward(flat_in, norm_in)
    normed_in = normed_full.astype(low)
    queries = jnp.dot(normed_in, full_query, preferred_element_type=f32).reshape(local, H, HD)
    keys_raw = jnp.dot(normed_in, full_key, preferred_element_type=f32)
    values = jnp.dot(normed_in, full_value, preferred_element_type=f32).astype(low)
    query_normed, query_unit, query_inv = norm_forward(queries, norm_query)
    key_normed, key_unit, key_inv = norm_forward(keys_raw, norm_key)
    cosine, sine = rope_tables(positions[0], HD)
    scale = HD ** (-0.5)
    query_rot = (rotate(query_normed, cosine[:, None, :], sine[:, None, :]) * scale).astype(low)
    key_rot = rotate(key_normed, cosine, sine).astype(low)
    kv_all = lax.all_gather(
        jnp.concatenate([key_rot, values], axis=1), "ctx", axis=0, tiled=True
    )
    key_all = kv_all[:, :HD]
    value_all = kv_all[:, HD:]
    scores = jnp.einsum("qhd,kd->hqk", query_rot, key_all, preferred_element_type=f32)
    allowed = my_seq[:, None] >= all_seq[None, :]
    scores = jnp.where(allowed[None], scores, -jnp.inf)
    highest = jnp.max(scores, axis=-1, keepdims=True)
    log_total = highest + jnp.log(jnp.sum(jnp.exp(scores - highest), axis=-1, keepdims=True))
    probs_full = jnp.exp(scores - log_total)
    probs = probs_full.astype(low)
    attended = (
        jnp.einsum("hqk,kd->qhd", probs, value_all, preferred_element_type=f32)
        .reshape(local, H * HD)
        .astype(low)
    )
    branch_attn = jnp.einsum("tc,dc->td", attended, full_output_t, preferred_element_type=f32)
    attn_normed, attn_unit, attn_inv = norm_forward(branch_attn, norm_attn)
    residual = flat_in + attn_normed
    pre_full, pre_unit, pre_inv = norm_forward(residual, norm_pre)
    normed_pre = pre_full.astype(low)
    rows_all = lax.all_gather(normed_pre, "fsdp", axis=0, tiled=True)
    gate = jnp.einsum("td,fd->tf", rows_all, w_gate, preferred_element_type=f32)
    upper = jnp.einsum("td,fd->tf", rows_all, w_up, preferred_element_type=f32)
    gelu_value, gelu_slope = gelu_pair(gate)
    hidden = (gelu_value * upper).astype(low)
    branch_ffn = lax.psum_scatter(
        jnp.dot(hidden, w_down, preferred_element_type=f32).astype(jnp.bfloat16),
        "fsdp",
        scatter_dimension=0,
        tiled=True,
    ).astype(jnp.float32)
    post_normed, post_unit, post_inv = norm_forward(branch_ffn, norm_post)
    outputs = (residual + post_normed).astype(low)
    grad_out = out_grad[0].astype(f32)
    grad_ffn_full, grad_gain_post = norm_backward(grad_out, post_unit, post_inv, norm_post)
    grad_ffn = grad_ffn_full.astype(low)
    grad_all = lax.all_gather(grad_ffn, "fsdp", axis=0, tiled=True)
    grad_hidden = jnp.einsum("td,fd->tf", grad_all, w_down, preferred_element_type=f32)
    grad_gate = (grad_hidden * upper * gelu_slope).astype(low)
    grad_up = (grad_hidden * gelu_value).astype(low)
    shard_gate = jnp.einsum("tf,td->fd", grad_gate, rows_all, preferred_element_type=f32)
    shard_up = jnp.einsum("tf,td->fd", grad_up, rows_all, preferred_element_type=f32)
    shard_down = jnp.einsum("tf,td->fd", hidden, grad_all, preferred_element_type=f32)
    grad_pre = lax.psum_scatter(
        (
            jnp.dot(grad_gate, w_gate, preferred_element_type=f32)
            + jnp.dot(grad_up, w_up, preferred_element_type=f32)
        ).astype(jnp.bfloat16),
        "fsdp",
        scatter_dimension=0,
        tiled=True,
    ).astype(jnp.float32)
    grad_from_pre, grad_gain_pre = norm_backward(grad_pre, pre_unit, pre_inv, norm_pre)
    grad_residual = grad_out + grad_from_pre
    grad_branch_full, grad_gain_attn = norm_backward(grad_residual, attn_unit, attn_inv, norm_attn)
    grad_branch = grad_branch_full.astype(low)
    term_output = jnp.einsum("tc,td->cd", attended, grad_branch, preferred_element_type=f32)
    grad_attended = jnp.einsum(
        "td,dc->tc", grad_branch, full_output_t, preferred_element_type=f32
    ).astype(low)
    grad_heads = grad_attended.reshape(local, H, HD)
    attended_heads = attended.reshape(local, H, HD)
    delta = jnp.transpose(jnp.sum(grad_heads.astype(f32) * attended_heads.astype(f32), axis=-1))[
        :, :, None
    ]
    grad_probs = jnp.einsum("qhd,kd->hqk", grad_heads, value_all, preferred_element_type=f32)
    grad_scores = (probs_full * (grad_probs - delta)).astype(low)
    value_term = jnp.einsum("hqk,qhd->kd", probs, grad_heads, preferred_element_type=f32)
    key_term = jnp.einsum("hqk,qhd->kd", grad_scores, query_rot, preferred_element_type=f32)
    key_value_terms = jnp.concatenate([key_term, value_term], axis=1)
    grad_query_rot = jnp.einsum("hqk,kd->qhd", grad_scores, key_all, preferred_element_type=f32)
    summed_kv = lax.psum_scatter(
        key_value_terms.astype(jnp.bfloat16), "ctx", scatter_dimension=0, tiled=True
    ).astype(jnp.float32)
    grad_key_rot = summed_kv[:, :HD]
    grad_values = summed_kv[:, HD:].astype(low)
    grad_q_normed = rotate_back(grad_query_rot * scale, cosine[:, None, :], sine[:, None, :])
    grad_q_full, grad_gain_query = norm_backward(grad_q_normed, query_unit, query_inv, norm_query)
    grad_k_normed = rotate_back(grad_key_rot, cosine, sine)
    grad_k_full, grad_gain_key = norm_backward(grad_k_normed, key_unit, key_inv, norm_key)
    grad_q_in = grad_q_full.reshape(local, H * HD).astype(low)
    grad_k_in = grad_k_full.astype(low)
    term_query = jnp.einsum("tc,td->cd", grad_q_in, normed_in, preferred_element_type=f32)
    term_key = jnp.einsum("tc,td->cd", grad_k_in, normed_in, preferred_element_type=f32)
    term_value = jnp.einsum("tc,td->cd", grad_values, normed_in, preferred_element_type=f32)
    grad_normed = (
        jnp.einsum("tc,dc->td", grad_q_in, full_query, preferred_element_type=f32)
        + jnp.einsum("tc,dc->td", grad_k_in, full_key, preferred_element_type=f32)
        + jnp.einsum("tc,dc->td", grad_values, full_value, preferred_element_type=f32)
    )
    grad_from_in, grad_gain_in = norm_backward(grad_normed, unit_in, inv_in, norm_in)
    in_grad = (grad_residual + grad_from_in).astype(low)

    def head_col(g):
        return jnp.pad(g.reshape(groups, head_shard), ((0, 0), (0, width_shard - head_shard))).reshape(-1)

    grad_gain_rows = jnp.stack(
        [
            grad_gain_in,
            grad_gain_attn,
            grad_gain_pre,
            grad_gain_post,
            head_col(grad_gain_query),
            head_col(grad_gain_key),
        ],
        axis=1,
    )
    grad_gain_rows = jnp.pad(grad_gain_rows, ((0, 0), (0, 8 - grad_gain_rows.shape[1]))).T
    grad_packed = jnp.concatenate([term_query, term_key, term_value, term_output], axis=0).astype(low)
    grad_shard = jnp.concatenate(
        [
            lax.psum_scatter(grad_packed, "fsdp", scatter_dimension=1, tiled=True),
            lax.psum_scatter(grad_gain_rows.astype(low), "fsdp", scatter_dimension=1, tiled=True),
        ],
        axis=0,
    )
    totals = lax.psum(
        (grad_shard, shard_gate.astype(low), shard_up.astype(low), shard_down.astype(low)), "ctx"
    )
    grad_shard = totals[0].astype(f32)
    grows = grad_shard[o4:]
    return (
        outputs[None],
        in_grad[None],
        grad_shard[:o1].T,
        grad_shard[o1:o2].T,
        grad_shard[o2:o3].T,
        grad_shard[o3:o4],
        totals[1].astype(f32),
        totals[2].astype(f32),
        totals[3].astype(f32),
        grows[0],
        grows[4, :head_shard],
        grows[5, :head_shard],
        grows[1],
        grows[2],
        grows[3],
    )


def solution(mesh):
    placed = (
        P("fsdp", "ctx", None),
        P("fsdp", "ctx", None),
        P("fsdp", "ctx"),
        P(),
        P("fsdp", None),
        P("fsdp", None),
        P("fsdp", None),
        P(None, "fsdp"),
        P("fsdp", None),
        P("fsdp", None),
        P("fsdp", None),
        P("fsdp"),
        P("fsdp"),
        P("fsdp"),
        P("fsdp"),
        P("fsdp"),
        P("fsdp"),
    )
    return jax.shard_map(
        body,
        mesh=mesh,
        in_specs=placed,
        out_specs=(
            P("fsdp", "ctx", None),
            P("fsdp", "ctx", None),
            P("fsdp", None),
            P("fsdp", None),
            P("fsdp", None),
            P(None, "fsdp"),
            P("fsdp", None),
            P("fsdp", None),
            P("fsdp", None),
            P("fsdp"),
            P("fsdp"),
            P("fsdp"),
            P("fsdp"),
            P("fsdp"),
            P("fsdp"),
        ),
        check_vma=False,
    )
```

```python
import jax
import jax.numpy as jnp
from jax import lax
from jax.sharding import PartitionSpec as P

H = 4
HD = 256


EPS = 1e-06
ROPE_BASE = 1000000.0
GELU_C = 0.7978845608028654
GELU_A = 0.044715


def norm_forward(values, gain):
    inverse = lax.rsqrt(jnp.mean(values * values, axis=-1, keepdims=True) + EPS)
    unit = values * inverse
    return (unit * gain, unit, inverse)


def norm_backward(upstream, unit, inverse, gain):
    scaled = upstream * gain
    inner = jnp.mean(scaled * unit, axis=-1, keepdims=True)
    leading = tuple(range(upstream.ndim - 1))
    return (inverse * (scaled - unit * inner), jnp.sum(upstream * unit, axis=leading))


def gelu_pair(gate):
    inner = GELU_C * (gate + GELU_A * gate * gate * gate)
    tangent = jnp.tanh(inner)
    value = 0.5 * gate * (1.0 + tangent)
    slope = 0.5 * (1.0 + tangent) + 0.5 * gate * (1.0 - tangent * tangent) * GELU_C * (
        1.0 + 3.0 * GELU_A * gate * gate
    )
    return (value, slope)


def rope_tables(positions, width):
    half = width // 2
    freqs = ROPE_BASE ** (-2.0 * jnp.arange(half, dtype=jnp.float32) / width)
    angles = positions.astype(jnp.float32)[:, None] * freqs[None, :]
    return (jnp.cos(angles), jnp.sin(angles))


def rotate(values, cosine, sine):
    half = values.shape[-1] // 2
    first = values[..., :half]
    second = values[..., half:]
    return jnp.concatenate(
        [first * cosine - second * sine, second * cosine + first * sine], axis=-1
    )


def rotate_back(values, cosine, sine):
    half = values.shape[-1] // 2
    first = values[..., :half]
    second = values[..., half:]
    return jnp.concatenate(
        [first * cosine + second * sine, second * cosine - first * sine], axis=-1
    )


def sequence_rows(order_flat, first_row, count, block):
    rows = first_row + jnp.arange(count, dtype=jnp.int32)
    slots = rows // block
    table = jnp.arange(order_flat.shape[0], dtype=jnp.int32)
    picked = jnp.sum(jnp.where(slots[:, None] == table[None, :], order_flat[None, :], 0), axis=1)
    return picked * block + rows % block


def pad_rows(shard, rows):
    return jnp.pad(shard, (0, rows - shard.shape[0]))


def body(
    inputs,
    out_grad,
    positions,
    block_order,
    w_query,
    w_key,
    w_value,
    w_output,
    w_gate,
    w_up,
    w_down,
    gain_in,
    gain_query,
    gain_key,
    gain_attn,
    gain_pre,
    gain_post,
):
    f32 = jnp.float32
    low = jnp.bfloat16
    tokens = inputs[0]
    local = tokens.shape[0]
    parts = lax.axis_size("ctx")
    groups = lax.axis_size("fsdp")
    total = local * parts
    block = local // 2
    width_shard = w_query.shape[0]
    qw = w_query.shape[1]
    kw = w_key.shape[1]
    gain_cols = jnp.stack(
        [
            gain_in,
            gain_attn,
            gain_pre,
            gain_post,
            pad_rows(gain_query, width_shard),
            pad_rows(gain_key, width_shard),
        ],
        axis=1,
    )
    gain_cols = jnp.pad(gain_cols, ((0, 0), (0, 128 - gain_cols.shape[1])))
    packed = jnp.concatenate([w_query, w_key, w_value, w_output.T, gain_cols], axis=1)
    packed_all = lax.all_gather(packed, "fsdp", axis=0, tiled=True)
    o1 = qw
    o2 = o1 + kw
    o3 = o2 + kw
    o4 = o3 + w_output.shape[0]
    full_query = packed_all[:, :o1]
    full_key = packed_all[:, o1:o2]
    full_value = packed_all[:, o2:o3]
    full_output_t = packed_all[:, o3:o4]
    gains_all = packed_all[:, o4:].astype(f32)
    head_shard = gain_query.shape[0]

    def head_gain(col):
        return col.reshape(groups, width_shard)[:, :head_shard].reshape(-1)

    norm_in = gains_all[:, 0]
    norm_attn = gains_all[:, 1]
    norm_pre = gains_all[:, 2]
    norm_post = gains_all[:, 3]
    norm_query = head_gain(gains_all[:, 4])
    norm_key = head_gain(gains_all[:, 5])
    ctx_index = lax.axis_index("ctx")
    order_flat = block_order.reshape(-1)
    my_seq = sequence_rows(order_flat, ctx_index * local, local, block)
    all_seq = sequence_rows(order_flat, 0, total, block)
    flat_in = tokens.astype(f32)
    normed_full, unit_in, inv_in = norm_forward(flat_in, norm_in)
    normed_in = normed_full.astype(low)
    queries = jnp.dot(normed_in, full_query, preferred_element_type=f32).reshape(local, H, HD)
    keys_raw = jnp.dot(normed_in, full_key, preferred_element_type=f32)
    values = jnp.dot(normed_in, full_value, preferred_element_type=f32).astype(low)
    query_normed, query_unit, query_inv = norm_forward(queries, norm_query)
    key_normed, key_unit, key_inv = norm_forward(keys_raw, norm_key)
    cosine, sine = rope_tables(positions[0], HD)
    scale = HD ** (-0.5)
    query_rot = (rotate(query_normed, cosine[:, None, :], sine[:, None, :]) * scale).astype(low)
    key_rot = rotate(key_normed, cosine, sine).astype(low)
    kv_all = lax.all_gather(
        jnp.concatenate([key_rot, values], axis=1), "ctx", axis=0, tiled=True
    )
    key_all = kv_all[:, :HD]
    value_all = kv_all[:, HD:]
    scores = jnp.einsum("qhd,kd->hqk", query_rot, key_all, preferred_element_type=f32)
    allowed = my_seq[:, None] >= all_seq[None, :]
    scores = jnp.where(allowed[None], scores, -jnp.inf)
    highest = jnp.max(scores, axis=-1, keepdims=True)
    log_total = highest + jnp.log(jnp.sum(jnp.exp(scores - highest), axis=-1, keepdims=True))
    probs_full = jnp.exp(scores - log_total)
    probs = probs_full.astype(low)
    attended = (
        jnp.einsum("hqk,kd->qhd", probs, value_all, preferred_element_type=f32)
        .reshape(local, H * HD)
        .astype(low)
    )
    branch_attn = jnp.einsum("tc,dc->td", attended, full_output_t, preferred_element_type=f32)
    attn_normed, attn_unit, attn_inv = norm_forward(branch_attn, norm_attn)
    residual = flat_in + attn_normed
    pre_full, pre_unit, pre_inv = norm_forward(residual, norm_pre)
    normed_pre = pre_full.astype(low)
    rows_all = lax.all_gather(normed_pre, "fsdp", axis=0, tiled=True)
    gate = jnp.einsum("td,fd->tf", rows_all, w_gate, preferred_element_type=f32)
    upper = jnp.einsum("td,fd->tf", rows_all, w_up, preferred_element_type=f32)
    gelu_value, gelu_slope = gelu_pair(gate)
    hidden = (gelu_value * upper).astype(low)
    branch_ffn = lax.psum_scatter(
        jnp.dot(hidden, w_down, preferred_element_type=f32).astype(jnp.bfloat16),
        "fsdp",
        scatter_dimension=0,
        tiled=True,
    ).astype(jnp.float32)
    post_normed, post_unit, post_inv = norm_forward(branch_ffn, norm_post)
    outputs = (residual + post_normed).astype(low)
    grad_out = out_grad[0].astype(f32)
    grad_ffn_full, grad_gain_post = norm_backward(grad_out, post_unit, post_inv, norm_post)
    grad_ffn = grad_ffn_full.astype(low)
    grad_all = lax.all_gather(grad_ffn, "fsdp", axis=0, tiled=True)
    grad_hidden = jnp.einsum("td,fd->tf", grad_all, w_down, preferred_element_type=f32)
    grad_gate = (grad_hidden * upper * gelu_slope).astype(low)
    grad_up = (grad_hidden * gelu_value).astype(low)
    shard_gate = jnp.einsum("tf,td->fd", grad_gate, rows_all, preferred_element_type=f32)
    shard_up = jnp.einsum("tf,td->fd", grad_up, rows_all, preferred_element_type=f32)
    shard_down = jnp.einsum("tf,td->fd", hidden, grad_all, preferred_element_type=f32)
    grad_pre = lax.psum_scatter(
        (
            jnp.dot(grad_gate, w_gate, preferred_element_type=f32)
            + jnp.dot(grad_up, w_up, preferred_element_type=f32)
        ).astype(jnp.bfloat16),
        "fsdp",
        scatter_dimension=0,
        tiled=True,
    ).astype(jnp.float32)
    grad_from_pre, grad_gain_pre = norm_backward(grad_pre, pre_unit, pre_inv, norm_pre)
    grad_residual = grad_out + grad_from_pre
    grad_branch_full, grad_gain_attn = norm_backward(grad_residual, attn_unit, attn_inv, norm_attn)
    grad_branch = grad_branch_full.astype(low)
    term_output = jnp.einsum("tc,td->cd", attended, grad_branch, preferred_element_type=f32)
    grad_attended = jnp.einsum(
        "td,dc->tc", grad_branch, full_output_t, preferred_element_type=f32
    ).astype(low)
    grad_heads = grad_attended.reshape(local, H, HD)
    attended_heads = attended.reshape(local, H, HD)
    delta = jnp.transpose(jnp.sum(grad_heads.astype(f32) * attended_heads.astype(f32), axis=-1))[
        :, :, None
    ]
    grad_probs = jnp.einsum("qhd,kd->hqk", grad_heads, value_all, preferred_element_type=f32)
    grad_scores = (probs_full * (grad_probs - delta)).astype(low)
    value_term = jnp.einsum("hqk,qhd->kd", probs, grad_heads, preferred_element_type=f32)
    key_term = jnp.einsum("hqk,qhd->kd", grad_scores, query_rot, preferred_element_type=f32)
    key_value_terms = jnp.concatenate([key_term, value_term], axis=1)
    grad_query_rot = jnp.einsum("hqk,kd->qhd", grad_scores, key_all, preferred_element_type=f32)
    summed_kv = lax.psum_scatter(
        key_value_terms.astype(jnp.bfloat16), "ctx", scatter_dimension=0, tiled=True
    ).astype(jnp.float32)
    grad_key_rot = summed_kv[:, :HD]
    grad_values = summed_kv[:, HD:].astype(low)
    grad_q_normed = rotate_back(grad_query_rot * scale, cosine[:, None, :], sine[:, None, :])
    grad_q_full, grad_gain_query = norm_backward(grad_q_normed, query_unit, query_inv, norm_query)
    grad_k_normed = rotate_back(grad_key_rot, cosine, sine)
    grad_k_full, grad_gain_key = norm_backward(grad_k_normed, key_unit, key_inv, norm_key)
    grad_q_in = grad_q_full.reshape(local, H * HD).astype(low)
    grad_k_in = grad_k_full.astype(low)
    term_query = jnp.einsum("tc,td->cd", grad_q_in, normed_in, preferred_element_type=f32)
    term_key = jnp.einsum("tc,td->cd", grad_k_in, normed_in, preferred_element_type=f32)
    term_value = jnp.einsum("tc,td->cd", grad_values, normed_in, preferred_element_type=f32)
    grad_normed = (
        jnp.einsum("tc,dc->td", grad_q_in, full_query, preferred_element_type=f32)
        + jnp.einsum("tc,dc->td", grad_k_in, full_key, preferred_element_type=f32)
        + jnp.einsum("tc,dc->td", grad_values, full_value, preferred_element_type=f32)
    )
    grad_from_in, grad_gain_in = norm_backward(grad_normed, unit_in, inv_in, norm_in)
    in_grad = (grad_residual + grad_from_in).astype(low)

    def head_col(g):
        return jnp.pad(g.reshape(groups, head_shard), ((0, 0), (0, width_shard - head_shard))).reshape(-1)

    grad_gain_rows = jnp.stack(
        [
            grad_gain_in,
            grad_gain_attn,
            grad_gain_pre,
            grad_gain_post,
            head_col(grad_gain_query),
            head_col(grad_gain_key),
        ],
        axis=1,
    )
    grad_gain_rows = jnp.pad(grad_gain_rows, ((0, 0), (0, 8 - grad_gain_rows.shape[1]))).T
    grad_packed = jnp.concatenate([term_query, term_key, term_value, term_output], axis=0).astype(low)
    grad_shard = jnp.concatenate(
        [
            lax.psum_scatter(grad_packed, "fsdp", scatter_dimension=1, tiled=True),
            lax.psum_scatter(grad_gain_rows.astype(low), "fsdp", scatter_dimension=1, tiled=True),
        ],
        axis=0,
    )
    ffn_units = shard_gate.shape[0]
    ffn_parts = jnp.concatenate([shard_gate, shard_up, shard_down], axis=0).astype(low)
    ffn_parts = ffn_parts.reshape(parts, -1, ffn_parts.shape[1])
    ffn_mine = jnp.sum(
        lax.all_to_all(ffn_parts, "ctx", 0, 0).astype(f32), axis=0
    ).astype(low)
    ffn_sums = lax.all_to_all(
        jnp.broadcast_to(ffn_mine[None], ffn_parts.shape), "ctx", 0, 0
    ).reshape(3 * ffn_units, -1).astype(f32)
    totals = (
        lax.psum(grad_shard, "ctx"),
        ffn_sums[:ffn_units],
        ffn_sums[ffn_units : 2 * ffn_units],
        ffn_sums[2 * ffn_units :],
    )
    grad_shard = totals[0].astype(f32)
    grows = grad_shard[o4:]
    return (
        outputs[None],
        in_grad[None],
        grad_shard[:o1].T,
        grad_shard[o1:o2].T,
        grad_shard[o2:o3].T,
        grad_shard[o3:o4],
        totals[1].astype(f32),
        totals[2].astype(f32),
        totals[3].astype(f32),
        grows[0],
        grows[4, :head_shard],
        grows[5, :head_shard],
        grows[1],
        grows[2],
        grows[3],
    )


def solution(mesh):
    placed = (
        P("fsdp", "ctx", None),
        P("fsdp", "ctx", None),
        P("fsdp", "ctx"),
        P(),
        P("fsdp", None),
        P("fsdp", None),
        P("fsdp", None),
        P(None, "fsdp"),
        P("fsdp", None),
        P("fsdp", None),
        P("fsdp", None),
        P("fsdp"),
        P("fsdp"),
        P("fsdp"),
        P("fsdp"),
        P("fsdp"),
        P("fsdp"),
    )
    return jax.shard_map(
        body,
        mesh=mesh,
        in_specs=placed,
        out_specs=(
            P("fsdp", "ctx", None),
            P("fsdp", "ctx", None),
            P("fsdp", None),
            P("fsdp", None),
            P("fsdp", None),
            P(None, "fsdp"),
            P("fsdp", None),
            P("fsdp", None),
            P("fsdp", None),
            P("fsdp"),
            P("fsdp"),
            P("fsdp"),
            P("fsdp"),
            P("fsdp"),
            P("fsdp"),
        ),
        check_vma=False,
    )
```

```python
import jax
import jax.numpy as jnp
from jax import lax
from jax.sharding import PartitionSpec as P

H = 4
HD = 256


EPS = 1e-06
ROPE_BASE = 1000000.0
GELU_C = 0.7978845608028654
GELU_A = 0.044715


def norm_forward(values, gain):
    inverse = lax.rsqrt(jnp.mean(values * values, axis=-1, keepdims=True) + EPS)
    unit = values * inverse
    return (unit * gain, unit, inverse)


def norm_backward(upstream, unit, inverse, gain):
    scaled = upstream * gain
    inner = jnp.mean(scaled * unit, axis=-1, keepdims=True)
    leading = tuple(range(upstream.ndim - 1))
    return (inverse * (scaled - unit * inner), jnp.sum(upstream * unit, axis=leading))


def gelu_pair(gate):
    inner = GELU_C * (gate + GELU_A * gate * gate * gate)
    tangent = jnp.tanh(inner)
    value = 0.5 * gate * (1.0 + tangent)
    slope = 0.5 * (1.0 + tangent) + 0.5 * gate * (1.0 - tangent * tangent) * GELU_C * (
        1.0 + 3.0 * GELU_A * gate * gate
    )
    return (value, slope)


def rope_tables(positions, width):
    half = width // 2
    freqs = ROPE_BASE ** (-2.0 * jnp.arange(half, dtype=jnp.float32) / width)
    angles = positions.astype(jnp.float32)[:, None] * freqs[None, :]
    return (jnp.cos(angles), jnp.sin(angles))


def rotate(values, cosine, sine):
    half = values.shape[-1] // 2
    first = values[..., :half]
    second = values[..., half:]
    return jnp.concatenate(
        [first * cosine - second * sine, second * cosine + first * sine], axis=-1
    )


def rotate_back(values, cosine, sine):
    half = values.shape[-1] // 2
    first = values[..., :half]
    second = values[..., half:]
    return jnp.concatenate(
        [first * cosine + second * sine, second * cosine - first * sine], axis=-1
    )


def sequence_rows(order_flat, first_row, count, block):
    rows = first_row + jnp.arange(count, dtype=jnp.int32)
    slots = rows // block
    table = jnp.arange(order_flat.shape[0], dtype=jnp.int32)
    picked = jnp.sum(jnp.where(slots[:, None] == table[None, :], order_flat[None, :], 0), axis=1)
    return picked * block + rows % block


def pad_rows(shard, rows):
    return jnp.pad(shard, (0, rows - shard.shape[0]))


def body(
    inputs,
    out_grad,
    positions,
    block_order,
    w_query,
    w_key,
    w_value,
    w_output,
    w_gate,
    w_up,
    w_down,
    gain_in,
    gain_query,
    gain_key,
    gain_attn,
    gain_pre,
    gain_post,
):
    f32 = jnp.float32
    low = jnp.bfloat16
    tokens = inputs[0]
    local = tokens.shape[0]
    parts = lax.axis_size("ctx")
    groups = lax.axis_size("fsdp")
    total = local * parts
    block = local // 2
    width_shard = w_query.shape[0]
    qw = w_query.shape[1]
    kw = w_key.shape[1]
    gain_cols = jnp.stack(
        [
            gain_in,
            gain_attn,
            gain_pre,
            gain_post,
            pad_rows(gain_query, width_shard),
            pad_rows(gain_key, width_shard),
        ],
        axis=1,
    )
    gain_cols = jnp.pad(gain_cols, ((0, 0), (0, 128 - gain_cols.shape[1])))
    packed = jnp.concatenate([w_query, w_key, w_value, w_output.T, gain_cols], axis=1)
    packed_all = lax.all_gather(packed, "fsdp", axis=0, tiled=True)
    o1 = qw
    o2 = o1 + kw
    o3 = o2 + kw
    o4 = o3 + w_output.shape[0]
    full_query = packed_all[:, :o1]
    full_key = packed_all[:, o1:o2]
    full_value = packed_all[:, o2:o3]
    full_output_t = packed_all[:, o3:o4]
    gains_all = packed_all[:, o4:].astype(f32)
    head_shard = gain_query.shape[0]

    def head_gain(col):
        return col.reshape(groups, width_shard)[:, :head_shard].reshape(-1)

    norm_in = gains_all[:, 0]
    norm_attn = gains_all[:, 1]
    norm_pre = gains_all[:, 2]
    norm_post = gains_all[:, 3]
    norm_query = head_gain(gains_all[:, 4])
    norm_key = head_gain(gains_all[:, 5])
    ctx_index = lax.axis_index("ctx")
    order_flat = block_order.reshape(-1)
    my_seq = sequence_rows(order_flat, ctx_index * local, local, block)
    all_seq = sequence_rows(order_flat, 0, total, block)
    flat_in = tokens.astype(f32)
    normed_full, unit_in, inv_in = norm_forward(flat_in, norm_in)
    normed_in = normed_full.astype(low)
    queries = jnp.dot(normed_in, full_query, preferred_element_type=f32).reshape(local, H, HD)
    keys_raw = jnp.dot(normed_in, full_key, preferred_element_type=f32)
    values = jnp.dot(normed_in, full_value, preferred_element_type=f32).astype(low)
    query_normed, query_unit, query_inv = norm_forward(queries, norm_query)
    key_normed, key_unit, key_inv = norm_forward(keys_raw, norm_key)
    cosine, sine = rope_tables(positions[0], HD)
    scale = HD ** (-0.5)
    query_rot = (rotate(query_normed, cosine[:, None, :], sine[:, None, :]) * scale).astype(low)
    key_rot = rotate(key_normed, cosine, sine).astype(low)
    kv_all = lax.all_gather(
        jnp.concatenate([key_rot, values], axis=1), "ctx", axis=0, tiled=True
    )
    key_all = kv_all[:, :HD]
    value_all = kv_all[:, HD:]
    scores = jnp.einsum("qhd,kd->hqk", query_rot, key_all, preferred_element_type=f32)
    allowed = my_seq[:, None] >= all_seq[None, :]
    scores = jnp.where(allowed[None], scores, -jnp.inf)
    highest = jnp.max(scores, axis=-1, keepdims=True)
    log_total = highest + jnp.log(jnp.sum(jnp.exp(scores - highest), axis=-1, keepdims=True))
    probs_full = jnp.exp(scores - log_total)
    probs = probs_full.astype(low)
    attended = (
        jnp.einsum("hqk,kd->qhd", probs, value_all, preferred_element_type=f32)
        .reshape(local, H * HD)
        .astype(low)
    )
    branch_attn = jnp.einsum("tc,dc->td", attended, full_output_t, preferred_element_type=f32)
    attn_normed, attn_unit, attn_inv = norm_forward(branch_attn, norm_attn)
    residual = flat_in + attn_normed
    pre_full, pre_unit, pre_inv = norm_forward(residual, norm_pre)
    normed_pre = pre_full.astype(low)
    rows_all = lax.all_gather(normed_pre, "fsdp", axis=0, tiled=True)
    gate = jnp.einsum("td,fd->tf", rows_all, w_gate, preferred_element_type=f32)
    upper = jnp.einsum("td,fd->tf", rows_all, w_up, preferred_element_type=f32)
    gelu_value, gelu_slope = gelu_pair(gate)
    hidden = (gelu_value * upper).astype(low)
    branch_ffn = lax.psum_scatter(
        jnp.dot(hidden, w_down, preferred_element_type=f32).astype(jnp.bfloat16),
        "fsdp",
        scatter_dimension=0,
        tiled=True,
    ).astype(jnp.float32)
    post_normed, post_unit, post_inv = norm_forward(branch_ffn, norm_post)
    outputs = (residual + post_normed).astype(low)
    grad_out = out_grad[0].astype(f32)
    grad_ffn_full, grad_gain_post = norm_backward(grad_out, post_unit, post_inv, norm_post)
    grad_ffn = grad_ffn_full.astype(low)
    grad_all = lax.all_gather(grad_ffn, "fsdp", axis=0, tiled=True)
    grad_hidden = jnp.einsum("td,fd->tf", grad_all, w_down, preferred_element_type=f32)
    grad_gate = (grad_hidden * upper * gelu_slope).astype(low)
    grad_up = (grad_hidden * gelu_value).astype(low)
    shard_gate = jnp.einsum("tf,td->fd", grad_gate, rows_all, preferred_element_type=f32)
    shard_up = jnp.einsum("tf,td->fd", grad_up, rows_all, preferred_element_type=f32)
    shard_down = jnp.einsum("tf,td->fd", hidden, grad_all, preferred_element_type=f32)
    grad_pre = lax.psum_scatter(
        (
            jnp.dot(grad_gate, w_gate, preferred_element_type=f32)
            + jnp.dot(grad_up, w_up, preferred_element_type=f32)
        ).astype(jnp.bfloat16),
        "fsdp",
        scatter_dimension=0,
        tiled=True,
    ).astype(jnp.float32)
    grad_from_pre, grad_gain_pre = norm_backward(grad_pre, pre_unit, pre_inv, norm_pre)
    grad_residual = grad_out + grad_from_pre
    grad_branch_full, grad_gain_attn = norm_backward(grad_residual, attn_unit, attn_inv, norm_attn)
    grad_branch = grad_branch_full.astype(low)
    term_output = jnp.einsum("tc,td->cd", attended, grad_branch, preferred_element_type=f32)
    grad_attended = jnp.einsum(
        "td,dc->tc", grad_branch, full_output_t, preferred_element_type=f32
    ).astype(low)
    grad_heads = grad_attended.reshape(local, H, HD)
    attended_heads = attended.reshape(local, H, HD)
    delta = jnp.transpose(jnp.sum(grad_heads.astype(f32) * attended_heads.astype(f32), axis=-1))[
        :, :, None
    ]
    grad_probs = jnp.einsum("qhd,kd->hqk", grad_heads, value_all, preferred_element_type=f32)
    grad_scores = (probs_full * (grad_probs - delta)).astype(low)
    value_term = jnp.einsum("hqk,qhd->kd", probs, grad_heads, preferred_element_type=f32)
    key_term = jnp.einsum("hqk,qhd->kd", grad_scores, query_rot, preferred_element_type=f32)
    key_value_terms = jnp.concatenate([key_term, value_term], axis=1)
    grad_query_rot = jnp.einsum("hqk,kd->qhd", grad_scores, key_all, preferred_element_type=f32)
    summed_kv = lax.psum_scatter(
        key_value_terms.astype(jnp.bfloat16), "ctx", scatter_dimension=0, tiled=True
    ).astype(jnp.float32)
    grad_key_rot = summed_kv[:, :HD]
    grad_values = summed_kv[:, HD:].astype(low)
    grad_q_normed = rotate_back(grad_query_rot * scale, cosine[:, None, :], sine[:, None, :])
    grad_q_full, grad_gain_query = norm_backward(grad_q_normed, query_unit, query_inv, norm_query)
    grad_k_normed = rotate_back(grad_key_rot, cosine, sine)
    grad_k_full, grad_gain_key = norm_backward(grad_k_normed, key_unit, key_inv, norm_key)
    grad_q_in = grad_q_full.reshape(local, H * HD).astype(low)
    grad_k_in = grad_k_full.astype(low)
    term_query = jnp.einsum("tc,td->cd", grad_q_in, normed_in, preferred_element_type=f32)
    term_key = jnp.einsum("tc,td->cd", grad_k_in, normed_in, preferred_element_type=f32)
    term_value = jnp.einsum("tc,td->cd", grad_values, normed_in, preferred_element_type=f32)
    grad_normed = (
        jnp.einsum("tc,dc->td", grad_q_in, full_query, preferred_element_type=f32)
        + jnp.einsum("tc,dc->td", grad_k_in, full_key, preferred_element_type=f32)
        + jnp.einsum("tc,dc->td", grad_values, full_value, preferred_element_type=f32)
    )
    grad_from_in, grad_gain_in = norm_backward(grad_normed, unit_in, inv_in, norm_in)
    in_grad = (grad_residual + grad_from_in).astype(low)

    def head_col(g):
        return jnp.pad(g.reshape(groups, head_shard), ((0, 0), (0, width_shard - head_shard))).reshape(-1)

    gain_block = jnp.stack(
        [
            grad_gain_in,
            grad_gain_attn,
            grad_gain_pre,
            grad_gain_post,
            head_col(grad_gain_query),
            head_col(grad_gain_key),
        ],
        axis=0,
    )
    gain_block = jnp.pad(gain_block, ((0, 8 - gain_block.shape[0]), (0, 0))).astype(low)
    gain_block = jnp.transpose(gain_block.reshape(8, groups, width_shard), (1, 0, 2))
    gain_shard = jnp.sum(lax.all_to_all(gain_block, "fsdp", 0, 0).astype(f32), axis=0)

    def ctx_sum(x):
        chunks = x.reshape(parts, -1, x.shape[1])
        mine = jnp.sum(lax.all_to_all(chunks, "ctx", 0, 0).astype(f32), axis=0).astype(low)
        return lax.all_to_all(jnp.broadcast_to(mine[None], chunks.shape), "ctx", 0, 0).reshape(x.shape)

    ffn_units = shard_gate.shape[0]
    ffn_sums = ctx_sum(
        jnp.concatenate([shard_gate, shard_up, shard_down], axis=0).astype(low)
    ).astype(f32)
    grad_packed = jnp.concatenate([term_query, term_key, term_value, term_output], axis=0).astype(low)
    grad_shard = jnp.concatenate(
        [
            lax.psum_scatter(grad_packed, "fsdp", scatter_dimension=1, tiled=True),
            gain_shard.astype(low),
        ],
        axis=0,
    )
    totals = (
        ctx_sum(grad_shard),
        ffn_sums[:ffn_units],
        ffn_sums[ffn_units : 2 * ffn_units],
        ffn_sums[2 * ffn_units :],
    )
    grad_shard = totals[0].astype(f32)
    grows = grad_shard[o4:]
    return (
        outputs[None],
        in_grad[None],
        grad_shard[:o1].T,
        grad_shard[o1:o2].T,
        grad_shard[o2:o3].T,
        grad_shard[o3:o4],
        totals[1].astype(f32),
        totals[2].astype(f32),
        totals[3].astype(f32),
        grows[0],
        grows[4, :head_shard],
        grows[5, :head_shard],
        grows[1],
        grows[2],
        grows[3],
    )


def solution(mesh):
    placed = (
        P("fsdp", "ctx", None),
        P("fsdp", "ctx", None),
        P("fsdp", "ctx"),
        P(),
        P("fsdp", None),
        P("fsdp", None),
        P("fsdp", None),
        P(None, "fsdp"),
        P("fsdp", None),
        P("fsdp", None),
        P("fsdp", None),
        P("fsdp"),
        P("fsdp"),
        P("fsdp"),
        P("fsdp"),
        P("fsdp"),
        P("fsdp"),
    )
    return jax.shard_map(
        body,
        mesh=mesh,
        in_specs=placed,
        out_specs=(
            P("fsdp", "ctx", None),
            P("fsdp", "ctx", None),
            P("fsdp", None),
            P("fsdp", None),
            P("fsdp", None),
            P(None, "fsdp"),
            P("fsdp", None),
            P("fsdp", None),
            P("fsdp", None),
            P("fsdp"),
            P("fsdp"),
            P("fsdp"),
            P("fsdp"),
            P("fsdp"),
            P("fsdp"),
        ),
        check_vma=False,
    )
```

```python
import jax
import jax.numpy as jnp
from jax import lax
from jax.sharding import PartitionSpec as P

H = 4
HD = 256


EPS = 1e-06
ROPE_BASE = 1000000.0
GELU_C = 0.7978845608028654
GELU_A = 0.044715


def norm_forward(values, gain):
    inverse = lax.rsqrt(jnp.mean(values * values, axis=-1, keepdims=True) + EPS)
    unit = values * inverse
    return (unit * gain, unit, inverse)


def norm_backward(upstream, unit, inverse, gain):
    scaled = upstream * gain
    inner = jnp.mean(scaled * unit, axis=-1, keepdims=True)
    leading = tuple(range(upstream.ndim - 1))
    return (inverse * (scaled - unit * inner), jnp.sum(upstream * unit, axis=leading))


def gelu_pair(gate):
    inner = GELU_C * (gate + GELU_A * gate * gate * gate)
    tangent = jnp.tanh(inner)
    value = 0.5 * gate * (1.0 + tangent)
    slope = 0.5 * (1.0 + tangent) + 0.5 * gate * (1.0 - tangent * tangent) * GELU_C * (
        1.0 + 3.0 * GELU_A * gate * gate
    )
    return (value, slope)


def rope_tables(positions, width):
    half = width // 2
    freqs = ROPE_BASE ** (-2.0 * jnp.arange(half, dtype=jnp.float32) / width)
    angles = positions.astype(jnp.float32)[:, None] * freqs[None, :]
    return (jnp.cos(angles), jnp.sin(angles))


def rotate(values, cosine, sine):
    half = values.shape[-1] // 2
    first = values[..., :half]
    second = values[..., half:]
    return jnp.concatenate(
        [first * cosine - second * sine, second * cosine + first * sine], axis=-1
    )


def rotate_back(values, cosine, sine):
    half = values.shape[-1] // 2
    first = values[..., :half]
    second = values[..., half:]
    return jnp.concatenate(
        [first * cosine + second * sine, second * cosine - first * sine], axis=-1
    )


def sequence_rows(order_flat, first_row, count, block):
    rows = first_row + jnp.arange(count, dtype=jnp.int32)
    slots = rows // block
    table = jnp.arange(order_flat.shape[0], dtype=jnp.int32)
    picked = jnp.sum(jnp.where(slots[:, None] == table[None, :], order_flat[None, :], 0), axis=1)
    return picked * block + rows % block


def pad_rows(shard, rows):
    return jnp.pad(shard, (0, rows - shard.shape[0]))


def a2a_sum(x, axis_name, count):
    pieces = lax.all_to_all(x.reshape(count, -1, *x.shape[1:]), axis_name, 0, 0)
    return jnp.sum(pieces.astype(jnp.float32), axis=0)


def a2a_gather(x, axis_name, count):
    copies = jnp.broadcast_to(x[None], (count,) + x.shape)
    return lax.all_to_all(copies, axis_name, 0, 0).reshape(count * x.shape[0], *x.shape[1:])


def body(
    inputs,
    out_grad,
    positions,
    block_order,
    w_query,
    w_key,
    w_value,
    w_output,
    w_gate,
    w_up,
    w_down,
    gain_in,
    gain_query,
    gain_key,
    gain_attn,
    gain_pre,
    gain_post,
):
    f32 = jnp.float32
    low = jnp.bfloat16
    tokens = inputs[0]
    local = tokens.shape[0]
    parts = lax.axis_size("ctx")
    groups = lax.axis_size("fsdp")
    total = local * parts
    block = local // 2
    width_shard = w_query.shape[0]
    qw = w_query.shape[1]
    kw = w_key.shape[1]
    gain_cols = jnp.stack(
        [
            gain_in,
            gain_attn,
            gain_pre,
            gain_post,
            pad_rows(gain_query, width_shard),
            pad_rows(gain_key, width_shard),
        ],
        axis=1,
    )
    gain_cols = jnp.pad(gain_cols, ((0, 0), (0, 128 - gain_cols.shape[1])))
    packed = jnp.concatenate([w_query, w_key, w_value, w_output.T, gain_cols], axis=1)
    packed_all = lax.all_gather(packed, "fsdp", axis=0, tiled=True)
    o1 = qw
    o2 = o1 + kw
    o3 = o2 + kw
    o4 = o3 + w_output.shape[0]
    full_query = packed_all[:, :o1]
    full_key = packed_all[:, o1:o2]
    full_value = packed_all[:, o2:o3]
    full_output_t = packed_all[:, o3:o4]
    gains_all = packed_all[:, o4:].astype(f32)
    head_shard = gain_query.shape[0]

    def head_gain(col):
        return col.reshape(groups, width_shard)[:, :head_shard].reshape(-1)

    norm_in = gains_all[:, 0]
    norm_attn = gains_all[:, 1]
    norm_pre = gains_all[:, 2]
    norm_post = gains_all[:, 3]
    norm_query = head_gain(gains_all[:, 4])
    norm_key = head_gain(gains_all[:, 5])
    ctx_index = lax.axis_index("ctx")
    order_flat = block_order.reshape(-1)
    my_seq = sequence_rows(order_flat, ctx_index * local, local, block)
    all_seq = sequence_rows(order_flat, 0, total, block)
    flat_in = tokens.astype(f32)
    normed_full, unit_in, inv_in = norm_forward(flat_in, norm_in)
    normed_in = normed_full.astype(low)
    queries = jnp.dot(normed_in, full_query, preferred_element_type=f32).reshape(local, H, HD)
    keys_raw = jnp.dot(normed_in, full_key, preferred_element_type=f32)
    values = jnp.dot(normed_in, full_value, preferred_element_type=f32).astype(low)
    query_normed, query_unit, query_inv = norm_forward(queries, norm_query)
    key_normed, key_unit, key_inv = norm_forward(keys_raw, norm_key)
    cosine, sine = rope_tables(positions[0], HD)
    scale = HD ** (-0.5)
    query_rot = (rotate(query_normed, cosine[:, None, :], sine[:, None, :]) * scale).astype(low)
    key_rot = rotate(key_normed, cosine, sine).astype(low)
    kv_all = a2a_gather(jnp.concatenate([key_rot, values], axis=1), "ctx", parts)
    key_all = kv_all[:, :HD]
    value_all = kv_all[:, HD:]
    scores = jnp.einsum("qhd,kd->hqk", query_rot, key_all, preferred_element_type=f32)
    allowed = my_seq[:, None] >= all_seq[None, :]
    scores = jnp.where(allowed[None], scores, -jnp.inf)
    highest = jnp.max(scores, axis=-1, keepdims=True)
    log_total = highest + jnp.log(jnp.sum(jnp.exp(scores - highest), axis=-1, keepdims=True))
    probs_full = jnp.exp(scores - log_total)
    probs = probs_full.astype(low)
    attended = (
        jnp.einsum("hqk,kd->qhd", probs, value_all, preferred_element_type=f32)
        .reshape(local, H * HD)
        .astype(low)
    )
    branch_attn = jnp.einsum("tc,dc->td", attended, full_output_t, preferred_element_type=f32)
    attn_normed, attn_unit, attn_inv = norm_forward(branch_attn, norm_attn)
    residual = flat_in + attn_normed
    pre_full, pre_unit, pre_inv = norm_forward(residual, norm_pre)
    normed_pre = pre_full.astype(low)
    rows_all = lax.all_gather(normed_pre, "fsdp", axis=0, tiled=True)
    gate = jnp.einsum("td,fd->tf", rows_all, w_gate, preferred_element_type=f32)
    upper = jnp.einsum("td,fd->tf", rows_all, w_up, preferred_element_type=f32)
    gelu_value, gelu_slope = gelu_pair(gate)
    hidden = (gelu_value * upper).astype(low)
    branch_ffn = a2a_sum(
        jnp.dot(hidden, w_down, preferred_element_type=f32).astype(jnp.bfloat16), "fsdp", groups
    )
    post_normed, post_unit, post_inv = norm_forward(branch_ffn, norm_post)
    outputs = (residual + post_normed).astype(low)
    grad_out = out_grad[0].astype(f32)
    grad_ffn_full, grad_gain_post = norm_backward(grad_out, post_unit, post_inv, norm_post)
    grad_ffn = grad_ffn_full.astype(low)
    grad_all = lax.all_gather(grad_ffn, "fsdp", axis=0, tiled=True)
    grad_hidden = jnp.einsum("td,fd->tf", grad_all, w_down, preferred_element_type=f32)
    grad_gate = (grad_hidden * upper * gelu_slope).astype(low)
    grad_up = (grad_hidden * gelu_value).astype(low)
    shard_gate = jnp.einsum("tf,td->fd", grad_gate, rows_all, preferred_element_type=f32)
    shard_up = jnp.einsum("tf,td->fd", grad_up, rows_all, preferred_element_type=f32)
    shard_down = jnp.einsum("tf,td->fd", hidden, grad_all, preferred_element_type=f32)
    grad_pre = a2a_sum(
        (
            jnp.dot(grad_gate, w_gate, preferred_element_type=f32)
            + jnp.dot(grad_up, w_up, preferred_element_type=f32)
        ).astype(jnp.bfloat16),
        "fsdp",
        groups,
    )
    grad_from_pre, grad_gain_pre = norm_backward(grad_pre, pre_unit, pre_inv, norm_pre)
    grad_residual = grad_out + grad_from_pre
    grad_branch_full, grad_gain_attn = norm_backward(grad_residual, attn_unit, attn_inv, norm_attn)
    grad_branch = grad_branch_full.astype(low)
    term_output = jnp.einsum("tc,td->cd", attended, grad_branch, preferred_element_type=f32)
    grad_attended = jnp.einsum(
        "td,dc->tc", grad_branch, full_output_t, preferred_element_type=f32
    ).astype(low)
    grad_heads = grad_attended.reshape(local, H, HD)
    attended_heads = attended.reshape(local, H, HD)
    delta = jnp.transpose(jnp.sum(grad_heads.astype(f32) * attended_heads.astype(f32), axis=-1))[
        :, :, None
    ]
    grad_probs = jnp.einsum("qhd,kd->hqk", grad_heads, value_all, preferred_element_type=f32)
    grad_scores = (probs_full * (grad_probs - delta)).astype(low)
    value_term = jnp.einsum("hqk,qhd->kd", probs, grad_heads, preferred_element_type=f32)
    key_term = jnp.einsum("hqk,qhd->kd", grad_scores, query_rot, preferred_element_type=f32)
    key_value_terms = jnp.concatenate([key_term, value_term], axis=1)
    grad_query_rot = jnp.einsum("hqk,kd->qhd", grad_scores, key_all, preferred_element_type=f32)
    summed_kv = a2a_sum(key_value_terms.astype(jnp.bfloat16), "ctx", parts)
    grad_key_rot = summed_kv[:, :HD]
    grad_values = summed_kv[:, HD:].astype(low)
    grad_q_normed = rotate_back(grad_query_rot * scale, cosine[:, None, :], sine[:, None, :])
    grad_q_full, grad_gain_query = norm_backward(grad_q_normed, query_unit, query_inv, norm_query)
    grad_k_normed = rotate_back(grad_key_rot, cosine, sine)
    grad_k_full, grad_gain_key = norm_backward(grad_k_normed, key_unit, key_inv, norm_key)
    grad_q_in = grad_q_full.reshape(local, H * HD).astype(low)
    grad_k_in = grad_k_full.astype(low)
    term_query = jnp.einsum("tc,td->cd", grad_q_in, normed_in, preferred_element_type=f32)
    term_key = jnp.einsum("tc,td->cd", grad_k_in, normed_in, preferred_element_type=f32)
    term_value = jnp.einsum("tc,td->cd", grad_values, normed_in, preferred_element_type=f32)
    grad_normed = (
        jnp.einsum("tc,dc->td", grad_q_in, full_query, preferred_element_type=f32)
        + jnp.einsum("tc,dc->td", grad_k_in, full_key, preferred_element_type=f32)
        + jnp.einsum("tc,dc->td", grad_values, full_value, preferred_element_type=f32)
    )
    grad_from_in, grad_gain_in = norm_backward(grad_normed, unit_in, inv_in, norm_in)
    in_grad = (grad_residual + grad_from_in).astype(low)

    def head_col(g):
        return jnp.pad(g.reshape(groups, head_shard), ((0, 0), (0, width_shard - head_shard))).reshape(-1)

    gain_block = jnp.stack(
        [
            grad_gain_in,
            grad_gain_attn,
            grad_gain_pre,
            grad_gain_post,
            head_col(grad_gain_query),
            head_col(grad_gain_key),
        ],
        axis=0,
    )
    gain_block = jnp.pad(gain_block, ((0, 8 - gain_block.shape[0]), (0, 0))).astype(low)
    gain_block = jnp.transpose(gain_block.reshape(8, groups, width_shard), (1, 0, 2))
    gain_shard = jnp.sum(lax.all_to_all(gain_block, "fsdp", 0, 0).astype(f32), axis=0)

    def ctx_sum(x):
        chunks = x.reshape(parts, -1, x.shape[1])
        mine = jnp.sum(lax.all_to_all(chunks, "ctx", 0, 0).astype(f32), axis=0).astype(low)
        return lax.all_to_all(jnp.broadcast_to(mine[None], chunks.shape), "ctx", 0, 0).reshape(x.shape)

    ffn_units = shard_gate.shape[0]
    ffn_sums = ctx_sum(
        jnp.concatenate([shard_gate, shard_up, shard_down], axis=0).astype(low)
    ).astype(f32)
    grad_packed = jnp.concatenate([term_query, term_key, term_value, term_output], axis=0).astype(low)
    grad_shard = jnp.concatenate(
        [
            lax.psum_scatter(grad_packed, "fsdp", scatter_dimension=1, tiled=True),
            gain_shard.astype(low),
        ],
        axis=0,
    )
    totals = (
        ctx_sum(grad_shard),
        ffn_sums[:ffn_units],
        ffn_sums[ffn_units : 2 * ffn_units],
        ffn_sums[2 * ffn_units :],
    )
    grad_shard = totals[0].astype(f32)
    grows = grad_shard[o4:]
    return (
        outputs[None],
        in_grad[None],
        grad_shard[:o1].T,
        grad_shard[o1:o2].T,
        grad_shard[o2:o3].T,
        grad_shard[o3:o4],
        totals[1].astype(f32),
        totals[2].astype(f32),
        totals[3].astype(f32),
        grows[0],
        grows[4, :head_shard],
        grows[5, :head_shard],
        grows[1],
        grows[2],
        grows[3],
    )


def solution(mesh):
    placed = (
        P("fsdp", "ctx", None),
        P("fsdp", "ctx", None),
        P("fsdp", "ctx"),
        P(),
        P("fsdp", None),
        P("fsdp", None),
        P("fsdp", None),
        P(None, "fsdp"),
        P("fsdp", None),
        P("fsdp", None),
        P("fsdp", None),
        P("fsdp"),
        P("fsdp"),
        P("fsdp"),
        P("fsdp"),
        P("fsdp"),
        P("fsdp"),
    )
    return jax.shard_map(
        body,
        mesh=mesh,
        in_specs=placed,
        out_specs=(
            P("fsdp", "ctx", None),
            P("fsdp", "ctx", None),
            P("fsdp", None),
            P("fsdp", None),
            P("fsdp", None),
            P(None, "fsdp"),
            P("fsdp", None),
            P("fsdp", None),
            P("fsdp", None),
            P("fsdp"),
            P("fsdp"),
            P("fsdp"),
            P("fsdp"),
            P("fsdp"),
            P("fsdp"),
        ),
        check_vma=False,
    )
```

```python
import jax
import jax.numpy as jnp
from jax import lax
from jax.sharding import PartitionSpec as P

H = 4
HD = 256


EPS = 1e-06
ROPE_BASE = 1000000.0
GELU_C = 0.7978845608028654
GELU_A = 0.044715


def norm_forward(values, gain):
    inverse = lax.rsqrt(jnp.mean(values * values, axis=-1, keepdims=True) + EPS)
    unit = values * inverse
    return (unit * gain, unit, inverse)


def norm_backward(upstream, unit, inverse, gain):
    scaled = upstream * gain
    inner = jnp.mean(scaled * unit, axis=-1, keepdims=True)
    leading = tuple(range(upstream.ndim - 1))
    return (inverse * (scaled - unit * inner), jnp.sum(upstream * unit, axis=leading))


def gelu_pair(gate):
    inner = GELU_C * (gate + GELU_A * gate * gate * gate)
    tangent = jnp.tanh(inner)
    value = 0.5 * gate * (1.0 + tangent)
    slope = 0.5 * (1.0 + tangent) + 0.5 * gate * (1.0 - tangent * tangent) * GELU_C * (
        1.0 + 3.0 * GELU_A * gate * gate
    )
    return (value, slope)


def rope_tables(positions, width):
    half = width // 2
    freqs = ROPE_BASE ** (-2.0 * jnp.arange(half, dtype=jnp.float32) / width)
    angles = positions.astype(jnp.float32)[:, None] * freqs[None, :]
    return (jnp.cos(angles), jnp.sin(angles))


def rotate(values, cosine, sine):
    half = values.shape[-1] // 2
    first = values[..., :half]
    second = values[..., half:]
    return jnp.concatenate(
        [first * cosine - second * sine, second * cosine + first * sine], axis=-1
    )


def rotate_back(values, cosine, sine):
    half = values.shape[-1] // 2
    first = values[..., :half]
    second = values[..., half:]
    return jnp.concatenate(
        [first * cosine + second * sine, second * cosine - first * sine], axis=-1
    )


def sequence_rows(order_flat, first_row, count, block):
    rows = first_row + jnp.arange(count, dtype=jnp.int32)
    slots = rows // block
    table = jnp.arange(order_flat.shape[0], dtype=jnp.int32)
    picked = jnp.sum(jnp.where(slots[:, None] == table[None, :], order_flat[None, :], 0), axis=1)
    return picked * block + rows % block


def pad_rows(shard, rows):
    return jnp.pad(shard, (0, rows - shard.shape[0]))


def a2a_sum(x, axis_name, count):
    pieces = lax.all_to_all(x.reshape(count, -1, *x.shape[1:]), axis_name, 0, 0)
    return jnp.sum(pieces.astype(jnp.float32), axis=0)


def a2a_gather(x, axis_name, count):
    copies = jnp.broadcast_to(x[None], (count,) + x.shape)
    return lax.all_to_all(copies, axis_name, 0, 0).reshape(count * x.shape[0], *x.shape[1:])


def body(
    inputs,
    out_grad,
    positions,
    block_order,
    w_query,
    w_key,
    w_value,
    w_output,
    w_gate,
    w_up,
    w_down,
    gain_in,
    gain_query,
    gain_key,
    gain_attn,
    gain_pre,
    gain_post,
):
    f32 = jnp.float32
    low = jnp.bfloat16
    tokens = inputs[0]
    local = tokens.shape[0]
    parts = lax.axis_size("ctx")
    groups = lax.axis_size("fsdp")
    total = local * parts
    block = local // 2
    width_shard = w_query.shape[0]
    qw = w_query.shape[1]
    kw = w_key.shape[1]
    gain_cols = jnp.stack(
        [
            gain_in,
            gain_attn,
            gain_pre,
            gain_post,
            pad_rows(gain_query, width_shard),
            pad_rows(gain_key, width_shard),
        ],
        axis=1,
    )
    gain_cols = jnp.pad(gain_cols, ((0, 0), (0, 128 - gain_cols.shape[1])))
    packed = jnp.concatenate([w_query, w_key, w_value, gain_cols], axis=1)
    packed_all = lax.all_gather(packed, "fsdp", axis=0, tiled=True)
    full_output_t = lax.all_gather(w_output.T, "fsdp", axis=0, tiled=True)
    o1 = qw
    o2 = o1 + kw
    o3 = o2 + kw
    o4 = o3 + w_output.shape[0]
    full_query = packed_all[:, :o1]
    full_key = packed_all[:, o1:o2]
    full_value = packed_all[:, o2:o3]
    gains_all = packed_all[:, o3:].astype(f32)
    head_shard = gain_query.shape[0]

    def head_gain(col):
        return col.reshape(groups, width_shard)[:, :head_shard].reshape(-1)

    norm_in = gains_all[:, 0]
    norm_attn = gains_all[:, 1]
    norm_pre = gains_all[:, 2]
    norm_post = gains_all[:, 3]
    norm_query = head_gain(gains_all[:, 4])
    norm_key = head_gain(gains_all[:, 5])
    ctx_index = lax.axis_index("ctx")
    order_flat = block_order.reshape(-1)
    my_seq = sequence_rows(order_flat, ctx_index * local, local, block)
    all_seq = sequence_rows(order_flat, 0, total, block)
    flat_in = tokens.astype(f32)
    normed_full, unit_in, inv_in = norm_forward(flat_in, norm_in)
    normed_in = normed_full.astype(low)
    queries = jnp.dot(normed_in, full_query, preferred_element_type=f32).reshape(local, H, HD)
    keys_raw = jnp.dot(normed_in, full_key, preferred_element_type=f32)
    values = jnp.dot(normed_in, full_value, preferred_element_type=f32).astype(low)
    query_normed, query_unit, query_inv = norm_forward(queries, norm_query)
    key_normed, key_unit, key_inv = norm_forward(keys_raw, norm_key)
    cosine, sine = rope_tables(positions[0], HD)
    scale = HD ** (-0.5)
    query_rot = (rotate(query_normed, cosine[:, None, :], sine[:, None, :]) * scale).astype(low)
    key_rot = rotate(key_normed, cosine, sine).astype(low)
    kv_all = a2a_gather(jnp.concatenate([key_rot, values], axis=1), "ctx", parts)
    key_all = kv_all[:, :HD]
    value_all = kv_all[:, HD:]
    scores = jnp.einsum("qhd,kd->hqk", query_rot, key_all, preferred_element_type=f32)
    allowed = my_seq[:, None] >= all_seq[None, :]
    scores = jnp.where(allowed[None], scores, -jnp.inf)
    highest = jnp.max(scores, axis=-1, keepdims=True)
    log_total = highest + jnp.log(jnp.sum(jnp.exp(scores - highest), axis=-1, keepdims=True))
    probs_full = jnp.exp(scores - log_total)
    probs = probs_full.astype(low)
    attended = (
        jnp.einsum("hqk,kd->qhd", probs, value_all, preferred_element_type=f32)
        .reshape(local, H * HD)
        .astype(low)
    )
    branch_attn = jnp.einsum("tc,dc->td", attended, full_output_t, preferred_element_type=f32)
    attn_normed, attn_unit, attn_inv = norm_forward(branch_attn, norm_attn)
    residual = flat_in + attn_normed
    pre_full, pre_unit, pre_inv = norm_forward(residual, norm_pre)
    normed_pre = pre_full.astype(low)
    rows_all = lax.all_gather(normed_pre, "fsdp", axis=0, tiled=True)
    gate = jnp.einsum("td,fd->tf", rows_all, w_gate, preferred_element_type=f32)
    upper = jnp.einsum("td,fd->tf", rows_all, w_up, preferred_element_type=f32)
    gelu_value, gelu_slope = gelu_pair(gate)
    hidden = (gelu_value * upper).astype(low)
    branch_ffn = a2a_sum(
        jnp.dot(hidden, w_down, preferred_element_type=f32).astype(jnp.bfloat16), "fsdp", groups
    )
    post_normed, post_unit, post_inv = norm_forward(branch_ffn, norm_post)
    outputs = (residual + post_normed).astype(low)
    grad_out = out_grad[0].astype(f32)
    grad_ffn_full, grad_gain_post = norm_backward(grad_out, post_unit, post_inv, norm_post)
    grad_ffn = grad_ffn_full.astype(low)
    grad_all = lax.all_gather(grad_ffn, "fsdp", axis=0, tiled=True)
    grad_hidden = jnp.einsum("td,fd->tf", grad_all, w_down, preferred_element_type=f32)
    grad_gate = (grad_hidden * upper * gelu_slope).astype(low)
    grad_up = (grad_hidden * gelu_value).astype(low)
    shard_gate = jnp.einsum("tf,td->fd", grad_gate, rows_all, preferred_element_type=f32)
    shard_up = jnp.einsum("tf,td->fd", grad_up, rows_all, preferred_element_type=f32)
    shard_down = jnp.einsum("tf,td->fd", hidden, grad_all, preferred_element_type=f32)
    pre_partial = (
        jnp.dot(grad_gate, w_gate, preferred_element_type=f32)
        + jnp.dot(grad_up, w_up, preferred_element_type=f32)
    ).astype(jnp.bfloat16)
    shard_gate, shard_up, shard_down, pre_partial = lax.optimization_barrier(
        (shard_gate.astype(low), shard_up.astype(low), shard_down.astype(low), pre_partial)
    )
    grad_pre = a2a_sum(pre_partial, "fsdp", groups)
    grad_from_pre, grad_gain_pre = norm_backward(grad_pre, pre_unit, pre_inv, norm_pre)
    grad_residual = grad_out + grad_from_pre
    grad_branch_full, grad_gain_attn = norm_backward(grad_residual, attn_unit, attn_inv, norm_attn)
    grad_branch = grad_branch_full.astype(low)
    term_output = jnp.einsum("tc,td->dc", attended, grad_branch, preferred_element_type=f32)
    grad_attended = jnp.einsum(
        "td,dc->tc", grad_branch, full_output_t, preferred_element_type=f32
    ).astype(low)
    grad_heads = grad_attended.reshape(local, H, HD)
    attended_heads = attended.reshape(local, H, HD)
    delta = jnp.transpose(jnp.sum(grad_heads.astype(f32) * attended_heads.astype(f32), axis=-1))[
        :, :, None
    ]
    grad_probs = jnp.einsum("qhd,kd->hqk", grad_heads, value_all, preferred_element_type=f32)
    grad_scores = (probs_full * (grad_probs - delta)).astype(low)
    value_term = jnp.einsum("hqk,qhd->kd", probs, grad_heads, preferred_element_type=f32)
    key_term = jnp.einsum("hqk,qhd->kd", grad_scores, query_rot, preferred_element_type=f32)
    key_value_terms = jnp.concatenate([key_term, value_term], axis=1)
    grad_query_rot = jnp.einsum("hqk,kd->qhd", grad_scores, key_all, preferred_element_type=f32)
    summed_kv = a2a_sum(key_value_terms.astype(jnp.bfloat16), "ctx", parts)
    ffn_sums = lax.psum((shard_gate, shard_up, shard_down), "ctx")
    ffn_sums, summed_kv = lax.optimization_barrier((ffn_sums, summed_kv))
    grad_key_rot = summed_kv[:, :HD]
    grad_values = summed_kv[:, HD:].astype(low)
    grad_q_normed = rotate_back(grad_query_rot * scale, cosine[:, None, :], sine[:, None, :])
    grad_q_full, grad_gain_query = norm_backward(grad_q_normed, query_unit, query_inv, norm_query)
    grad_k_normed = rotate_back(grad_key_rot, cosine, sine)
    grad_k_full, grad_gain_key = norm_backward(grad_k_normed, key_unit, key_inv, norm_key)
    grad_q_in = grad_q_full.reshape(local, H * HD).astype(low)
    grad_k_in = grad_k_full.astype(low)
    term_query = jnp.einsum("tc,td->dc", grad_q_in, normed_in, preferred_element_type=f32)
    term_key = jnp.einsum("tc,td->dc", grad_k_in, normed_in, preferred_element_type=f32)
    term_value = jnp.einsum("tc,td->dc", grad_values, normed_in, preferred_element_type=f32)
    grad_normed = (
        jnp.einsum("tc,dc->td", grad_q_in, full_query, preferred_element_type=f32)
        + jnp.einsum("tc,dc->td", grad_k_in, full_key, preferred_element_type=f32)
        + jnp.einsum("tc,dc->td", grad_values, full_value, preferred_element_type=f32)
    )
    grad_from_in, grad_gain_in = norm_backward(grad_normed, unit_in, inv_in, norm_in)
    in_grad = (grad_residual + grad_from_in).astype(low)

    def head_col(g):
        return jnp.pad(g.reshape(groups, head_shard), ((0, 0), (0, width_shard - head_shard))).reshape(-1)

    gain_block = jnp.stack(
        [
            grad_gain_in,
            grad_gain_attn,
            grad_gain_pre,
            grad_gain_post,
            head_col(grad_gain_query),
            head_col(grad_gain_key),
        ],
        axis=1,
    )
    gain_block = jnp.pad(gain_block, ((0, 0), (0, 8 - gain_block.shape[1])))

    def ctx_sum(x):
        chunks = x.reshape(parts, -1, x.shape[1])
        mine = jnp.sum(lax.all_to_all(chunks, "ctx", 0, 0).astype(f32), axis=0).astype(low)
        return lax.all_to_all(jnp.broadcast_to(mine[None], chunks.shape), "ctx", 0, 0).reshape(x.shape)

    grad_packed = jnp.concatenate(
        [term_query, term_key, term_value, term_output, gain_block], axis=1
    ).astype(low)
    grad_shard = a2a_sum(grad_packed, "fsdp", groups).astype(low).T
    totals = (
        ctx_sum(grad_shard),
        ffn_sums[0].astype(f32),
        ffn_sums[1].astype(f32),
        ffn_sums[2].astype(f32),
    )
    grad_shard = totals[0].astype(f32)
    grows = grad_shard[o4:]
    return (
        outputs[None],
        in_grad[None],
        grad_shard[:o1].T,
        grad_shard[o1:o2].T,
        grad_shard[o2:o3].T,
        grad_shard[o3:o4],
        totals[1].astype(f32),
        totals[2].astype(f32),
        totals[3].astype(f32),
        grows[0],
        grows[4, :head_shard],
        grows[5, :head_shard],
        grows[1],
        grows[2],
        grows[3],
    )


def solution(mesh):
    placed = (
        P("fsdp", "ctx", None),
        P("fsdp", "ctx", None),
        P("fsdp", "ctx"),
        P(),
        P("fsdp", None),
        P("fsdp", None),
        P("fsdp", None),
        P(None, "fsdp"),
        P("fsdp", None),
        P("fsdp", None),
        P("fsdp", None),
        P("fsdp"),
        P("fsdp"),
        P("fsdp"),
        P("fsdp"),
        P("fsdp"),
        P("fsdp"),
    )
    return jax.shard_map(
        body,
        mesh=mesh,
        in_specs=placed,
        out_specs=(
            P("fsdp", "ctx", None),
            P("fsdp", "ctx", None),
            P("fsdp", None),
            P("fsdp", None),
            P("fsdp", None),
            P(None, "fsdp"),
            P("fsdp", None),
            P("fsdp", None),
            P("fsdp", None),
            P("fsdp"),
            P("fsdp"),
            P("fsdp"),
            P("fsdp"),
            P("fsdp"),
            P("fsdp"),
        ),
        check_vma=False,
    )
```

```python
import jax
import jax.numpy as jnp
from jax import lax
from jax.sharding import PartitionSpec as P

H = 4
HD = 256


EPS = 1e-06
ROPE_BASE = 1000000.0
GELU_C = 0.7978845608028654
GELU_A = 0.044715


def norm_forward(values, gain):
    inverse = lax.rsqrt(jnp.mean(values * values, axis=-1, keepdims=True) + EPS)
    unit = values * inverse
    return (unit * gain, unit, inverse)


def norm_backward(upstream, unit, inverse, gain):
    scaled = upstream * gain
    inner = jnp.mean(scaled * unit, axis=-1, keepdims=True)
    leading = tuple(range(upstream.ndim - 1))
    return (inverse * (scaled - unit * inner), jnp.sum(upstream * unit, axis=leading))


def gelu_pair(gate):
    inner = GELU_C * (gate + GELU_A * gate * gate * gate)
    tangent = jnp.tanh(inner)
    value = 0.5 * gate * (1.0 + tangent)
    slope = 0.5 * (1.0 + tangent) + 0.5 * gate * (1.0 - tangent * tangent) * GELU_C * (
        1.0 + 3.0 * GELU_A * gate * gate
    )
    return (value, slope)


def rope_tables(positions, width):
    half = width // 2
    freqs = ROPE_BASE ** (-2.0 * jnp.arange(half, dtype=jnp.float32) / width)
    angles = positions.astype(jnp.float32)[:, None] * freqs[None, :]
    return (jnp.cos(angles), jnp.sin(angles))


def rotate(values, cosine, sine):
    half = values.shape[-1] // 2
    first = values[..., :half]
    second = values[..., half:]
    return jnp.concatenate(
        [first * cosine - second * sine, second * cosine + first * sine], axis=-1
    )


def rotate_back(values, cosine, sine):
    half = values.shape[-1] // 2
    first = values[..., :half]
    second = values[..., half:]
    return jnp.concatenate(
        [first * cosine + second * sine, second * cosine - first * sine], axis=-1
    )


def sequence_rows(order_flat, first_row, count, block):
    rows = first_row + jnp.arange(count, dtype=jnp.int32)
    slots = rows // block
    table = jnp.arange(order_flat.shape[0], dtype=jnp.int32)
    picked = jnp.sum(jnp.where(slots[:, None] == table[None, :], order_flat[None, :], 0), axis=1)
    return picked * block + rows % block


def pad_rows(shard, rows):
    return jnp.pad(shard, (0, rows - shard.shape[0]))


def a2a_sum(x, axis_name, count):
    pieces = lax.all_to_all(x.reshape(count, -1, *x.shape[1:]), axis_name, 0, 0)
    return jnp.sum(pieces.astype(jnp.float32), axis=0)


def a2a_gather(x, axis_name, count):
    copies = jnp.broadcast_to(x[None], (count,) + x.shape)
    return lax.all_to_all(copies, axis_name, 0, 0).reshape(count * x.shape[0], *x.shape[1:])


def body(
    inputs,
    out_grad,
    positions,
    block_order,
    w_query,
    w_key,
    w_value,
    w_output,
    w_gate,
    w_up,
    w_down,
    gain_in,
    gain_query,
    gain_key,
    gain_attn,
    gain_pre,
    gain_post,
):
    f32 = jnp.float32
    low = jnp.bfloat16
    tokens = inputs[0]
    local = tokens.shape[0]
    parts = lax.axis_size("ctx")
    groups = lax.axis_size("fsdp")
    total = local * parts
    block = local // 2
    width_shard = w_query.shape[0]
    qw = w_query.shape[1]
    kw = w_key.shape[1]
    gain_cols = jnp.stack(
        [
            gain_in,
            gain_attn,
            gain_pre,
            gain_post,
            pad_rows(gain_query, width_shard),
            pad_rows(gain_key, width_shard),
        ],
        axis=1,
    )
    gain_cols = jnp.pad(gain_cols, ((0, 0), (0, 128 - gain_cols.shape[1])))
    packed = jnp.concatenate([w_query, w_key, w_value, gain_cols], axis=1)
    packed_all = lax.all_gather(packed, "fsdp", axis=0, tiled=True)
    full_output_t = lax.all_gather(w_output.T, "fsdp", axis=0, tiled=True)
    o1 = qw
    o2 = o1 + kw
    o3 = o2 + kw
    o4 = o3 + w_output.shape[0]
    full_query = packed_all[:, :o1]
    full_key = packed_all[:, o1:o2]
    full_value = packed_all[:, o2:o3]
    gains_all = packed_all[:, o3:].astype(f32)
    head_shard = gain_query.shape[0]

    def head_gain(col):
        return col.reshape(groups, width_shard)[:, :head_shard].reshape(-1)

    norm_in = gains_all[:, 0]
    norm_attn = gains_all[:, 1]
    norm_pre = gains_all[:, 2]
    norm_post = gains_all[:, 3]
    norm_query = head_gain(gains_all[:, 4])
    norm_key = head_gain(gains_all[:, 5])
    ctx_index = lax.axis_index("ctx")
    order_flat = block_order.reshape(-1)
    my_seq = sequence_rows(order_flat, ctx_index * local, local, block)
    all_seq = sequence_rows(order_flat, 0, total, block)
    flat_in = tokens.astype(f32)
    normed_full, unit_in, inv_in = norm_forward(flat_in, norm_in)
    normed_in = normed_full.astype(low)
    queries = jnp.dot(normed_in, full_query, preferred_element_type=f32).reshape(local, H, HD)
    keys_raw = jnp.dot(normed_in, full_key, preferred_element_type=f32)
    values = jnp.dot(normed_in, full_value, preferred_element_type=f32).astype(low)
    query_normed, query_unit, query_inv = norm_forward(queries, norm_query)
    key_normed, key_unit, key_inv = norm_forward(keys_raw, norm_key)
    cosine, sine = rope_tables(positions[0], HD)
    scale = HD ** (-0.5)
    query_rot = (rotate(query_normed, cosine[:, None, :], sine[:, None, :]) * scale).astype(low)
    key_rot = rotate(key_normed, cosine, sine).astype(low)
    kv_all = a2a_gather(jnp.concatenate([key_rot, values], axis=1), "ctx", parts)
    key_all = kv_all[:, :HD]
    value_all = kv_all[:, HD:]
    scores = jnp.einsum("qhd,kd->hqk", query_rot, key_all, preferred_element_type=f32)
    allowed = my_seq[:, None] >= all_seq[None, :]
    scores = jnp.where(allowed[None], scores, -jnp.inf)
    highest = jnp.max(scores, axis=-1, keepdims=True)
    log_total = highest + jnp.log(jnp.sum(jnp.exp(scores - highest), axis=-1, keepdims=True))
    probs_full = jnp.exp(scores - log_total)
    probs = probs_full.astype(low)
    attended = (
        jnp.einsum("hqk,kd->qhd", probs, value_all, preferred_element_type=f32)
        .reshape(local, H * HD)
        .astype(low)
    )
    branch_attn = jnp.einsum("tc,dc->td", attended, full_output_t, preferred_element_type=f32)
    attn_normed, attn_unit, attn_inv = norm_forward(branch_attn, norm_attn)
    residual = flat_in + attn_normed
    pre_full, pre_unit, pre_inv = norm_forward(residual, norm_pre)
    normed_pre = pre_full.astype(low)
    rows_all = lax.all_gather(normed_pre, "fsdp", axis=0, tiled=True)
    gate = jnp.einsum("td,fd->tf", rows_all, w_gate, preferred_element_type=f32)
    upper = jnp.einsum("td,fd->tf", rows_all, w_up, preferred_element_type=f32)
    gelu_value, gelu_slope = gelu_pair(gate)
    hidden = (gelu_value * upper).astype(low)
    branch_ffn = a2a_sum(
        jnp.dot(hidden, w_down, preferred_element_type=f32).astype(jnp.bfloat16), "fsdp", groups
    )
    post_normed, post_unit, post_inv = norm_forward(branch_ffn, norm_post)
    outputs = (residual + post_normed).astype(low)
    grad_out = out_grad[0].astype(f32)
    grad_ffn_full, grad_gain_post = norm_backward(grad_out, post_unit, post_inv, norm_post)
    grad_ffn = grad_ffn_full.astype(low)
    grad_all = lax.all_gather(grad_ffn, "fsdp", axis=0, tiled=True)
    grad_hidden = jnp.einsum("td,fd->tf", grad_all, w_down, preferred_element_type=f32)
    grad_gate = (grad_hidden * upper * gelu_slope).astype(low)
    grad_up = (grad_hidden * gelu_value).astype(low)
    shard_gate = jnp.einsum("tf,td->fd", grad_gate, rows_all, preferred_element_type=f32)
    shard_up = jnp.einsum("tf,td->fd", grad_up, rows_all, preferred_element_type=f32)
    shard_down = jnp.einsum("tf,td->fd", hidden, grad_all, preferred_element_type=f32)
    grad_pre = a2a_sum(
        (
            jnp.dot(grad_gate, w_gate, preferred_element_type=f32)
            + jnp.dot(grad_up, w_up, preferred_element_type=f32)
        ).astype(jnp.bfloat16),
        "fsdp",
        groups,
    )
    grad_from_pre, grad_gain_pre = norm_backward(grad_pre, pre_unit, pre_inv, norm_pre)
    grad_residual = grad_out + grad_from_pre
    grad_branch_full, grad_gain_attn = norm_backward(grad_residual, attn_unit, attn_inv, norm_attn)
    grad_branch = grad_branch_full.astype(low)
    term_output = jnp.einsum("tc,td->cd", attended, grad_branch, preferred_element_type=f32)
    grad_attended = jnp.einsum(
        "td,dc->tc", grad_branch, full_output_t, preferred_element_type=f32
    ).astype(low)
    grad_heads = grad_attended.reshape(local, H, HD)
    attended_heads = attended.reshape(local, H, HD)
    delta = jnp.transpose(jnp.sum(grad_heads.astype(f32) * attended_heads.astype(f32), axis=-1))[
        :, :, None
    ]
    grad_probs = jnp.einsum("qhd,kd->hqk", grad_heads, value_all, preferred_element_type=f32)
    grad_scores = (probs_full * (grad_probs - delta)).astype(low)
    value_term = jnp.einsum("hqk,qhd->kd", probs, grad_heads, preferred_element_type=f32)
    key_term = jnp.einsum("hqk,qhd->kd", grad_scores, query_rot, preferred_element_type=f32)
    key_value_terms = jnp.concatenate([key_term, value_term], axis=1)
    grad_query_rot = jnp.einsum("hqk,kd->qhd", grad_scores, key_all, preferred_element_type=f32)
    summed_kv = a2a_sum(key_value_terms.astype(jnp.bfloat16), "ctx", parts)
    grad_key_rot = summed_kv[:, :HD]
    grad_values = summed_kv[:, HD:].astype(low)
    grad_q_normed = rotate_back(grad_query_rot * scale, cosine[:, None, :], sine[:, None, :])
    grad_q_full, grad_gain_query = norm_backward(grad_q_normed, query_unit, query_inv, norm_query)
    grad_k_normed = rotate_back(grad_key_rot, cosine, sine)
    grad_k_full, grad_gain_key = norm_backward(grad_k_normed, key_unit, key_inv, norm_key)
    grad_q_in = grad_q_full.reshape(local, H * HD).astype(low)
    grad_k_in = grad_k_full.astype(low)
    output_shard = lax.psum_scatter(term_output.astype(low), "fsdp", scatter_dimension=1, tiled=True)
    output_shard, grad_q_in, grad_k_in, grad_values = lax.optimization_barrier(
        (output_shard, grad_q_in, grad_k_in, grad_values)
    )
    term_query = jnp.einsum("tc,td->cd", grad_q_in, normed_in, preferred_element_type=f32)
    term_key = jnp.einsum("tc,td->cd", grad_k_in, normed_in, preferred_element_type=f32)
    term_value = jnp.einsum("tc,td->cd", grad_values, normed_in, preferred_element_type=f32)
    grad_normed = (
        jnp.einsum("tc,dc->td", grad_q_in, full_query, preferred_element_type=f32)
        + jnp.einsum("tc,dc->td", grad_k_in, full_key, preferred_element_type=f32)
        + jnp.einsum("tc,dc->td", grad_values, full_value, preferred_element_type=f32)
    )
    grad_from_in, grad_gain_in = norm_backward(grad_normed, unit_in, inv_in, norm_in)
    in_grad = (grad_residual + grad_from_in).astype(low)

    def head_col(g):
        return jnp.pad(g.reshape(groups, head_shard), ((0, 0), (0, width_shard - head_shard))).reshape(-1)

    gain_block = jnp.stack(
        [
            grad_gain_in,
            grad_gain_attn,
            grad_gain_pre,
            grad_gain_post,
            head_col(grad_gain_query),
            head_col(grad_gain_key),
        ],
        axis=0,
    )
    gain_block = jnp.pad(gain_block, ((0, 8 - gain_block.shape[0]), (0, 0))).astype(low)
    gain_block = jnp.transpose(gain_block.reshape(8, groups, width_shard), (1, 0, 2))
    gain_shard = jnp.sum(lax.all_to_all(gain_block, "fsdp", 0, 0).astype(f32), axis=0)

    def ctx_sum(x):
        chunks = x.reshape(parts, -1, x.shape[1])
        mine = jnp.sum(lax.all_to_all(chunks, "ctx", 0, 0).astype(f32), axis=0).astype(low)
        return lax.all_to_all(jnp.broadcast_to(mine[None], chunks.shape), "ctx", 0, 0).reshape(x.shape)

    ffn_units = shard_gate.shape[0]
    ffn_sums = ctx_sum(
        jnp.concatenate([shard_gate, shard_up, shard_down], axis=0).astype(low)
    ).astype(f32)
    grad_packed = jnp.concatenate([term_query, term_key, term_value], axis=0).astype(low)
    grad_shard = jnp.concatenate(
        [
            lax.psum_scatter(grad_packed, "fsdp", scatter_dimension=1, tiled=True),
            output_shard,
            gain_shard.astype(low),
        ],
        axis=0,
    )
    totals = (
        ctx_sum(grad_shard),
        ffn_sums[:ffn_units],
        ffn_sums[ffn_units : 2 * ffn_units],
        ffn_sums[2 * ffn_units :],
    )
    grad_shard = totals[0].astype(f32)
    grows = grad_shard[o4:]
    return (
        outputs[None],
        in_grad[None],
        grad_shard[:o1].T,
        grad_shard[o1:o2].T,
        grad_shard[o2:o3].T,
        grad_shard[o3:o4],
        totals[1].astype(f32),
        totals[2].astype(f32),
        totals[3].astype(f32),
        grows[0],
        grows[4, :head_shard],
        grows[5, :head_shard],
        grows[1],
        grows[2],
        grows[3],
    )


def solution(mesh):
    placed = (
        P("fsdp", "ctx", None),
        P("fsdp", "ctx", None),
        P("fsdp", "ctx"),
        P(),
        P("fsdp", None),
        P("fsdp", None),
        P("fsdp", None),
        P(None, "fsdp"),
        P("fsdp", None),
        P("fsdp", None),
        P("fsdp", None),
        P("fsdp"),
        P("fsdp"),
        P("fsdp"),
        P("fsdp"),
        P("fsdp"),
        P("fsdp"),
    )
    return jax.shard_map(
        body,
        mesh=mesh,
        in_specs=placed,
        out_specs=(
            P("fsdp", "ctx", None),
            P("fsdp", "ctx", None),
            P("fsdp", None),
            P("fsdp", None),
            P("fsdp", None),
            P(None, "fsdp"),
            P("fsdp", None),
            P("fsdp", None),
            P("fsdp", None),
            P("fsdp"),
            P("fsdp"),
            P("fsdp"),
            P("fsdp"),
            P("fsdp"),
            P("fsdp"),
        ),
        check_vma=False,
    )
```

```python
import jax
import jax.numpy as jnp
from jax import lax
from jax.sharding import PartitionSpec as P

H = 4
HD = 256


EPS = 1e-06
ROPE_BASE = 1000000.0
GELU_C = 0.7978845608028654
GELU_A = 0.044715


def norm_forward(values, gain):
    inverse = lax.rsqrt(jnp.mean(values * values, axis=-1, keepdims=True) + EPS)
    unit = values * inverse
    return (unit * gain, unit, inverse)


def norm_backward(upstream, unit, inverse, gain):
    scaled = upstream * gain
    inner = jnp.mean(scaled * unit, axis=-1, keepdims=True)
    leading = tuple(range(upstream.ndim - 1))
    return (inverse * (scaled - unit * inner), jnp.sum(upstream * unit, axis=leading))


def gelu_pair(gate):
    inner = GELU_C * (gate + GELU_A * gate * gate * gate)
    tangent = jnp.tanh(inner)
    value = 0.5 * gate * (1.0 + tangent)
    slope = 0.5 * (1.0 + tangent) + 0.5 * gate * (1.0 - tangent * tangent) * GELU_C * (
        1.0 + 3.0 * GELU_A * gate * gate
    )
    return (value, slope)


def rope_tables(positions, width):
    half = width // 2
    freqs = ROPE_BASE ** (-2.0 * jnp.arange(half, dtype=jnp.float32) / width)
    angles = positions.astype(jnp.float32)[:, None] * freqs[None, :]
    return (jnp.cos(angles), jnp.sin(angles))


def rotate(values, cosine, sine):
    half = values.shape[-1] // 2
    first = values[..., :half]
    second = values[..., half:]
    return jnp.concatenate(
        [first * cosine - second * sine, second * cosine + first * sine], axis=-1
    )


def rotate_back(values, cosine, sine):
    half = values.shape[-1] // 2
    first = values[..., :half]
    second = values[..., half:]
    return jnp.concatenate(
        [first * cosine + second * sine, second * cosine - first * sine], axis=-1
    )


def sequence_rows(order_flat, first_row, count, block):
    rows = first_row + jnp.arange(count, dtype=jnp.int32)
    slots = rows // block
    table = jnp.arange(order_flat.shape[0], dtype=jnp.int32)
    picked = jnp.sum(jnp.where(slots[:, None] == table[None, :], order_flat[None, :], 0), axis=1)
    return picked * block + rows % block


def pad_rows(shard, rows):
    return jnp.pad(shard, (0, rows - shard.shape[0]))


def a2a_sum(x, axis_name, count):
    pieces = lax.all_to_all(x.reshape(count, -1, *x.shape[1:]), axis_name, 0, 0)
    return jnp.sum(pieces.astype(jnp.float32), axis=0)


def a2a_gather(x, axis_name, count):
    copies = jnp.broadcast_to(x[None], (count,) + x.shape)
    return lax.all_to_all(copies, axis_name, 0, 0).reshape(count * x.shape[0], *x.shape[1:])


def body(
    inputs,
    out_grad,
    positions,
    block_order,
    w_query,
    w_key,
    w_value,
    w_output,
    w_gate,
    w_up,
    w_down,
    gain_in,
    gain_query,
    gain_key,
    gain_attn,
    gain_pre,
    gain_post,
):
    f32 = jnp.float32
    low = jnp.bfloat16
    tokens = inputs[0]
    local = tokens.shape[0]
    parts = lax.axis_size("ctx")
    groups = lax.axis_size("fsdp")
    total = local * parts
    block = local // 2
    width_shard = w_query.shape[0]
    qw = w_query.shape[1]
    kw = w_key.shape[1]
    gain_cols = jnp.stack(
        [
            gain_in,
            gain_attn,
            gain_pre,
            gain_post,
            pad_rows(gain_query, width_shard),
            pad_rows(gain_key, width_shard),
        ],
        axis=1,
    )
    gain_cols = jnp.pad(gain_cols, ((0, 0), (0, 128 - gain_cols.shape[1])))
    packed = jnp.concatenate([w_query, w_key, w_value, gain_cols], axis=1)
    packed_all = lax.all_gather(packed, "fsdp", axis=0, tiled=True)
    full_output_t = lax.all_gather(w_output.T, "fsdp", axis=0, tiled=True)
    o1 = qw
    o2 = o1 + kw
    o3 = o2 + kw
    o4 = o3 + w_output.shape[0]
    full_query = packed_all[:, :o1]
    full_key = packed_all[:, o1:o2]
    full_value = packed_all[:, o2:o3]
    gains_all = packed_all[:, o3:].astype(f32)
    head_shard = gain_query.shape[0]

    def head_gain(col):
        return col.reshape(groups, width_shard)[:, :head_shard].reshape(-1)

    norm_in = gains_all[:, 0]
    norm_attn = gains_all[:, 1]
    norm_pre = gains_all[:, 2]
    norm_post = gains_all[:, 3]
    norm_query = head_gain(gains_all[:, 4])
    norm_key = head_gain(gains_all[:, 5])
    ctx_index = lax.axis_index("ctx")
    order_flat = block_order.reshape(-1)
    my_seq = sequence_rows(order_flat, ctx_index * local, local, block)
    all_seq = sequence_rows(order_flat, 0, total, block)
    flat_in = tokens.astype(f32)
    normed_full, unit_in, inv_in = norm_forward(flat_in, norm_in)
    normed_in = normed_full.astype(low)
    queries = jnp.dot(normed_in, full_query, preferred_element_type=f32).reshape(local, H, HD)
    keys_raw = jnp.dot(normed_in, full_key, preferred_element_type=f32)
    values = jnp.dot(normed_in, full_value, preferred_element_type=f32).astype(low)
    query_normed, query_unit, query_inv = norm_forward(queries, norm_query)
    key_normed, key_unit, key_inv = norm_forward(keys_raw, norm_key)
    cosine, sine = rope_tables(positions[0], HD)
    scale = HD ** (-0.5)
    query_rot = (rotate(query_normed, cosine[:, None, :], sine[:, None, :]) * scale).astype(low)
    key_rot = rotate(key_normed, cosine, sine).astype(low)
    kv_all = a2a_gather(jnp.concatenate([key_rot, values], axis=1), "ctx", parts)
    key_all = kv_all[:, :HD]
    value_all = kv_all[:, HD:]
    scores = jnp.einsum("qhd,kd->hqk", query_rot, key_all, preferred_element_type=f32)
    allowed = my_seq[:, None] >= all_seq[None, :]
    scores = jnp.where(allowed[None], scores, -jnp.inf)
    highest = jnp.max(scores, axis=-1, keepdims=True)
    log_total = highest + jnp.log(jnp.sum(jnp.exp(scores - highest), axis=-1, keepdims=True))
    probs_full = jnp.exp(scores - log_total)
    probs = probs_full.astype(low)
    attended = (
        jnp.einsum("hqk,kd->qhd", probs, value_all, preferred_element_type=f32)
        .reshape(local, H * HD)
        .astype(low)
    )
    branch_attn = jnp.einsum("tc,dc->td", attended, full_output_t, preferred_element_type=f32)
    attn_normed, attn_unit, attn_inv = norm_forward(branch_attn, norm_attn)
    residual = flat_in + attn_normed
    pre_full, pre_unit, pre_inv = norm_forward(residual, norm_pre)
    normed_pre = pre_full.astype(low)
    rows_all = lax.all_gather(normed_pre, "fsdp", axis=0, tiled=True)
    gate = jnp.einsum("td,fd->tf", rows_all, w_gate, preferred_element_type=f32)
    upper = jnp.einsum("td,fd->tf", rows_all, w_up, preferred_element_type=f32)
    gelu_value, gelu_slope = gelu_pair(gate)
    hidden = (gelu_value * upper).astype(low)
    branch_ffn = a2a_sum(
        jnp.dot(hidden, w_down, preferred_element_type=f32).astype(jnp.bfloat16), "fsdp", groups
    )
    post_normed, post_unit, post_inv = norm_forward(branch_ffn, norm_post)
    outputs = (residual + post_normed).astype(low)
    grad_out = out_grad[0].astype(f32)
    grad_ffn_full, grad_gain_post = norm_backward(grad_out, post_unit, post_inv, norm_post)
    grad_ffn = grad_ffn_full.astype(low)
    grad_all = lax.all_gather(grad_ffn, "fsdp", axis=0, tiled=True)
    grad_hidden = jnp.einsum("td,fd->tf", grad_all, w_down, preferred_element_type=f32)
    grad_gate = (grad_hidden * upper * gelu_slope).astype(low)
    grad_up = (grad_hidden * gelu_value).astype(low)
    shard_gate = jnp.einsum("tf,td->fd", grad_gate, rows_all, preferred_element_type=f32)
    shard_up = jnp.einsum("tf,td->fd", grad_up, rows_all, preferred_element_type=f32)
    shard_down = jnp.einsum("tf,td->fd", hidden, grad_all, preferred_element_type=f32)
    pre_partial = (
        jnp.dot(grad_gate, w_gate, preferred_element_type=f32)
        + jnp.dot(grad_up, w_up, preferred_element_type=f32)
    ).astype(jnp.bfloat16)
    ffn_packed = jnp.concatenate([shard_gate, shard_up, shard_down], axis=0).astype(low)
    ffn_rows = ffn_packed.shape[0]
    ffn_step = 8 * parts
    ffn_packed = jnp.pad(ffn_packed, ((0, -ffn_rows % ffn_step), (0, 0)))
    ffn_packed, pre_partial = lax.optimization_barrier((ffn_packed, pre_partial))
    ffn_mine = lax.psum_scatter(ffn_packed, "ctx", scatter_dimension=0, tiled=True)
    grad_pre = a2a_sum(pre_partial, "fsdp", groups)
    grad_from_pre, grad_gain_pre = norm_backward(grad_pre, pre_unit, pre_inv, norm_pre)
    grad_residual = grad_out + grad_from_pre
    grad_branch_full, grad_gain_attn = norm_backward(grad_residual, attn_unit, attn_inv, norm_attn)
    grad_branch = grad_branch_full.astype(low)
    term_output = jnp.einsum("tc,td->cd", attended, grad_branch, preferred_element_type=f32)
    grad_attended = jnp.einsum(
        "td,dc->tc", grad_branch, full_output_t, preferred_element_type=f32
    ).astype(low)
    grad_heads = grad_attended.reshape(local, H, HD)
    attended_heads = attended.reshape(local, H, HD)
    delta = jnp.transpose(jnp.sum(grad_heads.astype(f32) * attended_heads.astype(f32), axis=-1))[
        :, :, None
    ]
    grad_probs = jnp.einsum("qhd,kd->hqk", grad_heads, value_all, preferred_element_type=f32)
    grad_scores = (probs_full * (grad_probs - delta)).astype(low)
    value_term = jnp.einsum("hqk,qhd->kd", probs, grad_heads, preferred_element_type=f32)
    key_term = jnp.einsum("hqk,qhd->kd", grad_scores, query_rot, preferred_element_type=f32)
    key_value_terms = jnp.concatenate([key_term, value_term], axis=1)
    grad_query_rot = jnp.einsum("hqk,kd->qhd", grad_scores, key_all, preferred_element_type=f32)
    summed_kv = a2a_sum(key_value_terms.astype(jnp.bfloat16), "ctx", parts)
    ffn_mine, summed_kv = lax.optimization_barrier((ffn_mine, summed_kv))
    grad_key_rot = summed_kv[:, :HD]
    grad_values = summed_kv[:, HD:].astype(low)
    grad_q_normed = rotate_back(grad_query_rot * scale, cosine[:, None, :], sine[:, None, :])
    grad_q_full, grad_gain_query = norm_backward(grad_q_normed, query_unit, query_inv, norm_query)
    grad_k_normed = rotate_back(grad_key_rot, cosine, sine)
    grad_k_full, grad_gain_key = norm_backward(grad_k_normed, key_unit, key_inv, norm_key)
    grad_q_in = grad_q_full.reshape(local, H * HD).astype(low)
    grad_k_in = grad_k_full.astype(low)
    term_query = jnp.einsum("tc,td->cd", grad_q_in, normed_in, preferred_element_type=f32)
    term_key = jnp.einsum("tc,td->cd", grad_k_in, normed_in, preferred_element_type=f32)
    term_value = jnp.einsum("tc,td->cd", grad_values, normed_in, preferred_element_type=f32)
    grad_normed = (
        jnp.einsum("tc,dc->td", grad_q_in, full_query, preferred_element_type=f32)
        + jnp.einsum("tc,dc->td", grad_k_in, full_key, preferred_element_type=f32)
        + jnp.einsum("tc,dc->td", grad_values, full_value, preferred_element_type=f32)
    )
    grad_from_in, grad_gain_in = norm_backward(grad_normed, unit_in, inv_in, norm_in)
    in_grad = (grad_residual + grad_from_in).astype(low)

    def head_col(g):
        return jnp.pad(g.reshape(groups, head_shard), ((0, 0), (0, width_shard - head_shard))).reshape(-1)

    gain_block = jnp.stack(
        [
            grad_gain_in,
            grad_gain_attn,
            grad_gain_pre,
            grad_gain_post,
            head_col(grad_gain_query),
            head_col(grad_gain_key),
        ],
        axis=0,
    )
    gain_block = jnp.pad(gain_block, ((0, 8 - gain_block.shape[0]), (0, 0))).astype(low)
    gain_block = jnp.transpose(gain_block.reshape(8, groups, width_shard), (1, 0, 2))
    gain_shard = jnp.sum(lax.all_to_all(gain_block, "fsdp", 0, 0).astype(f32), axis=0)

    def ctx_sum(x):
        chunks = x.reshape(parts, -1, x.shape[1])
        mine = jnp.sum(lax.all_to_all(chunks, "ctx", 0, 0).astype(f32), axis=0).astype(low)
        return lax.all_to_all(jnp.broadcast_to(mine[None], chunks.shape), "ctx", 0, 0).reshape(x.shape)

    ffn_units = shard_gate.shape[0]
    ffn_sums = a2a_gather(ffn_mine, "ctx", parts)[:ffn_rows].astype(f32)
    grad_packed = jnp.concatenate([term_query, term_key, term_value, term_output], axis=0).astype(low)
    grad_shard = jnp.concatenate(
        [
            lax.psum_scatter(grad_packed, "fsdp", scatter_dimension=1, tiled=True),
            gain_shard.astype(low),
        ],
        axis=0,
    )
    totals = (
        ctx_sum(grad_shard),
        ffn_sums[:ffn_units],
        ffn_sums[ffn_units : 2 * ffn_units],
        ffn_sums[2 * ffn_units :],
    )
    grad_shard = totals[0].astype(f32)
    grows = grad_shard[o4:]
    return (
        outputs[None],
        in_grad[None],
        grad_shard[:o1].T,
        grad_shard[o1:o2].T,
        grad_shard[o2:o3].T,
        grad_shard[o3:o4],
        totals[1].astype(f32),
        totals[2].astype(f32),
        totals[3].astype(f32),
        grows[0],
        grows[4, :head_shard],
        grows[5, :head_shard],
        grows[1],
        grows[2],
        grows[3],
    )


def solution(mesh):
    placed = (
        P("fsdp", "ctx", None),
        P("fsdp", "ctx", None),
        P("fsdp", "ctx"),
        P(),
        P("fsdp", None),
        P("fsdp", None),
        P("fsdp", None),
        P(None, "fsdp"),
        P("fsdp", None),
        P("fsdp", None),
        P("fsdp", None),
        P("fsdp"),
        P("fsdp"),
        P("fsdp"),
        P("fsdp"),
        P("fsdp"),
        P("fsdp"),
    )
    return jax.shard_map(
        body,
        mesh=mesh,
        in_specs=placed,
        out_specs=(
            P("fsdp", "ctx", None),
            P("fsdp", "ctx", None),
            P("fsdp", None),
            P("fsdp", None),
            P("fsdp", None),
            P(None, "fsdp"),
            P("fsdp", None),
            P("fsdp", None),
            P("fsdp", None),
            P("fsdp"),
            P("fsdp"),
            P("fsdp"),
            P("fsdp"),
            P("fsdp"),
            P("fsdp"),
        ),
        check_vma=False,
    )
```

```python
import jax
import jax.numpy as jnp
from jax import lax
from jax.sharding import PartitionSpec as P

H = 4
HD = 256


EPS = 1e-06
ROPE_BASE = 1000000.0
GELU_C = 0.7978845608028654
GELU_A = 0.044715


def norm_forward(values, gain):
    inverse = lax.rsqrt(jnp.mean(values * values, axis=-1, keepdims=True) + EPS)
    unit = values * inverse
    return (unit * gain, unit, inverse)


def norm_backward(upstream, unit, inverse, gain):
    scaled = upstream * gain
    inner = jnp.mean(scaled * unit, axis=-1, keepdims=True)
    leading = tuple(range(upstream.ndim - 1))
    return (inverse * (scaled - unit * inner), jnp.sum(upstream * unit, axis=leading))


def gelu_pair(gate):
    inner = GELU_C * (gate + GELU_A * gate * gate * gate)
    tangent = jnp.tanh(inner)
    value = 0.5 * gate * (1.0 + tangent)
    slope = 0.5 * (1.0 + tangent) + 0.5 * gate * (1.0 - tangent * tangent) * GELU_C * (
        1.0 + 3.0 * GELU_A * gate * gate
    )
    return (value, slope)


def rope_tables(positions, width):
    half = width // 2
    freqs = ROPE_BASE ** (-2.0 * jnp.arange(half, dtype=jnp.float32) / width)
    angles = positions.astype(jnp.float32)[:, None] * freqs[None, :]
    return (jnp.cos(angles), jnp.sin(angles))


def rotate(values, cosine, sine):
    half = values.shape[-1] // 2
    first = values[..., :half]
    second = values[..., half:]
    return jnp.concatenate(
        [first * cosine - second * sine, second * cosine + first * sine], axis=-1
    )


def rotate_back(values, cosine, sine):
    half = values.shape[-1] // 2
    first = values[..., :half]
    second = values[..., half:]
    return jnp.concatenate(
        [first * cosine + second * sine, second * cosine - first * sine], axis=-1
    )


def sequence_rows(order_flat, first_row, count, block):
    rows = first_row + jnp.arange(count, dtype=jnp.int32)
    slots = rows // block
    table = jnp.arange(order_flat.shape[0], dtype=jnp.int32)
    picked = jnp.sum(jnp.where(slots[:, None] == table[None, :], order_flat[None, :], 0), axis=1)
    return picked * block + rows % block


def pad_rows(shard, rows):
    return jnp.pad(shard, (0, rows - shard.shape[0]))


def a2a_sum(x, axis_name, count):
    pieces = lax.all_to_all(x.reshape(count, -1, *x.shape[1:]), axis_name, 0, 0)
    return jnp.sum(pieces.astype(jnp.float32), axis=0)


def a2a_gather(x, axis_name, count):
    copies = jnp.broadcast_to(x[None], (count,) + x.shape)
    return lax.all_to_all(copies, axis_name, 0, 0).reshape(count * x.shape[0], *x.shape[1:])


def body(
    inputs,
    out_grad,
    positions,
    block_order,
    w_query,
    w_key,
    w_value,
    w_output,
    w_gate,
    w_up,
    w_down,
    gain_in,
    gain_query,
    gain_key,
    gain_attn,
    gain_pre,
    gain_post,
):
    f32 = jnp.float32
    low = jnp.bfloat16
    tokens = inputs[0]
    local = tokens.shape[0]
    parts = lax.axis_size("ctx")
    groups = lax.axis_size("fsdp")
    total = local * parts
    block = local // 2
    width_shard = w_query.shape[0]
    qw = w_query.shape[1]
    kw = w_key.shape[1]
    gain_cols = jnp.stack(
        [
            gain_in,
            gain_attn,
            gain_pre,
            gain_post,
            pad_rows(gain_query, width_shard),
            pad_rows(gain_key, width_shard),
        ],
        axis=1,
    )
    gain_cols = jnp.pad(gain_cols, ((0, 0), (0, 128 - gain_cols.shape[1])))
    packed = jnp.concatenate([w_query, w_key, w_value, w_output.T, gain_cols], axis=1)
    packed_all = lax.all_gather(packed, "fsdp", axis=0, tiled=True)
    o1 = qw
    o2 = o1 + kw
    o3 = o2 + kw
    o4 = o3 + w_output.shape[0]
    full_query = packed_all[:, :o1]
    full_key = packed_all[:, o1:o2]
    full_value = packed_all[:, o2:o3]
    full_output_t = packed_all[:, o3:o4]
    gains_all = packed_all[:, o4:].astype(f32)
    head_shard = gain_query.shape[0]

    def head_gain(col):
        return col.reshape(groups, width_shard)[:, :head_shard].reshape(-1)

    norm_in = gains_all[:, 0]
    norm_attn = gains_all[:, 1]
    norm_pre = gains_all[:, 2]
    norm_post = gains_all[:, 3]
    norm_query = head_gain(gains_all[:, 4])
    norm_key = head_gain(gains_all[:, 5])
    ctx_index = lax.axis_index("ctx")
    order_flat = block_order.reshape(-1)
    my_seq = sequence_rows(order_flat, ctx_index * local, local, block)
    all_seq = sequence_rows(order_flat, 0, total, block)
    flat_in = tokens.astype(f32)
    normed_full, unit_in, inv_in = norm_forward(flat_in, norm_in)
    normed_in = normed_full.astype(low)
    queries = jnp.dot(normed_in, full_query, preferred_element_type=f32).reshape(local, H, HD)
    keys_raw = jnp.dot(normed_in, full_key, preferred_element_type=f32)
    values = jnp.dot(normed_in, full_value, preferred_element_type=f32).astype(low)
    query_normed, query_unit, query_inv = norm_forward(queries, norm_query)
    key_normed, key_unit, key_inv = norm_forward(keys_raw, norm_key)
    cosine, sine = rope_tables(positions[0], HD)
    scale = HD ** (-0.5)
    query_rot = (rotate(query_normed, cosine[:, None, :], sine[:, None, :]) * scale).astype(low)
    key_rot = rotate(key_normed, cosine, sine).astype(low)
    kv_all = a2a_gather(jnp.concatenate([key_rot, values], axis=1), "ctx", parts)
    key_all = kv_all[:, :HD]
    value_all = kv_all[:, HD:]
    scores = jnp.einsum("qhd,kd->hqk", query_rot, key_all, preferred_element_type=f32)
    allowed = my_seq[:, None] >= all_seq[None, :]
    scores = jnp.where(allowed[None], scores, -jnp.inf)
    highest = jnp.max(scores, axis=-1, keepdims=True)
    log_total = highest + jnp.log(jnp.sum(jnp.exp(scores - highest), axis=-1, keepdims=True))
    probs_full = jnp.exp(scores - log_total)
    probs = probs_full.astype(low)
    attended = (
        jnp.einsum("hqk,kd->qhd", probs, value_all, preferred_element_type=f32)
        .reshape(local, H * HD)
        .astype(low)
    )
    branch_attn = jnp.einsum("tc,dc->td", attended, full_output_t, preferred_element_type=f32)
    attn_normed, attn_unit, attn_inv = norm_forward(branch_attn, norm_attn)
    residual = flat_in + attn_normed
    pre_full, pre_unit, pre_inv = norm_forward(residual, norm_pre)
    normed_pre = pre_full.astype(low)
    rows_all = lax.all_gather(normed_pre, "fsdp", axis=0, tiled=True)
    gate = jnp.einsum("td,fd->tf", rows_all, w_gate, preferred_element_type=f32)
    upper = jnp.einsum("td,fd->tf", rows_all, w_up, preferred_element_type=f32)
    gelu_value, gelu_slope = gelu_pair(gate)
    hidden = (gelu_value * upper).astype(low)
    branch_ffn = a2a_sum(
        jnp.dot(hidden, w_down, preferred_element_type=f32).astype(jnp.bfloat16), "fsdp", groups
    )
    post_normed, post_unit, post_inv = norm_forward(branch_ffn, norm_post)
    outputs = (residual + post_normed).astype(low)
    grad_out = out_grad[0].astype(f32)
    grad_ffn_full, grad_gain_post = norm_backward(grad_out, post_unit, post_inv, norm_post)
    grad_ffn = grad_ffn_full.astype(low)
    grad_all = lax.all_gather(grad_ffn, "fsdp", axis=0, tiled=True)
    grad_hidden = jnp.einsum("td,fd->tf", grad_all, w_down, preferred_element_type=f32)
    grad_gate = (grad_hidden * upper * gelu_slope).astype(low)
    grad_up = (grad_hidden * gelu_value).astype(low)
    shard_gate = jnp.einsum("tf,td->fd", grad_gate, rows_all, preferred_element_type=f32)
    shard_up = jnp.einsum("tf,td->fd", grad_up, rows_all, preferred_element_type=f32)
    shard_down = jnp.einsum("tf,td->fd", hidden, grad_all, preferred_element_type=f32)
    pre_partial = (
        jnp.dot(grad_gate, w_gate, preferred_element_type=f32)
        + jnp.dot(grad_up, w_up, preferred_element_type=f32)
    ).astype(jnp.bfloat16)
    ffn_packed = jnp.concatenate([shard_gate, shard_up, shard_down], axis=0).astype(low)
    ffn_packed, pre_partial = lax.optimization_barrier((ffn_packed, pre_partial))
    grad_pre = a2a_sum(pre_partial, "fsdp", groups)
    ffn_mine = a2a_sum(ffn_packed, "ctx", parts).astype(low)
    grad_from_pre, grad_gain_pre = norm_backward(grad_pre, pre_unit, pre_inv, norm_pre)
    grad_residual = grad_out + grad_from_pre
    grad_branch_full, grad_gain_attn = norm_backward(grad_residual, attn_unit, attn_inv, norm_attn)
    grad_branch = grad_branch_full.astype(low)
    term_output = jnp.einsum("tc,td->cd", attended, grad_branch, preferred_element_type=f32)
    grad_attended = jnp.einsum(
        "td,dc->tc", grad_branch, full_output_t, preferred_element_type=f32
    ).astype(low)
    grad_heads = grad_attended.reshape(local, H, HD)
    attended_heads = attended.reshape(local, H, HD)
    delta = jnp.transpose(jnp.sum(grad_heads.astype(f32) * attended_heads.astype(f32), axis=-1))[
        :, :, None
    ]
    grad_probs = jnp.einsum("qhd,kd->hqk", grad_heads, value_all, preferred_element_type=f32)
    grad_scores = (probs_full * (grad_probs - delta)).astype(low)
    value_term = jnp.einsum("hqk,qhd->kd", probs, grad_heads, preferred_element_type=f32)
    key_term = jnp.einsum("hqk,qhd->kd", grad_scores, query_rot, preferred_element_type=f32)
    key_value_terms = jnp.concatenate([key_term, value_term], axis=1)
    grad_query_rot = jnp.einsum("hqk,kd->qhd", grad_scores, key_all, preferred_element_type=f32)
    summed_kv = a2a_sum(key_value_terms.astype(jnp.bfloat16), "ctx", parts)
    ffn_sums = a2a_gather(ffn_mine, "ctx", parts)
    ffn_sums, summed_kv = lax.optimization_barrier((ffn_sums, summed_kv))
    grad_key_rot = summed_kv[:, :HD]
    grad_values = summed_kv[:, HD:].astype(low)
    grad_q_normed = rotate_back(grad_query_rot * scale, cosine[:, None, :], sine[:, None, :])
    grad_q_full, grad_gain_query = norm_backward(grad_q_normed, query_unit, query_inv, norm_query)
    grad_k_normed = rotate_back(grad_key_rot, cosine, sine)
    grad_k_full, grad_gain_key = norm_backward(grad_k_normed, key_unit, key_inv, norm_key)
    grad_q_in = grad_q_full.reshape(local, H * HD).astype(low)
    grad_k_in = grad_k_full.astype(low)
    term_query = jnp.einsum("tc,td->cd", grad_q_in, normed_in, preferred_element_type=f32)
    term_key = jnp.einsum("tc,td->cd", grad_k_in, normed_in, preferred_element_type=f32)
    term_value = jnp.einsum("tc,td->cd", grad_values, normed_in, preferred_element_type=f32)
    grad_normed = (
        jnp.einsum("tc,dc->td", grad_q_in, full_query, preferred_element_type=f32)
        + jnp.einsum("tc,dc->td", grad_k_in, full_key, preferred_element_type=f32)
        + jnp.einsum("tc,dc->td", grad_values, full_value, preferred_element_type=f32)
    )
    grad_from_in, grad_gain_in = norm_backward(grad_normed, unit_in, inv_in, norm_in)
    in_grad = (grad_residual + grad_from_in).astype(low)

    def head_col(g):
        return jnp.pad(g.reshape(groups, head_shard), ((0, 0), (0, width_shard - head_shard))).reshape(-1)

    gain_block = jnp.stack(
        [
            grad_gain_in,
            grad_gain_attn,
            grad_gain_pre,
            grad_gain_post,
            head_col(grad_gain_query),
            head_col(grad_gain_key),
        ],
        axis=0,
    )
    gain_block = jnp.pad(gain_block, ((0, 8 - gain_block.shape[0]), (0, 0))).astype(low)
    gain_block = jnp.transpose(gain_block.reshape(8, groups, width_shard), (1, 0, 2))
    gain_shard = jnp.sum(lax.all_to_all(gain_block, "fsdp", 0, 0).astype(f32), axis=0)

    def ctx_sum(x):
        chunks = x.reshape(parts, -1, x.shape[1])
        mine = jnp.sum(lax.all_to_all(chunks, "ctx", 0, 0).astype(f32), axis=0).astype(low)
        return lax.all_to_all(jnp.broadcast_to(mine[None], chunks.shape), "ctx", 0, 0).reshape(x.shape)

    ffn_units = shard_gate.shape[0]
    ffn_sums = ffn_sums.astype(f32)
    grad_packed = jnp.concatenate([term_query, term_key, term_value, term_output], axis=0).astype(low)
    grad_shard = jnp.concatenate(
        [
            lax.psum_scatter(grad_packed, "fsdp", scatter_dimension=1, tiled=True),
            gain_shard.astype(low),
        ],
        axis=0,
    )
    totals = (
        ctx_sum(grad_shard),
        ffn_sums[:ffn_units],
        ffn_sums[ffn_units : 2 * ffn_units],
        ffn_sums[2 * ffn_units :],
    )
    grad_shard = totals[0].astype(f32)
    grows = grad_shard[o4:]
    return (
        outputs[None],
        in_grad[None],
        grad_shard[:o1].T,
        grad_shard[o1:o2].T,
        grad_shard[o2:o3].T,
        grad_shard[o3:o4],
        totals[1].astype(f32),
        totals[2].astype(f32),
        totals[3].astype(f32),
        grows[0],
        grows[4, :head_shard],
        grows[5, :head_shard],
        grows[1],
        grows[2],
        grows[3],
    )


def solution(mesh):
    placed = (
        P("fsdp", "ctx", None),
        P("fsdp", "ctx", None),
        P("fsdp", "ctx"),
        P(),
        P("fsdp", None),
        P("fsdp", None),
        P("fsdp", None),
        P(None, "fsdp"),
        P("fsdp", None),
        P("fsdp", None),
        P("fsdp", None),
        P("fsdp"),
        P("fsdp"),
        P("fsdp"),
        P("fsdp"),
        P("fsdp"),
        P("fsdp"),
    )
    return jax.shard_map(
        body,
        mesh=mesh,
        in_specs=placed,
        out_specs=(
            P("fsdp", "ctx", None),
            P("fsdp", "ctx", None),
            P("fsdp", None),
            P("fsdp", None),
            P("fsdp", None),
            P(None, "fsdp"),
            P("fsdp", None),
            P("fsdp", None),
            P("fsdp", None),
            P("fsdp"),
            P("fsdp"),
            P("fsdp"),
            P("fsdp"),
            P("fsdp"),
            P("fsdp"),
        ),
        check_vma=False,
    )
```

```python
import jax
import jax.numpy as jnp
from jax import lax
from jax.sharding import PartitionSpec as P

H = 4
HD = 256


EPS = 1e-06
ROPE_BASE = 1000000.0
GELU_C = 0.7978845608028654
GELU_A = 0.044715


def norm_forward(values, gain):
    inverse = lax.rsqrt(jnp.mean(values * values, axis=-1, keepdims=True) + EPS)
    unit = values * inverse
    return (unit * gain, unit, inverse)


def norm_backward(upstream, unit, inverse, gain):
    scaled = upstream * gain
    inner = jnp.mean(scaled * unit, axis=-1, keepdims=True)
    leading = tuple(range(upstream.ndim - 1))
    return (inverse * (scaled - unit * inner), jnp.sum(upstream * unit, axis=leading))


def gelu_pair(gate):
    inner = GELU_C * (gate + GELU_A * gate * gate * gate)
    tangent = jnp.tanh(inner)
    value = 0.5 * gate * (1.0 + tangent)
    slope = 0.5 * (1.0 + tangent) + 0.5 * gate * (1.0 - tangent * tangent) * GELU_C * (
        1.0 + 3.0 * GELU_A * gate * gate
    )
    return (value, slope)


def rope_tables(positions, width):
    half = width // 2
    freqs = ROPE_BASE ** (-2.0 * jnp.arange(half, dtype=jnp.float32) / width)
    angles = positions.astype(jnp.float32)[:, None] * freqs[None, :]
    return (jnp.cos(angles), jnp.sin(angles))


def rotate(values, cosine, sine):
    half = values.shape[-1] // 2
    first = values[..., :half]
    second = values[..., half:]
    return jnp.concatenate(
        [first * cosine - second * sine, second * cosine + first * sine], axis=-1
    )


def rotate_back(values, cosine, sine):
    half = values.shape[-1] // 2
    first = values[..., :half]
    second = values[..., half:]
    return jnp.concatenate(
        [first * cosine + second * sine, second * cosine - first * sine], axis=-1
    )


def sequence_rows(order_flat, first_row, count, block):
    rows = first_row + jnp.arange(count, dtype=jnp.int32)
    slots = rows // block
    table = jnp.arange(order_flat.shape[0], dtype=jnp.int32)
    picked = jnp.sum(jnp.where(slots[:, None] == table[None, :], order_flat[None, :], 0), axis=1)
    return picked * block + rows % block


def pad_rows(shard, rows):
    return jnp.pad(shard, (0, rows - shard.shape[0]))


def a2a_sum(x, axis_name, count):
    pieces = lax.all_to_all(x.reshape(count, -1, *x.shape[1:]), axis_name, 0, 0)
    return jnp.sum(pieces.astype(jnp.float32), axis=0)


def a2a_gather(x, axis_name, count):
    copies = jnp.broadcast_to(x[None], (count,) + x.shape)
    return lax.all_to_all(copies, axis_name, 0, 0).reshape(count * x.shape[0], *x.shape[1:])


def body(
    inputs,
    out_grad,
    positions,
    block_order,
    w_query,
    w_key,
    w_value,
    w_output,
    w_gate,
    w_up,
    w_down,
    gain_in,
    gain_query,
    gain_key,
    gain_attn,
    gain_pre,
    gain_post,
):
    f32 = jnp.float32
    low = jnp.bfloat16
    tokens = inputs[0]
    local = tokens.shape[0]
    parts = lax.axis_size("ctx")
    groups = lax.axis_size("fsdp")
    total = local * parts
    block = local // 2
    width_shard = w_query.shape[0]
    qw = w_query.shape[1]
    kw = w_key.shape[1]
    gain_cols = jnp.stack(
        [
            gain_in,
            gain_attn,
            gain_pre,
            gain_post,
            pad_rows(gain_query, width_shard),
            pad_rows(gain_key, width_shard),
        ],
        axis=1,
    )
    gain_cols = jnp.pad(gain_cols, ((0, 0), (0, 128 - gain_cols.shape[1])))
    packed = jnp.concatenate([w_query, w_key, w_value, gain_cols], axis=1)
    packed_all = lax.all_gather(packed, "fsdp", axis=0, tiled=True)
    full_output_t = a2a_gather(w_output.T, "fsdp", groups)
    o1 = qw
    o2 = o1 + kw
    o3 = o2 + kw
    o4 = o3 + w_output.shape[0]
    full_query = packed_all[:, :o1]
    full_key = packed_all[:, o1:o2]
    full_value = packed_all[:, o2:o3]
    gains_all = packed_all[:, o3:].astype(f32)
    head_shard = gain_query.shape[0]

    def head_gain(col):
        return col.reshape(groups, width_shard)[:, :head_shard].reshape(-1)

    norm_in = gains_all[:, 0]
    norm_attn = gains_all[:, 1]
    norm_pre = gains_all[:, 2]
    norm_post = gains_all[:, 3]
    norm_query = head_gain(gains_all[:, 4])
    norm_key = head_gain(gains_all[:, 5])
    ctx_index = lax.axis_index("ctx")
    order_flat = block_order.reshape(-1)
    my_seq = sequence_rows(order_flat, ctx_index * local, local, block)
    all_seq = sequence_rows(order_flat, 0, total, block)
    flat_in = tokens.astype(f32)
    normed_full, unit_in, inv_in = norm_forward(flat_in, norm_in)
    normed_in = normed_full.astype(low)
    queries = jnp.dot(normed_in, full_query, preferred_element_type=f32).reshape(local, H, HD)
    keys_raw = jnp.dot(normed_in, full_key, preferred_element_type=f32)
    values = jnp.dot(normed_in, full_value, preferred_element_type=f32).astype(low)
    query_normed, query_unit, query_inv = norm_forward(queries, norm_query)
    key_normed, key_unit, key_inv = norm_forward(keys_raw, norm_key)
    cosine, sine = rope_tables(positions[0], HD)
    scale = HD ** (-0.5)
    query_rot = (rotate(query_normed, cosine[:, None, :], sine[:, None, :]) * scale).astype(low)
    key_rot = rotate(key_normed, cosine, sine).astype(low)
    kv_all = a2a_gather(jnp.concatenate([key_rot, values], axis=1), "ctx", parts)
    key_all = kv_all[:, :HD]
    value_all = kv_all[:, HD:]
    scores = jnp.einsum("qhd,kd->hqk", query_rot, key_all, preferred_element_type=f32)
    allowed = my_seq[:, None] >= all_seq[None, :]
    scores = jnp.where(allowed[None], scores, -jnp.inf)
    highest = jnp.max(scores, axis=-1, keepdims=True)
    log_total = highest + jnp.log(jnp.sum(jnp.exp(scores - highest), axis=-1, keepdims=True))
    probs_full = jnp.exp(scores - log_total)
    probs = probs_full.astype(low)
    attended = (
        jnp.einsum("hqk,kd->qhd", probs, value_all, preferred_element_type=f32)
        .reshape(local, H * HD)
        .astype(low)
    )
    branch_attn = jnp.einsum("tc,dc->td", attended, full_output_t, preferred_element_type=f32)
    attn_normed, attn_unit, attn_inv = norm_forward(branch_attn, norm_attn)
    residual = flat_in + attn_normed
    pre_full, pre_unit, pre_inv = norm_forward(residual, norm_pre)
    normed_pre = pre_full.astype(low)
    rows_all = lax.all_gather(normed_pre, "fsdp", axis=0, tiled=True)
    gate = jnp.einsum("td,fd->tf", rows_all, w_gate, preferred_element_type=f32)
    upper = jnp.einsum("td,fd->tf", rows_all, w_up, preferred_element_type=f32)
    gelu_value, gelu_slope = gelu_pair(gate)
    hidden = (gelu_value * upper).astype(low)
    branch_ffn = a2a_sum(
        jnp.dot(hidden, w_down, preferred_element_type=f32).astype(jnp.bfloat16), "fsdp", groups
    )
    post_normed, post_unit, post_inv = norm_forward(branch_ffn, norm_post)
    outputs = (residual + post_normed).astype(low)
    grad_out = out_grad[0].astype(f32)
    grad_ffn_full, grad_gain_post = norm_backward(grad_out, post_unit, post_inv, norm_post)
    grad_ffn = grad_ffn_full.astype(low)
    grad_all = lax.all_gather(grad_ffn, "fsdp", axis=0, tiled=True)
    grad_hidden = jnp.einsum("td,fd->tf", grad_all, w_down, preferred_element_type=f32)
    grad_gate = (grad_hidden * upper * gelu_slope).astype(low)
    grad_up = (grad_hidden * gelu_value).astype(low)
    shard_gate = jnp.einsum("tf,td->fd", grad_gate, rows_all, preferred_element_type=f32)
    shard_up = jnp.einsum("tf,td->fd", grad_up, rows_all, preferred_element_type=f32)
    shard_down = jnp.einsum("tf,td->fd", hidden, grad_all, preferred_element_type=f32)
    grad_pre = a2a_sum(
        (
            jnp.dot(grad_gate, w_gate, preferred_element_type=f32)
            + jnp.dot(grad_up, w_up, preferred_element_type=f32)
        ).astype(jnp.bfloat16),
        "fsdp",
        groups,
    )
    grad_from_pre, grad_gain_pre = norm_backward(grad_pre, pre_unit, pre_inv, norm_pre)
    grad_residual = grad_out + grad_from_pre
    grad_branch_full, grad_gain_attn = norm_backward(grad_residual, attn_unit, attn_inv, norm_attn)
    grad_branch = grad_branch_full.astype(low)
    term_output = jnp.einsum("tc,td->cd", attended, grad_branch, preferred_element_type=f32)
    grad_attended = jnp.einsum(
        "td,dc->tc", grad_branch, full_output_t, preferred_element_type=f32
    ).astype(low)
    grad_heads = grad_attended.reshape(local, H, HD)
    attended_heads = attended.reshape(local, H, HD)
    delta = jnp.transpose(jnp.sum(grad_heads.astype(f32) * attended_heads.astype(f32), axis=-1))[
        :, :, None
    ]
    grad_probs = jnp.einsum("qhd,kd->hqk", grad_heads, value_all, preferred_element_type=f32)
    grad_scores = (probs_full * (grad_probs - delta)).astype(low)
    value_term = jnp.einsum("hqk,qhd->kd", probs, grad_heads, preferred_element_type=f32)
    key_term = jnp.einsum("hqk,qhd->kd", grad_scores, query_rot, preferred_element_type=f32)
    key_value_terms = jnp.concatenate([key_term, value_term], axis=1)
    grad_query_rot = jnp.einsum("hqk,kd->qhd", grad_scores, key_all, preferred_element_type=f32)
    summed_kv = a2a_sum(key_value_terms.astype(jnp.bfloat16), "ctx", parts)
    grad_key_rot = summed_kv[:, :HD]
    grad_values = summed_kv[:, HD:].astype(low)
    grad_q_normed = rotate_back(grad_query_rot * scale, cosine[:, None, :], sine[:, None, :])
    grad_q_full, grad_gain_query = norm_backward(grad_q_normed, query_unit, query_inv, norm_query)
    grad_k_normed = rotate_back(grad_key_rot, cosine, sine)
    grad_k_full, grad_gain_key = norm_backward(grad_k_normed, key_unit, key_inv, norm_key)
    grad_q_in = grad_q_full.reshape(local, H * HD).astype(low)
    grad_k_in = grad_k_full.astype(low)
    term_query = jnp.einsum("tc,td->cd", grad_q_in, normed_in, preferred_element_type=f32)
    term_key = jnp.einsum("tc,td->cd", grad_k_in, normed_in, preferred_element_type=f32)
    term_value = jnp.einsum("tc,td->cd", grad_values, normed_in, preferred_element_type=f32)
    grad_normed = (
        jnp.einsum("tc,dc->td", grad_q_in, full_query, preferred_element_type=f32)
        + jnp.einsum("tc,dc->td", grad_k_in, full_key, preferred_element_type=f32)
        + jnp.einsum("tc,dc->td", grad_values, full_value, preferred_element_type=f32)
    )
    grad_from_in, grad_gain_in = norm_backward(grad_normed, unit_in, inv_in, norm_in)
    in_grad = (grad_residual + grad_from_in).astype(low)

    def head_col(g):
        return jnp.pad(g.reshape(groups, head_shard), ((0, 0), (0, width_shard - head_shard))).reshape(-1)

    gain_block = jnp.stack(
        [
            grad_gain_in,
            grad_gain_attn,
            grad_gain_pre,
            grad_gain_post,
            head_col(grad_gain_query),
            head_col(grad_gain_key),
        ],
        axis=0,
    )
    gain_block = jnp.pad(gain_block, ((0, 8 - gain_block.shape[0]), (0, 0))).astype(low)
    gain_block = jnp.transpose(gain_block.reshape(8, groups, width_shard), (1, 0, 2))
    gain_shard = jnp.sum(lax.all_to_all(gain_block, "fsdp", 0, 0).astype(f32), axis=0)

    def ctx_sum(x):
        chunks = x.reshape(parts, -1, x.shape[1])
        mine = jnp.sum(lax.all_to_all(chunks, "ctx", 0, 0).astype(f32), axis=0).astype(low)
        return lax.all_to_all(jnp.broadcast_to(mine[None], chunks.shape), "ctx", 0, 0).reshape(x.shape)

    ffn_units = shard_gate.shape[0]
    ffn_sums = ctx_sum(
        jnp.concatenate([shard_gate, shard_up, shard_down], axis=0).astype(low)
    ).astype(f32)
    grad_packed = jnp.concatenate([term_query, term_key, term_value, term_output], axis=0).astype(low)
    grad_shard = jnp.concatenate(
        [
            lax.psum_scatter(grad_packed, "fsdp", scatter_dimension=1, tiled=True),
            gain_shard.astype(low),
        ],
        axis=0,
    )
    totals = (
        ctx_sum(grad_shard),
        ffn_sums[:ffn_units],
        ffn_sums[ffn_units : 2 * ffn_units],
        ffn_sums[2 * ffn_units :],
    )
    grad_shard = totals[0].astype(f32)
    grows = grad_shard[o4:]
    return (
        outputs[None],
        in_grad[None],
        grad_shard[:o1].T,
        grad_shard[o1:o2].T,
        grad_shard[o2:o3].T,
        grad_shard[o3:o4],
        totals[1].astype(f32),
        totals[2].astype(f32),
        totals[3].astype(f32),
        grows[0],
        grows[4, :head_shard],
        grows[5, :head_shard],
        grows[1],
        grows[2],
        grows[3],
    )


def solution(mesh):
    placed = (
        P("fsdp", "ctx", None),
        P("fsdp", "ctx", None),
        P("fsdp", "ctx"),
        P(),
        P("fsdp", None),
        P("fsdp", None),
        P("fsdp", None),
        P(None, "fsdp"),
        P("fsdp", None),
        P("fsdp", None),
        P("fsdp", None),
        P("fsdp"),
        P("fsdp"),
        P("fsdp"),
        P("fsdp"),
        P("fsdp"),
        P("fsdp"),
    )
    return jax.shard_map(
        body,
        mesh=mesh,
        in_specs=placed,
        out_specs=(
            P("fsdp", "ctx", None),
            P("fsdp", "ctx", None),
            P("fsdp", None),
            P("fsdp", None),
            P("fsdp", None),
            P(None, "fsdp"),
            P("fsdp", None),
            P("fsdp", None),
            P("fsdp", None),
            P("fsdp"),
            P("fsdp"),
            P("fsdp"),
            P("fsdp"),
            P("fsdp"),
            P("fsdp"),
        ),
        check_vma=False,
    )
```

```python
import jax
import jax.numpy as jnp
from jax import lax
from jax.sharding import PartitionSpec as P

H = 4
HD = 256


EPS = 1e-06
ROPE_BASE = 1000000.0
GELU_C = 0.7978845608028654
GELU_A = 0.044715


def norm_forward(values, gain):
    inverse = lax.rsqrt(jnp.mean(values * values, axis=-1, keepdims=True) + EPS)
    unit = values * inverse
    return (unit * gain, unit, inverse)


def norm_backward(upstream, unit, inverse, gain):
    scaled = upstream * gain
    inner = jnp.mean(scaled * unit, axis=-1, keepdims=True)
    leading = tuple(range(upstream.ndim - 1))
    return (inverse * (scaled - unit * inner), jnp.sum(upstream * unit, axis=leading))


def gelu_pair(gate):
    inner = GELU_C * (gate + GELU_A * gate * gate * gate)
    tangent = jnp.tanh(inner)
    value = 0.5 * gate * (1.0 + tangent)
    slope = 0.5 * (1.0 + tangent) + 0.5 * gate * (1.0 - tangent * tangent) * GELU_C * (
        1.0 + 3.0 * GELU_A * gate * gate
    )
    return (value, slope)


def rope_tables(positions, width):
    half = width // 2
    freqs = ROPE_BASE ** (-2.0 * jnp.arange(half, dtype=jnp.float32) / width)
    angles = positions.astype(jnp.float32)[:, None] * freqs[None, :]
    return (jnp.cos(angles), jnp.sin(angles))


def rotate(values, cosine, sine):
    half = values.shape[-1] // 2
    first = values[..., :half]
    second = values[..., half:]
    return jnp.concatenate(
        [first * cosine - second * sine, second * cosine + first * sine], axis=-1
    )


def rotate_back(values, cosine, sine):
    half = values.shape[-1] // 2
    first = values[..., :half]
    second = values[..., half:]
    return jnp.concatenate(
        [first * cosine + second * sine, second * cosine - first * sine], axis=-1
    )


def sequence_rows(order_flat, first_row, count, block):
    rows = first_row + jnp.arange(count, dtype=jnp.int32)
    slots = rows // block
    table = jnp.arange(order_flat.shape[0], dtype=jnp.int32)
    picked = jnp.sum(jnp.where(slots[:, None] == table[None, :], order_flat[None, :], 0), axis=1)
    return picked * block + rows % block


def pad_rows(shard, rows):
    return jnp.pad(shard, (0, rows - shard.shape[0]))


def a2a_sum(x, axis_name, count):
    pieces = lax.all_to_all(x.reshape(count, -1, *x.shape[1:]), axis_name, 0, 0)
    return jnp.sum(pieces.astype(jnp.float32), axis=0)


def a2a_gather(x, axis_name, count):
    copies = jnp.broadcast_to(x[None], (count,) + x.shape)
    return lax.all_to_all(copies, axis_name, 0, 0).reshape(count * x.shape[0], *x.shape[1:])


def body(
    inputs,
    out_grad,
    positions,
    block_order,
    w_query,
    w_key,
    w_value,
    w_output,
    w_gate,
    w_up,
    w_down,
    gain_in,
    gain_query,
    gain_key,
    gain_attn,
    gain_pre,
    gain_post,
):
    f32 = jnp.float32
    low = jnp.bfloat16
    tokens = inputs[0]
    local = tokens.shape[0]
    parts = lax.axis_size("ctx")
    groups = lax.axis_size("fsdp")
    total = local * parts
    block = local // 2
    width_shard = w_query.shape[0]
    qw = w_query.shape[1]
    kw = w_key.shape[1]
    gain_cols = jnp.stack(
        [
            gain_in,
            gain_attn,
            gain_pre,
            gain_post,
            pad_rows(gain_query, width_shard),
            pad_rows(gain_key, width_shard),
        ],
        axis=1,
    )
    gain_cols = jnp.pad(gain_cols, ((0, 0), (0, 128 - gain_cols.shape[1])))
    packed = jnp.concatenate([w_query, w_key, w_value, w_output.T, gain_cols], axis=1)
    packed_all = lax.all_gather(packed, "fsdp", axis=0, tiled=True)
    o1 = qw
    o2 = o1 + kw
    o3 = o2 + kw
    o4 = o3 + w_output.shape[0]
    full_query = packed_all[:, :o1]
    full_key = packed_all[:, o1:o2]
    full_value = packed_all[:, o2:o3]
    full_output_t = packed_all[:, o3:o4]
    gains_all = packed_all[:, o4:].astype(f32)
    head_shard = gain_query.shape[0]

    def head_gain(col):
        return col.reshape(groups, width_shard)[:, :head_shard].reshape(-1)

    norm_in = gains_all[:, 0]
    norm_attn = gains_all[:, 1]
    norm_pre = gains_all[:, 2]
    norm_post = gains_all[:, 3]
    norm_query = head_gain(gains_all[:, 4])
    norm_key = head_gain(gains_all[:, 5])
    ctx_index = lax.axis_index("ctx")
    order_flat = block_order.reshape(-1)
    my_seq = sequence_rows(order_flat, ctx_index * local, local, block)
    all_seq = sequence_rows(order_flat, 0, total, block)
    flat_in = tokens.astype(f32)
    normed_full, unit_in, inv_in = norm_forward(flat_in, norm_in)
    normed_in = normed_full.astype(low)
    queries = jnp.dot(normed_in, full_query, preferred_element_type=f32).reshape(local, H, HD)
    keys_raw = jnp.dot(normed_in, full_key, preferred_element_type=f32)
    values = jnp.dot(normed_in, full_value, preferred_element_type=f32).astype(low)
    query_normed, query_unit, query_inv = norm_forward(queries, norm_query)
    key_normed, key_unit, key_inv = norm_forward(keys_raw, norm_key)
    cosine, sine = rope_tables(positions[0], HD)
    scale = HD ** (-0.5)
    query_rot = (rotate(query_normed, cosine[:, None, :], sine[:, None, :]) * scale).astype(low)
    key_rot = rotate(key_normed, cosine, sine).astype(low)
    kv_all = a2a_gather(jnp.concatenate([key_rot, values], axis=1), "ctx", parts)
    key_all = kv_all[:, :HD]
    value_all = kv_all[:, HD:]
    scores = jnp.einsum("qhd,kd->hqk", query_rot, key_all, preferred_element_type=f32)
    allowed = my_seq[:, None] >= all_seq[None, :]
    scores = jnp.where(allowed[None], scores, -jnp.inf)
    highest = jnp.max(scores, axis=-1, keepdims=True)
    log_total = highest + jnp.log(jnp.sum(jnp.exp(scores - highest), axis=-1, keepdims=True))
    probs_full = jnp.exp(scores - log_total)
    probs = probs_full.astype(low)
    attended = (
        jnp.einsum("hqk,kd->qhd", probs, value_all, preferred_element_type=f32)
        .reshape(local, H * HD)
        .astype(low)
    )
    branch_attn = jnp.einsum("tc,dc->td", attended, full_output_t, preferred_element_type=f32)
    attn_normed, attn_unit, attn_inv = norm_forward(branch_attn, norm_attn)
    residual = flat_in + attn_normed
    pre_full, pre_unit, pre_inv = norm_forward(residual, norm_pre)
    normed_pre = pre_full.astype(low)
    rows_all = a2a_gather(normed_pre, "fsdp", groups)
    gate = jnp.einsum("td,fd->tf", rows_all, w_gate, preferred_element_type=f32)
    upper = jnp.einsum("td,fd->tf", rows_all, w_up, preferred_element_type=f32)
    gelu_value, gelu_slope = gelu_pair(gate)
    hidden = (gelu_value * upper).astype(low)
    branch_ffn = a2a_sum(
        jnp.dot(hidden, w_down, preferred_element_type=f32).astype(jnp.bfloat16), "fsdp", groups
    )
    post_normed, post_unit, post_inv = norm_forward(branch_ffn, norm_post)
    outputs = (residual + post_normed).astype(low)
    grad_out = out_grad[0].astype(f32)
    grad_ffn_full, grad_gain_post = norm_backward(grad_out, post_unit, post_inv, norm_post)
    grad_ffn = grad_ffn_full.astype(low)
    grad_all = a2a_gather(grad_ffn, "fsdp", groups)
    grad_hidden = jnp.einsum("td,fd->tf", grad_all, w_down, preferred_element_type=f32)
    grad_gate = (grad_hidden * upper * gelu_slope).astype(low)
    grad_up = (grad_hidden * gelu_value).astype(low)
    shard_gate = jnp.einsum("tf,td->fd", grad_gate, rows_all, preferred_element_type=f32)
    shard_up = jnp.einsum("tf,td->fd", grad_up, rows_all, preferred_element_type=f32)
    shard_down = jnp.einsum("tf,td->fd", hidden, grad_all, preferred_element_type=f32)
    grad_pre = a2a_sum(
        (
            jnp.dot(grad_gate, w_gate, preferred_element_type=f32)
            + jnp.dot(grad_up, w_up, preferred_element_type=f32)
        ).astype(jnp.bfloat16),
        "fsdp",
        groups,
    )
    grad_from_pre, grad_gain_pre = norm_backward(grad_pre, pre_unit, pre_inv, norm_pre)
    grad_residual = grad_out + grad_from_pre
    grad_branch_full, grad_gain_attn = norm_backward(grad_residual, attn_unit, attn_inv, norm_attn)
    grad_branch = grad_branch_full.astype(low)
    term_output = jnp.einsum("tc,td->cd", attended, grad_branch, preferred_element_type=f32)
    grad_attended = jnp.einsum(
        "td,dc->tc", grad_branch, full_output_t, preferred_element_type=f32
    ).astype(low)
    grad_heads = grad_attended.reshape(local, H, HD)
    attended_heads = attended.reshape(local, H, HD)
    delta = jnp.transpose(jnp.sum(grad_heads.astype(f32) * attended_heads.astype(f32), axis=-1))[
        :, :, None
    ]
    grad_probs = jnp.einsum("qhd,kd->hqk", grad_heads, value_all, preferred_element_type=f32)
    grad_scores = (probs_full * (grad_probs - delta)).astype(low)
    value_term = jnp.einsum("hqk,qhd->kd", probs, grad_heads, preferred_element_type=f32)
    key_term = jnp.einsum("hqk,qhd->kd", grad_scores, query_rot, preferred_element_type=f32)
    key_value_terms = jnp.concatenate([key_term, value_term], axis=1)
    grad_query_rot = jnp.einsum("hqk,kd->qhd", grad_scores, key_all, preferred_element_type=f32)
    summed_kv = a2a_sum(key_value_terms.astype(jnp.bfloat16), "ctx", parts)
    grad_key_rot = summed_kv[:, :HD]
    grad_values = summed_kv[:, HD:].astype(low)
    grad_q_normed = rotate_back(grad_query_rot * scale, cosine[:, None, :], sine[:, None, :])
    grad_q_full, grad_gain_query = norm_backward(grad_q_normed, query_unit, query_inv, norm_query)
    grad_k_normed = rotate_back(grad_key_rot, cosine, sine)
    grad_k_full, grad_gain_key = norm_backward(grad_k_normed, key_unit, key_inv, norm_key)
    grad_q_in = grad_q_full.reshape(local, H * HD).astype(low)
    grad_k_in = grad_k_full.astype(low)
    term_query = jnp.einsum("tc,td->cd", grad_q_in, normed_in, preferred_element_type=f32)
    term_key = jnp.einsum("tc,td->cd", grad_k_in, normed_in, preferred_element_type=f32)
    term_value = jnp.einsum("tc,td->cd", grad_values, normed_in, preferred_element_type=f32)
    grad_normed = (
        jnp.einsum("tc,dc->td", grad_q_in, full_query, preferred_element_type=f32)
        + jnp.einsum("tc,dc->td", grad_k_in, full_key, preferred_element_type=f32)
        + jnp.einsum("tc,dc->td", grad_values, full_value, preferred_element_type=f32)
    )
    grad_from_in, grad_gain_in = norm_backward(grad_normed, unit_in, inv_in, norm_in)
    in_grad = (grad_residual + grad_from_in).astype(low)

    def head_col(g):
        return jnp.pad(g.reshape(groups, head_shard), ((0, 0), (0, width_shard - head_shard))).reshape(-1)

    gain_block = jnp.stack(
        [
            grad_gain_in,
            grad_gain_attn,
            grad_gain_pre,
            grad_gain_post,
            head_col(grad_gain_query),
            head_col(grad_gain_key),
        ],
        axis=0,
    )
    gain_block = jnp.pad(gain_block, ((0, 8 - gain_block.shape[0]), (0, 0))).astype(low)
    gain_block = jnp.transpose(gain_block.reshape(8, groups, width_shard), (1, 0, 2))
    gain_shard = jnp.sum(lax.all_to_all(gain_block, "fsdp", 0, 0).astype(f32), axis=0)

    def ctx_sum(x):
        chunks = x.reshape(parts, -1, x.shape[1])
        mine = jnp.sum(lax.all_to_all(chunks, "ctx", 0, 0).astype(f32), axis=0).astype(low)
        return lax.all_to_all(jnp.broadcast_to(mine[None], chunks.shape), "ctx", 0, 0).reshape(x.shape)

    ffn_units = shard_gate.shape[0]
    ffn_sums = ctx_sum(
        jnp.concatenate([shard_gate, shard_up, shard_down], axis=0).astype(low)
    ).astype(f32)
    grad_packed = jnp.concatenate([term_query, term_key, term_value, term_output], axis=0).astype(low)
    grad_shard = jnp.concatenate(
        [
            lax.psum_scatter(grad_packed, "fsdp", scatter_dimension=1, tiled=True),
            gain_shard.astype(low),
        ],
        axis=0,
    )
    totals = (
        ctx_sum(grad_shard),
        ffn_sums[:ffn_units],
        ffn_sums[ffn_units : 2 * ffn_units],
        ffn_sums[2 * ffn_units :],
    )
    grad_shard = totals[0].astype(f32)
    grows = grad_shard[o4:]
    return (
        outputs[None],
        in_grad[None],
        grad_shard[:o1].T,
        grad_shard[o1:o2].T,
        grad_shard[o2:o3].T,
        grad_shard[o3:o4],
        totals[1].astype(f32),
        totals[2].astype(f32),
        totals[3].astype(f32),
        grows[0],
        grows[4, :head_shard],
        grows[5, :head_shard],
        grows[1],
        grows[2],
        grows[3],
    )


def solution(mesh):
    placed = (
        P("fsdp", "ctx", None),
        P("fsdp", "ctx", None),
        P("fsdp", "ctx"),
        P(),
        P("fsdp", None),
        P("fsdp", None),
        P("fsdp", None),
        P(None, "fsdp"),
        P("fsdp", None),
        P("fsdp", None),
        P("fsdp", None),
        P("fsdp"),
        P("fsdp"),
        P("fsdp"),
        P("fsdp"),
        P("fsdp"),
        P("fsdp"),
    )
    return jax.shard_map(
        body,
        mesh=mesh,
        in_specs=placed,
        out_specs=(
            P("fsdp", "ctx", None),
            P("fsdp", "ctx", None),
            P("fsdp", None),
            P("fsdp", None),
            P("fsdp", None),
            P(None, "fsdp"),
            P("fsdp", None),
            P("fsdp", None),
            P("fsdp", None),
            P("fsdp"),
            P("fsdp"),
            P("fsdp"),
            P("fsdp"),
            P("fsdp"),
            P("fsdp"),
        ),
        check_vma=False,
    )
```

```python
import jax
import jax.numpy as jnp
from jax import lax
from jax.sharding import PartitionSpec as P

H = 4
HD = 256


EPS = 1e-06
ROPE_BASE = 1000000.0
GELU_C = 0.7978845608028654
GELU_A = 0.044715


def norm_forward(values, gain):
    inverse = lax.rsqrt(jnp.mean(values * values, axis=-1, keepdims=True) + EPS)
    unit = values * inverse
    return (unit * gain, unit, inverse)


def norm_backward(upstream, unit, inverse, gain):
    scaled = upstream * gain
    inner = jnp.mean(scaled * unit, axis=-1, keepdims=True)
    leading = tuple(range(upstream.ndim - 1))
    return (inverse * (scaled - unit * inner), jnp.sum(upstream * unit, axis=leading))


def gelu_pair(gate):
    inner = GELU_C * (gate + GELU_A * gate * gate * gate)
    tangent = jnp.tanh(inner)
    value = 0.5 * gate * (1.0 + tangent)
    slope = 0.5 * (1.0 + tangent) + 0.5 * gate * (1.0 - tangent * tangent) * GELU_C * (
        1.0 + 3.0 * GELU_A * gate * gate
    )
    return (value, slope)


def rope_tables(positions, width):
    half = width // 2
    freqs = ROPE_BASE ** (-2.0 * jnp.arange(half, dtype=jnp.float32) / width)
    angles = positions.astype(jnp.float32)[:, None] * freqs[None, :]
    return (jnp.cos(angles), jnp.sin(angles))


def rotate(values, cosine, sine):
    half = values.shape[-1] // 2
    first = values[..., :half]
    second = values[..., half:]
    return jnp.concatenate(
        [first * cosine - second * sine, second * cosine + first * sine], axis=-1
    )


def rotate_back(values, cosine, sine):
    half = values.shape[-1] // 2
    first = values[..., :half]
    second = values[..., half:]
    return jnp.concatenate(
        [first * cosine + second * sine, second * cosine - first * sine], axis=-1
    )


def sequence_rows(order_flat, first_row, count, block):
    rows = first_row + jnp.arange(count, dtype=jnp.int32)
    slots = rows // block
    table = jnp.arange(order_flat.shape[0], dtype=jnp.int32)
    picked = jnp.sum(jnp.where(slots[:, None] == table[None, :], order_flat[None, :], 0), axis=1)
    return picked * block + rows % block


def pad_rows(shard, rows):
    return jnp.pad(shard, (0, rows - shard.shape[0]))


def a2a_sum(x, axis_name, count):
    pieces = lax.all_to_all(x.reshape(count, -1, *x.shape[1:]), axis_name, 0, 0)
    return jnp.sum(pieces.astype(jnp.float32), axis=0)


def a2a_gather(x, axis_name, count):
    copies = jnp.broadcast_to(x[None], (count,) + x.shape)
    return lax.all_to_all(copies, axis_name, 0, 0).reshape(count * x.shape[0], *x.shape[1:])


def body(
    inputs,
    out_grad,
    positions,
    block_order,
    w_query,
    w_key,
    w_value,
    w_output,
    w_gate,
    w_up,
    w_down,
    gain_in,
    gain_query,
    gain_key,
    gain_attn,
    gain_pre,
    gain_post,
):
    f32 = jnp.float32
    low = jnp.bfloat16
    tokens = inputs[0]
    local = tokens.shape[0]
    parts = lax.axis_size("ctx")
    groups = lax.axis_size("fsdp")
    total = local * parts
    block = local // 2
    width_shard = w_query.shape[0]
    qw = w_query.shape[1]
    kw = w_key.shape[1]
    gain_cols = jnp.stack(
        [
            gain_in,
            gain_attn,
            gain_pre,
            gain_post,
            pad_rows(gain_query, width_shard),
            pad_rows(gain_key, width_shard),
        ],
        axis=1,
    )
    gain_cols = jnp.pad(gain_cols, ((0, 0), (0, 128 - gain_cols.shape[1])))
    packed = jnp.concatenate([w_query, w_key, w_value, w_output.T, gain_cols], axis=1)
    packed_all = lax.all_gather(packed, "fsdp", axis=0, tiled=True)
    o1 = qw
    o2 = o1 + kw
    o3 = o2 + kw
    o4 = o3 + w_output.shape[0]
    full_query = packed_all[:, :o1]
    full_key = packed_all[:, o1:o2]
    full_value = packed_all[:, o2:o3]
    full_output_t = packed_all[:, o3:o4]
    gains_all = packed_all[:, o4:].astype(f32)
    head_shard = gain_query.shape[0]

    def head_gain(col):
        return col.reshape(groups, width_shard)[:, :head_shard].reshape(-1)

    norm_in = gains_all[:, 0]
    norm_attn = gains_all[:, 1]
    norm_pre = gains_all[:, 2]
    norm_post = gains_all[:, 3]
    norm_query = head_gain(gains_all[:, 4])
    norm_key = head_gain(gains_all[:, 5])
    ctx_index = lax.axis_index("ctx")
    order_flat = block_order.reshape(-1)
    my_seq = sequence_rows(order_flat, ctx_index * local, local, block)
    all_seq = sequence_rows(order_flat, 0, total, block)
    flat_in = tokens.astype(f32)
    normed_full, unit_in, inv_in = norm_forward(flat_in, norm_in)
    normed_in = normed_full.astype(low)
    queries = jnp.dot(normed_in, full_query, preferred_element_type=f32).reshape(local, H, HD)
    keys_raw = jnp.dot(normed_in, full_key, preferred_element_type=f32)
    values = jnp.dot(normed_in, full_value, preferred_element_type=f32).astype(low)
    query_normed, query_unit, query_inv = norm_forward(queries, norm_query)
    key_normed, key_unit, key_inv = norm_forward(keys_raw, norm_key)
    cosine, sine = rope_tables(positions[0], HD)
    scale = HD ** (-0.5)
    query_rot = (rotate(query_normed, cosine[:, None, :], sine[:, None, :]) * scale).astype(low)
    key_rot = rotate(key_normed, cosine, sine).astype(low)
    kv_all = a2a_gather(jnp.concatenate([key_rot, values], axis=1), "ctx", parts)
    key_all = kv_all[:, :HD]
    value_all = kv_all[:, HD:]
    scores = jnp.einsum("qhd,kd->hqk", query_rot, key_all, preferred_element_type=f32)
    allowed = my_seq[:, None] >= all_seq[None, :]
    scores = jnp.where(allowed[None], scores, -jnp.inf)
    highest = jnp.max(scores, axis=-1, keepdims=True)
    log_total = highest + jnp.log(jnp.sum(jnp.exp(scores - highest), axis=-1, keepdims=True))
    probs_full = jnp.exp(scores - log_total)
    probs = probs_full.astype(low)
    attended = (
        jnp.einsum("hqk,kd->qhd", probs, value_all, preferred_element_type=f32)
        .reshape(local, H * HD)
        .astype(low)
    )
    branch_attn = jnp.einsum("tc,dc->td", attended, full_output_t, preferred_element_type=f32)
    attn_normed, attn_unit, attn_inv = norm_forward(branch_attn, norm_attn)
    residual = flat_in + attn_normed
    pre_full, pre_unit, pre_inv = norm_forward(residual, norm_pre)
    normed_pre = pre_full.astype(low)
    rows_all = lax.all_gather(normed_pre, "fsdp", axis=0, tiled=True)
    gate = jnp.einsum("td,fd->tf", rows_all, w_gate, preferred_element_type=f32)
    upper = jnp.einsum("td,fd->tf", rows_all, w_up, preferred_element_type=f32)
    gelu_value, gelu_slope = gelu_pair(gate)
    hidden = (gelu_value * upper).astype(low)
    branch_ffn = a2a_sum(
        jnp.dot(hidden, w_down, preferred_element_type=f32).astype(jnp.bfloat16), "fsdp", groups
    )
    post_normed, post_unit, post_inv = norm_forward(branch_ffn, norm_post)
    outputs = (residual + post_normed).astype(low)
    grad_out = out_grad[0].astype(f32)
    grad_ffn_full, grad_gain_post = norm_backward(grad_out, post_unit, post_inv, norm_post)
    grad_ffn = grad_ffn_full.astype(low)
    grad_all = lax.all_gather(grad_ffn, "fsdp", axis=0, tiled=True)
    grad_hidden = jnp.einsum("td,fd->tf", grad_all, w_down, preferred_element_type=f32)
    grad_gate = (grad_hidden * upper * gelu_slope).astype(low)
    grad_up = (grad_hidden * gelu_value).astype(low)
    shard_gate = jnp.einsum("tf,td->fd", grad_gate, rows_all, preferred_element_type=f32)
    shard_up = jnp.einsum("tf,td->fd", grad_up, rows_all, preferred_element_type=f32)
    shard_down = jnp.einsum("tf,td->fd", hidden, grad_all, preferred_element_type=f32)
    grad_pre = a2a_sum(
        (
            jnp.dot(grad_gate, w_gate, preferred_element_type=f32)
            + jnp.dot(grad_up, w_up, preferred_element_type=f32)
        ).astype(jnp.bfloat16),
        "fsdp",
        groups,
    )
    grad_from_pre, grad_gain_pre = norm_backward(grad_pre, pre_unit, pre_inv, norm_pre)
    grad_residual = grad_out + grad_from_pre
    grad_branch_full, grad_gain_attn = norm_backward(grad_residual, attn_unit, attn_inv, norm_attn)
    grad_branch = grad_branch_full.astype(low)
    term_output = jnp.einsum("tc,td->cd", attended, grad_branch, preferred_element_type=f32)
    grad_attended = jnp.einsum(
        "td,dc->tc", grad_branch, full_output_t, preferred_element_type=f32
    ).astype(low)
    grad_heads = grad_attended.reshape(local, H, HD)
    attended_heads = attended.reshape(local, H, HD)
    delta = jnp.transpose(jnp.sum(grad_heads.astype(f32) * attended_heads.astype(f32), axis=-1))[
        :, :, None
    ]
    grad_probs = jnp.einsum("qhd,kd->hqk", grad_heads, value_all, preferred_element_type=f32)
    grad_scores = (probs_full * (grad_probs - delta)).astype(low)
    value_term = jnp.einsum("hqk,qhd->kd", probs, grad_heads, preferred_element_type=f32)
    key_term = jnp.einsum("hqk,qhd->kd", grad_scores, query_rot, preferred_element_type=f32)
    key_value_terms = jnp.concatenate([key_term, value_term], axis=1)
    grad_query_rot = jnp.einsum("hqk,kd->qhd", grad_scores, key_all, preferred_element_type=f32)
    summed_kv = a2a_sum(key_value_terms.astype(jnp.bfloat16), "ctx", parts)
    grad_key_rot = summed_kv[:, :HD]
    grad_values = summed_kv[:, HD:].astype(low)
    grad_q_normed = rotate_back(grad_query_rot * scale, cosine[:, None, :], sine[:, None, :])
    grad_q_full, grad_gain_query = norm_backward(grad_q_normed, query_unit, query_inv, norm_query)
    grad_k_normed = rotate_back(grad_key_rot, cosine, sine)
    grad_k_full, grad_gain_key = norm_backward(grad_k_normed, key_unit, key_inv, norm_key)
    grad_q_in = grad_q_full.reshape(local, H * HD).astype(low)
    grad_k_in = grad_k_full.astype(low)
    term_qkv = jnp.einsum(
        "tc,td->cd",
        jnp.concatenate([grad_q_in, grad_k_in, grad_values], axis=1),
        normed_in,
        preferred_element_type=f32,
    )
    grad_normed = (
        jnp.einsum("tc,dc->td", grad_q_in, full_query, preferred_element_type=f32)
        + jnp.einsum("tc,dc->td", grad_k_in, full_key, preferred_element_type=f32)
        + jnp.einsum("tc,dc->td", grad_values, full_value, preferred_element_type=f32)
    )
    grad_from_in, grad_gain_in = norm_backward(grad_normed, unit_in, inv_in, norm_in)
    in_grad = (grad_residual + grad_from_in).astype(low)

    def head_col(g):
        return jnp.pad(g.reshape(groups, head_shard), ((0, 0), (0, width_shard - head_shard))).reshape(-1)

    gain_block = jnp.stack(
        [
            grad_gain_in,
            grad_gain_attn,
            grad_gain_pre,
            grad_gain_post,
            head_col(grad_gain_query),
            head_col(grad_gain_key),
        ],
        axis=0,
    )
    gain_block = jnp.pad(gain_block, ((0, 8 - gain_block.shape[0]), (0, 0))).astype(low)
    gain_block = jnp.transpose(gain_block.reshape(8, groups, width_shard), (1, 0, 2))
    gain_shard = jnp.sum(lax.all_to_all(gain_block, "fsdp", 0, 0).astype(f32), axis=0)

    def ctx_sum(x):
        chunks = x.reshape(parts, -1, x.shape[1])
        mine = jnp.sum(lax.all_to_all(chunks, "ctx", 0, 0).astype(f32), axis=0).astype(low)
        return lax.all_to_all(jnp.broadcast_to(mine[None], chunks.shape), "ctx", 0, 0).reshape(x.shape)

    ffn_units = shard_gate.shape[0]
    ffn_sums = ctx_sum(
        jnp.concatenate([shard_gate, shard_up, shard_down], axis=0).astype(low)
    ).astype(f32)
    grad_packed = jnp.concatenate([term_qkv, term_output], axis=0).astype(low)
    grad_shard = jnp.concatenate(
        [
            lax.psum_scatter(grad_packed, "fsdp", scatter_dimension=1, tiled=True),
            gain_shard.astype(low),
        ],
        axis=0,
    )
    totals = (
        ctx_sum(grad_shard),
        ffn_sums[:ffn_units],
        ffn_sums[ffn_units : 2 * ffn_units],
        ffn_sums[2 * ffn_units :],
    )
    grad_shard = totals[0].astype(f32)
    grows = grad_shard[o4:]
    return (
        outputs[None],
        in_grad[None],
        grad_shard[:o1].T,
        grad_shard[o1:o2].T,
        grad_shard[o2:o3].T,
        grad_shard[o3:o4],
        totals[1].astype(f32),
        totals[2].astype(f32),
        totals[3].astype(f32),
        grows[0],
        grows[4, :head_shard],
        grows[5, :head_shard],
        grows[1],
        grows[2],
        grows[3],
    )


def solution(mesh):
    placed = (
        P("fsdp", "ctx", None),
        P("fsdp", "ctx", None),
        P("fsdp", "ctx"),
        P(),
        P("fsdp", None),
        P("fsdp", None),
        P("fsdp", None),
        P(None, "fsdp"),
        P("fsdp", None),
        P("fsdp", None),
        P("fsdp", None),
        P("fsdp"),
        P("fsdp"),
        P("fsdp"),
        P("fsdp"),
        P("fsdp"),
        P("fsdp"),
    )
    return jax.shard_map(
        body,
        mesh=mesh,
        in_specs=placed,
        out_specs=(
            P("fsdp", "ctx", None),
            P("fsdp", "ctx", None),
            P("fsdp", None),
            P("fsdp", None),
            P("fsdp", None),
            P(None, "fsdp"),
            P("fsdp", None),
            P("fsdp", None),
            P("fsdp", None),
            P("fsdp"),
            P("fsdp"),
            P("fsdp"),
            P("fsdp"),
            P("fsdp"),
            P("fsdp"),
        ),
        check_vma=False,
    )
```

```python
import jax
import jax.numpy as jnp
from jax import lax
from jax.sharding import PartitionSpec as P

H = 4
HD = 256


EPS = 1e-06
ROPE_BASE = 1000000.0
GELU_C = 0.7978845608028654
GELU_A = 0.044715


def norm_forward(values, gain):
    inverse = lax.rsqrt(jnp.mean(values * values, axis=-1, keepdims=True) + EPS)
    unit = values * inverse
    return (unit * gain, unit, inverse)


def norm_backward(upstream, unit, inverse, gain):
    scaled = upstream * gain
    inner = jnp.mean(scaled * unit, axis=-1, keepdims=True)
    leading = tuple(range(upstream.ndim - 1))
    return (inverse * (scaled - unit * inner), jnp.sum(upstream * unit, axis=leading))


def gelu_pair(gate):
    inner = GELU_C * (gate + GELU_A * gate * gate * gate)
    tangent = jnp.tanh(inner)
    value = 0.5 * gate * (1.0 + tangent)
    slope = 0.5 * (1.0 + tangent) + 0.5 * gate * (1.0 - tangent * tangent) * GELU_C * (
        1.0 + 3.0 * GELU_A * gate * gate
    )
    return (value, slope)


def rope_tables(positions, width):
    half = width // 2
    freqs = ROPE_BASE ** (-2.0 * jnp.arange(half, dtype=jnp.float32) / width)
    angles = positions.astype(jnp.float32)[:, None] * freqs[None, :]
    return (jnp.cos(angles), jnp.sin(angles))


def rotate(values, cosine, sine):
    half = values.shape[-1] // 2
    first = values[..., :half]
    second = values[..., half:]
    return jnp.concatenate(
        [first * cosine - second * sine, second * cosine + first * sine], axis=-1
    )


def rotate_back(values, cosine, sine):
    half = values.shape[-1] // 2
    first = values[..., :half]
    second = values[..., half:]
    return jnp.concatenate(
        [first * cosine + second * sine, second * cosine - first * sine], axis=-1
    )


def sequence_rows(order_flat, first_row, count, block):
    rows = first_row + jnp.arange(count, dtype=jnp.int32)
    slots = rows // block
    table = jnp.arange(order_flat.shape[0], dtype=jnp.int32)
    picked = jnp.sum(jnp.where(slots[:, None] == table[None, :], order_flat[None, :], 0), axis=1)
    return picked * block + rows % block


def pad_rows(shard, rows):
    return jnp.pad(shard, (0, rows - shard.shape[0]))


def a2a_sum(x, axis_name, count):
    pieces = lax.all_to_all(x.reshape(count, -1, *x.shape[1:]), axis_name, 0, 0)
    return jnp.sum(pieces.astype(jnp.float32), axis=0)


def a2a_gather(x, axis_name, count):
    copies = jnp.broadcast_to(x[None], (count,) + x.shape)
    return lax.all_to_all(copies, axis_name, 0, 0).reshape(count * x.shape[0], *x.shape[1:])


def body(
    inputs,
    out_grad,
    positions,
    block_order,
    w_query,
    w_key,
    w_value,
    w_output,
    w_gate,
    w_up,
    w_down,
    gain_in,
    gain_query,
    gain_key,
    gain_attn,
    gain_pre,
    gain_post,
):
    f32 = jnp.float32
    low = jnp.bfloat16
    tokens = inputs[0]
    local = tokens.shape[0]
    parts = lax.axis_size("ctx")
    groups = lax.axis_size("fsdp")
    total = local * parts
    block = local // 2
    width_shard = w_query.shape[0]
    qw = w_query.shape[1]
    kw = w_key.shape[1]
    gain_cols = jnp.stack(
        [
            gain_in,
            gain_attn,
            gain_pre,
            gain_post,
            pad_rows(gain_query, width_shard),
            pad_rows(gain_key, width_shard),
        ],
        axis=1,
    )
    gain_cols = jnp.pad(gain_cols, ((0, 0), (0, 128 - gain_cols.shape[1])))
    packed = jnp.concatenate([w_query, w_key, w_value, w_output.T, gain_cols], axis=1)
    packed_all = lax.all_gather(packed, "fsdp", axis=0, tiled=True)
    o1 = qw
    o2 = o1 + kw
    o3 = o2 + kw
    o4 = o3 + w_output.shape[0]
    full_query = packed_all[:, :o1]
    full_key = packed_all[:, o1:o2]
    full_value = packed_all[:, o2:o3]
    full_output_t = packed_all[:, o3:o4]
    gains_all = packed_all[:, o4:].astype(f32)
    head_shard = gain_query.shape[0]

    def head_gain(col):
        return col.reshape(groups, width_shard)[:, :head_shard].reshape(-1)

    norm_in = gains_all[:, 0]
    norm_attn = gains_all[:, 1]
    norm_pre = gains_all[:, 2]
    norm_post = gains_all[:, 3]
    norm_query = head_gain(gains_all[:, 4])
    norm_key = head_gain(gains_all[:, 5])
    ctx_index = lax.axis_index("ctx")
    order_flat = block_order.reshape(-1)
    my_seq = sequence_rows(order_flat, ctx_index * local, local, block)
    all_seq = sequence_rows(order_flat, 0, total, block)
    flat_in = tokens.astype(f32)
    normed_full, unit_in, inv_in = norm_forward(flat_in, norm_in)
    normed_in = normed_full.astype(low)
    queries = jnp.dot(normed_in, full_query, preferred_element_type=f32).reshape(local, H, HD)
    keys_raw = jnp.dot(normed_in, full_key, preferred_element_type=f32)
    values = jnp.dot(normed_in, full_value, preferred_element_type=f32).astype(low)
    query_normed, query_unit, query_inv = norm_forward(queries, norm_query)
    key_normed, key_unit, key_inv = norm_forward(keys_raw, norm_key)
    cosine, sine = rope_tables(positions[0], HD)
    scale = HD ** (-0.5)
    query_rot = (rotate(query_normed, cosine[:, None, :], sine[:, None, :]) * scale).astype(low)
    key_rot = rotate(key_normed, cosine, sine).astype(low)
    kv_all = a2a_gather(jnp.concatenate([key_rot, values], axis=1), "ctx", parts)
    key_all = kv_all[:, :HD]
    value_all = kv_all[:, HD:]
    scores = jnp.einsum("qhd,kd->hqk", query_rot, key_all, preferred_element_type=f32)
    allowed = my_seq[:, None] >= all_seq[None, :]
    scores = jnp.where(allowed[None], scores, -jnp.inf)
    highest = jnp.max(scores, axis=-1, keepdims=True)
    log_total = highest + jnp.log(jnp.sum(jnp.exp(scores - highest), axis=-1, keepdims=True))
    probs_full = jnp.exp(scores - log_total)
    probs = probs_full.astype(low)
    attended = (
        jnp.einsum("hqk,kd->qhd", probs, value_all, preferred_element_type=f32)
        .reshape(local, H * HD)
        .astype(low)
    )
    branch_attn = jnp.einsum("tc,dc->td", attended, full_output_t, preferred_element_type=f32)
    attn_normed, attn_unit, attn_inv = norm_forward(branch_attn, norm_attn)
    residual = flat_in + attn_normed
    pre_full, pre_unit, pre_inv = norm_forward(residual, norm_pre)
    normed_pre = pre_full.astype(low)
    rows_all = lax.all_gather(normed_pre, "fsdp", axis=0, tiled=True)
    gate = jnp.einsum("td,fd->tf", rows_all, w_gate, preferred_element_type=f32)
    upper = jnp.einsum("td,fd->tf", rows_all, w_up, preferred_element_type=f32)
    gelu_value, gelu_slope = gelu_pair(gate)
    hidden = (gelu_value * upper).astype(low)
    branch_ffn = a2a_sum(
        jnp.dot(hidden, w_down, preferred_element_type=f32).astype(jnp.bfloat16), "fsdp", groups
    )
    post_normed, post_unit, post_inv = norm_forward(branch_ffn, norm_post)
    outputs = (residual + post_normed).astype(low)
    grad_out = out_grad[0].astype(f32)
    grad_ffn_full, grad_gain_post = norm_backward(grad_out, post_unit, post_inv, norm_post)
    grad_ffn = grad_ffn_full.astype(low)
    grad_all = lax.all_gather(grad_ffn, "fsdp", axis=0, tiled=True)
    grad_hidden = jnp.einsum("td,fd->tf", grad_all, w_down, preferred_element_type=f32)
    grad_gate = (grad_hidden * upper * gelu_slope).astype(low)
    grad_up = (grad_hidden * gelu_value).astype(low)
    shard_gate = jnp.einsum("tf,td->fd", grad_gate, rows_all, preferred_element_type=f32)
    shard_up = jnp.einsum("tf,td->fd", grad_up, rows_all, preferred_element_type=f32)
    shard_down = jnp.einsum("tf,td->fd", hidden, grad_all, preferred_element_type=f32)
    grad_pre = a2a_sum(
        (
            jnp.dot(grad_gate, w_gate, preferred_element_type=f32)
            + jnp.dot(grad_up, w_up, preferred_element_type=f32)
        ).astype(jnp.bfloat16),
        "fsdp",
        groups,
    )
    grad_from_pre, grad_gain_pre = norm_backward(grad_pre, pre_unit, pre_inv, norm_pre)
    grad_residual = grad_out + grad_from_pre
    grad_branch_full, grad_gain_attn = norm_backward(grad_residual, attn_unit, attn_inv, norm_attn)
    grad_branch = grad_branch_full.astype(low)
    term_output = jnp.einsum("tc,td->cd", attended, grad_branch, preferred_element_type=f32)
    grad_attended = jnp.einsum(
        "td,dc->tc", grad_branch, full_output_t, preferred_element_type=f32
    ).astype(low)
    grad_heads = grad_attended.reshape(local, H, HD)
    attended_heads = attended.reshape(local, H, HD)
    delta = jnp.transpose(jnp.sum(grad_heads.astype(f32) * attended_heads.astype(f32), axis=-1))[
        :, :, None
    ]
    grad_probs = jnp.einsum("qhd,kd->hqk", grad_heads, value_all, preferred_element_type=f32)
    grad_scores = (probs_full * (grad_probs - delta)).astype(low)
    value_term = jnp.einsum("hqk,qhd->kd", probs, grad_heads, preferred_element_type=f32)
    key_term = jnp.einsum("hqk,qhd->kd", grad_scores, query_rot, preferred_element_type=f32)
    key_value_terms = jnp.concatenate([key_term, value_term], axis=1)
    grad_query_rot = jnp.einsum("hqk,kd->qhd", grad_scores, key_all, preferred_element_type=f32)
    summed_kv = a2a_sum(key_value_terms.astype(jnp.bfloat16), "ctx", parts)
    grad_key_rot = summed_kv[:, :HD]
    grad_values = summed_kv[:, HD:].astype(low)
    grad_q_normed = rotate_back(grad_query_rot * scale, cosine[:, None, :], sine[:, None, :])
    grad_q_full, grad_gain_query = norm_backward(grad_q_normed, query_unit, query_inv, norm_query)
    grad_k_normed = rotate_back(grad_key_rot, cosine, sine)
    grad_k_full, grad_gain_key = norm_backward(grad_k_normed, key_unit, key_inv, norm_key)
    grad_q_in = grad_q_full.reshape(local, H * HD).astype(low)
    grad_k_in = grad_k_full.astype(low)
    term_query = jnp.einsum("tc,td->cd", grad_q_in, normed_in, preferred_element_type=f32)
    term_key = jnp.einsum("tc,td->cd", grad_k_in, normed_in, preferred_element_type=f32)
    term_value = jnp.einsum("tc,td->cd", grad_values, normed_in, preferred_element_type=f32)
    grad_normed = (
        jnp.einsum("tc,dc->td", grad_q_in, full_query, preferred_element_type=f32)
        + jnp.einsum("tc,dc->td", grad_k_in, full_key, preferred_element_type=f32)
        + jnp.einsum("tc,dc->td", grad_values, full_value, preferred_element_type=f32)
    )
    grad_from_in, grad_gain_in = norm_backward(grad_normed, unit_in, inv_in, norm_in)
    in_grad = (grad_residual + grad_from_in).astype(low)

    def head_col(g):
        return jnp.pad(g.reshape(groups, head_shard), ((0, 0), (0, width_shard - head_shard))).reshape(-1)

    gain_block = jnp.stack(
        [
            grad_gain_in,
            grad_gain_attn,
            grad_gain_pre,
            grad_gain_post,
            head_col(grad_gain_query),
            head_col(grad_gain_key),
        ],
        axis=0,
    )
    gain_block = jnp.pad(gain_block, ((0, 8 - gain_block.shape[0]), (0, 0))).astype(low)
    gain_block = jnp.transpose(gain_block.reshape(8, groups, width_shard), (1, 0, 2))
    gain_shard = jnp.sum(lax.all_to_all(gain_block, "fsdp", 0, 0).astype(f32), axis=0)

    def ctx_sum(x):
        chunks = x.reshape(parts, -1, x.shape[1])
        mine = jnp.sum(lax.all_to_all(chunks, "ctx", 0, 0).astype(f32), axis=0).astype(low)
        return lax.all_to_all(jnp.broadcast_to(mine[None], chunks.shape), "ctx", 0, 0).reshape(x.shape)

    ffn_units = shard_gate.shape[0]
    ffn_packed = jnp.concatenate([shard_gate, shard_up, shard_down], axis=0).astype(low)
    ffn_rows = ffn_packed.shape[0]
    ffn_packed = jnp.pad(ffn_packed, ((0, -ffn_rows % (8 * parts)), (0, 0)))
    ffn_mine = a2a_sum(ffn_packed, "ctx", parts).astype(low)
    ffn_sums = lax.all_gather(ffn_mine, "ctx", axis=0, tiled=True)[:ffn_rows].astype(f32)
    grad_packed = jnp.concatenate([term_query, term_key, term_value, term_output], axis=0).astype(low)
    grad_shard = jnp.concatenate(
        [
            lax.psum_scatter(grad_packed, "fsdp", scatter_dimension=1, tiled=True),
            gain_shard.astype(low),
        ],
        axis=0,
    )
    totals = (
        ctx_sum(grad_shard),
        ffn_sums[:ffn_units],
        ffn_sums[ffn_units : 2 * ffn_units],
        ffn_sums[2 * ffn_units :],
    )
    grad_shard = totals[0].astype(f32)
    grows = grad_shard[o4:]
    return (
        outputs[None],
        in_grad[None],
        grad_shard[:o1].T,
        grad_shard[o1:o2].T,
        grad_shard[o2:o3].T,
        grad_shard[o3:o4],
        totals[1].astype(f32),
        totals[2].astype(f32),
        totals[3].astype(f32),
        grows[0],
        grows[4, :head_shard],
        grows[5, :head_shard],
        grows[1],
        grows[2],
        grows[3],
    )


def solution(mesh):
    placed = (
        P("fsdp", "ctx", None),
        P("fsdp", "ctx", None),
        P("fsdp", "ctx"),
        P(),
        P("fsdp", None),
        P("fsdp", None),
        P("fsdp", None),
        P(None, "fsdp"),
        P("fsdp", None),
        P("fsdp", None),
        P("fsdp", None),
        P("fsdp"),
        P("fsdp"),
        P("fsdp"),
        P("fsdp"),
        P("fsdp"),
        P("fsdp"),
    )
    return jax.shard_map(
        body,
        mesh=mesh,
        in_specs=placed,
        out_specs=(
            P("fsdp", "ctx", None),
            P("fsdp", "ctx", None),
            P("fsdp", None),
            P("fsdp", None),
            P("fsdp", None),
            P(None, "fsdp"),
            P("fsdp", None),
            P("fsdp", None),
            P("fsdp", None),
            P("fsdp"),
            P("fsdp"),
            P("fsdp"),
            P("fsdp"),
            P("fsdp"),
            P("fsdp"),
        ),
        check_vma=False,
    )
```

```python
import jax
import jax.numpy as jnp
from jax import lax
from jax.sharding import PartitionSpec as P

H = 4
HD = 256


EPS = 1e-06
ROPE_BASE = 1000000.0
GELU_C = 0.7978845608028654
GELU_A = 0.044715


def norm_forward(values, gain):
    inverse = lax.rsqrt(jnp.mean(values * values, axis=-1, keepdims=True) + EPS)
    unit = values * inverse
    return (unit * gain, unit, inverse)


def norm_backward(upstream, unit, inverse, gain):
    scaled = upstream * gain
    inner = jnp.mean(scaled * unit, axis=-1, keepdims=True)
    leading = tuple(range(upstream.ndim - 1))
    return (inverse * (scaled - unit * inner), jnp.sum(upstream * unit, axis=leading))


def gelu_pair(gate):
    inner = GELU_C * (gate + GELU_A * gate * gate * gate)
    tangent = jnp.tanh(inner)
    value = 0.5 * gate * (1.0 + tangent)
    slope = 0.5 * (1.0 + tangent) + 0.5 * gate * (1.0 - tangent * tangent) * GELU_C * (
        1.0 + 3.0 * GELU_A * gate * gate
    )
    return (value, slope)


def rope_tables(positions, width):
    half = width // 2
    freqs = ROPE_BASE ** (-2.0 * jnp.arange(half, dtype=jnp.float32) / width)
    angles = positions.astype(jnp.float32)[:, None] * freqs[None, :]
    return (jnp.cos(angles), jnp.sin(angles))


def rotate(values, cosine, sine):
    half = values.shape[-1] // 2
    first = values[..., :half]
    second = values[..., half:]
    return jnp.concatenate(
        [first * cosine - second * sine, second * cosine + first * sine], axis=-1
    )


def rotate_back(values, cosine, sine):
    half = values.shape[-1] // 2
    first = values[..., :half]
    second = values[..., half:]
    return jnp.concatenate(
        [first * cosine + second * sine, second * cosine - first * sine], axis=-1
    )


def sequence_rows(order_flat, first_row, count, block):
    rows = first_row + jnp.arange(count, dtype=jnp.int32)
    slots = rows // block
    table = jnp.arange(order_flat.shape[0], dtype=jnp.int32)
    picked = jnp.sum(jnp.where(slots[:, None] == table[None, :], order_flat[None, :], 0), axis=1)
    return picked * block + rows % block


def pad_rows(shard, rows):
    return jnp.pad(shard, (0, rows - shard.shape[0]))


def a2a_sum(x, axis_name, count):
    pieces = lax.all_to_all(x.reshape(count, -1, *x.shape[1:]), axis_name, 0, 0)
    return jnp.sum(pieces.astype(jnp.float32), axis=0)


def a2a_gather(x, axis_name, count):
    copies = jnp.broadcast_to(x[None], (count,) + x.shape)
    return lax.all_to_all(copies, axis_name, 0, 0).reshape(count * x.shape[0], *x.shape[1:])


def body(
    inputs,
    out_grad,
    positions,
    block_order,
    w_query,
    w_key,
    w_value,
    w_output,
    w_gate,
    w_up,
    w_down,
    gain_in,
    gain_query,
    gain_key,
    gain_attn,
    gain_pre,
    gain_post,
):
    f32 = jnp.float32
    low = jnp.bfloat16
    tokens = inputs[0]
    local = tokens.shape[0]
    parts = lax.axis_size("ctx")
    groups = lax.axis_size("fsdp")
    total = local * parts
    block = local // 2
    width_shard = w_query.shape[0]
    qw = w_query.shape[1]
    kw = w_key.shape[1]
    gain_cols = jnp.stack(
        [
            gain_in,
            gain_attn,
            gain_pre,
            gain_post,
            pad_rows(gain_query, width_shard),
            pad_rows(gain_key, width_shard),
        ],
        axis=1,
    )
    gain_cols = jnp.pad(gain_cols, ((0, 0), (0, 128 - gain_cols.shape[1])))
    packed = jnp.concatenate([w_query, w_key, w_value, w_output.T, gain_cols], axis=1)
    packed_all = lax.all_gather(packed, "fsdp", axis=0, tiled=True)
    o1 = qw
    o2 = o1 + kw
    o3 = o2 + kw
    o4 = o3 + w_output.shape[0]
    full_query = packed_all[:, :o1]
    full_key = packed_all[:, o1:o2]
    full_value = packed_all[:, o2:o3]
    full_output_t = packed_all[:, o3:o4]
    gains_all = packed_all[:, o4:].astype(f32)
    head_shard = gain_query.shape[0]

    def head_gain(col):
        return col.reshape(groups, width_shard)[:, :head_shard].reshape(-1)

    norm_in = gains_all[:, 0]
    norm_attn = gains_all[:, 1]
    norm_pre = gains_all[:, 2]
    norm_post = gains_all[:, 3]
    norm_query = head_gain(gains_all[:, 4])
    norm_key = head_gain(gains_all[:, 5])
    ctx_index = lax.axis_index("ctx")
    order_flat = block_order.reshape(-1)
    my_seq = sequence_rows(order_flat, ctx_index * local, local, block)
    all_seq = sequence_rows(order_flat, 0, total, block)
    flat_in = tokens.astype(f32)
    normed_full, unit_in, inv_in = norm_forward(flat_in, norm_in)
    normed_in = normed_full.astype(low)
    queries = jnp.dot(normed_in, full_query, preferred_element_type=f32).reshape(local, H, HD)
    keys_raw = jnp.dot(normed_in, full_key, preferred_element_type=f32)
    values = jnp.dot(normed_in, full_value, preferred_element_type=f32).astype(low)
    query_normed, query_unit, query_inv = norm_forward(queries, norm_query)
    key_normed, key_unit, key_inv = norm_forward(keys_raw, norm_key)
    cosine, sine = rope_tables(positions[0], HD)
    scale = HD ** (-0.5)
    query_rot = (rotate(query_normed, cosine[:, None, :], sine[:, None, :]) * scale).astype(low)
    key_rot = rotate(key_normed, cosine, sine).astype(low)
    kv_all = a2a_gather(jnp.concatenate([key_rot, values], axis=1), "ctx", parts)
    key_all = kv_all[:, :HD]
    value_all = kv_all[:, HD:]
    scores = jnp.einsum("qhd,kd->hqk", query_rot, key_all, preferred_element_type=f32)
    allowed = my_seq[:, None] >= all_seq[None, :]
    scores = jnp.where(allowed[None], scores, -jnp.inf)
    highest = jnp.max(scores, axis=-1, keepdims=True)
    log_total = highest + jnp.log(jnp.sum(jnp.exp(scores - highest), axis=-1, keepdims=True))
    probs_full = jnp.exp(scores - log_total)
    probs = probs_full.astype(low)
    attended = (
        jnp.einsum("hqk,kd->qhd", probs, value_all, preferred_element_type=f32)
        .reshape(local, H * HD)
        .astype(low)
    )
    branch_attn = jnp.einsum("tc,dc->td", attended, full_output_t, preferred_element_type=f32)
    attn_normed, attn_unit, attn_inv = norm_forward(branch_attn, norm_attn)
    residual = flat_in + attn_normed
    pre_full, pre_unit, pre_inv = norm_forward(residual, norm_pre)
    normed_pre = pre_full.astype(low)
    rows_all = lax.all_gather(normed_pre, "fsdp", axis=0, tiled=True)
    gate = jnp.einsum("td,fd->tf", rows_all, w_gate, preferred_element_type=f32)
    upper = jnp.einsum("td,fd->tf", rows_all, w_up, preferred_element_type=f32)
    gelu_value, gelu_slope = gelu_pair(gate)
    hidden = (gelu_value * upper).astype(low)
    branch_ffn = a2a_sum(
        jnp.dot(hidden, w_down, preferred_element_type=f32).astype(jnp.bfloat16), "fsdp", groups
    )
    post_normed, post_unit, post_inv = norm_forward(branch_ffn, norm_post)
    outputs = (residual + post_normed).astype(low)
    grad_out = out_grad[0].astype(f32)
    grad_ffn_full, grad_gain_post = norm_backward(grad_out, post_unit, post_inv, norm_post)
    grad_ffn = grad_ffn_full.astype(low)
    grad_all = a2a_gather(grad_ffn, "fsdp", groups)
    grad_hidden = jnp.einsum("td,fd->tf", grad_all, w_down, preferred_element_type=f32)
    grad_gate = (grad_hidden * upper * gelu_slope).astype(low)
    grad_up = (grad_hidden * gelu_value).astype(low)
    shard_gate = jnp.einsum("tf,td->fd", grad_gate, rows_all, preferred_element_type=f32)
    shard_up = jnp.einsum("tf,td->fd", grad_up, rows_all, preferred_element_type=f32)
    shard_down = jnp.einsum("tf,td->fd", hidden, grad_all, preferred_element_type=f32)
    grad_pre = a2a_sum(
        (
            jnp.dot(grad_gate, w_gate, preferred_element_type=f32)
            + jnp.dot(grad_up, w_up, preferred_element_type=f32)
        ).astype(jnp.bfloat16),
        "fsdp",
        groups,
    )
    grad_from_pre, grad_gain_pre = norm_backward(grad_pre, pre_unit, pre_inv, norm_pre)
    grad_residual = grad_out + grad_from_pre
    grad_branch_full, grad_gain_attn = norm_backward(grad_residual, attn_unit, attn_inv, norm_attn)
    grad_branch = grad_branch_full.astype(low)
    term_output = jnp.einsum("tc,td->cd", attended, grad_branch, preferred_element_type=f32)
    grad_attended = jnp.einsum(
        "td,dc->tc", grad_branch, full_output_t, preferred_element_type=f32
    ).astype(low)
    grad_heads = grad_attended.reshape(local, H, HD)
    attended_heads = attended.reshape(local, H, HD)
    delta = jnp.transpose(jnp.sum(grad_heads.astype(f32) * attended_heads.astype(f32), axis=-1))[
        :, :, None
    ]
    grad_probs = jnp.einsum("qhd,kd->hqk", grad_heads, value_all, preferred_element_type=f32)
    grad_scores = (probs_full * (grad_probs - delta)).astype(low)
    value_term = jnp.einsum("hqk,qhd->kd", probs, grad_heads, preferred_element_type=f32)
    key_term = jnp.einsum("hqk,qhd->kd", grad_scores, query_rot, preferred_element_type=f32)
    key_value_terms = jnp.concatenate([key_term, value_term], axis=1)
    grad_query_rot = jnp.einsum("hqk,kd->qhd", grad_scores, key_all, preferred_element_type=f32)
    summed_kv = a2a_sum(key_value_terms.astype(jnp.bfloat16), "ctx", parts)
    grad_key_rot = summed_kv[:, :HD]
    grad_values = summed_kv[:, HD:].astype(low)
    grad_q_normed = rotate_back(grad_query_rot * scale, cosine[:, None, :], sine[:, None, :])
    grad_q_full, grad_gain_query = norm_backward(grad_q_normed, query_unit, query_inv, norm_query)
    grad_k_normed = rotate_back(grad_key_rot, cosine, sine)
    grad_k_full, grad_gain_key = norm_backward(grad_k_normed, key_unit, key_inv, norm_key)
    grad_q_in = grad_q_full.reshape(local, H * HD).astype(low)
    grad_k_in = grad_k_full.astype(low)
    term_query = jnp.einsum("tc,td->cd", grad_q_in, normed_in, preferred_element_type=f32)
    term_key = jnp.einsum("tc,td->cd", grad_k_in, normed_in, preferred_element_type=f32)
    term_value = jnp.einsum("tc,td->cd", grad_values, normed_in, preferred_element_type=f32)
    grad_normed = (
        jnp.einsum("tc,dc->td", grad_q_in, full_query, preferred_element_type=f32)
        + jnp.einsum("tc,dc->td", grad_k_in, full_key, preferred_element_type=f32)
        + jnp.einsum("tc,dc->td", grad_values, full_value, preferred_element_type=f32)
    )
    grad_from_in, grad_gain_in = norm_backward(grad_normed, unit_in, inv_in, norm_in)
    in_grad = (grad_residual + grad_from_in).astype(low)

    def head_col(g):
        return jnp.pad(g.reshape(groups, head_shard), ((0, 0), (0, width_shard - head_shard))).reshape(-1)

    gain_block = jnp.stack(
        [
            grad_gain_in,
            grad_gain_attn,
            grad_gain_pre,
            grad_gain_post,
            head_col(grad_gain_query),
            head_col(grad_gain_key),
        ],
        axis=0,
    )
    gain_block = jnp.pad(gain_block, ((0, 8 - gain_block.shape[0]), (0, 0))).astype(low)
    gain_block = jnp.transpose(gain_block.reshape(8, groups, width_shard), (1, 0, 2))
    gain_shard = jnp.sum(lax.all_to_all(gain_block, "fsdp", 0, 0).astype(f32), axis=0)

    def ctx_sum(x):
        chunks = x.reshape(parts, -1, x.shape[1])
        mine = jnp.sum(lax.all_to_all(chunks, "ctx", 0, 0).astype(f32), axis=0).astype(low)
        return lax.all_to_all(jnp.broadcast_to(mine[None], chunks.shape), "ctx", 0, 0).reshape(x.shape)

    ffn_units = shard_gate.shape[0]
    ffn_sums = ctx_sum(
        jnp.concatenate([shard_gate, shard_up, shard_down], axis=0).astype(low)
    ).astype(f32)
    grad_packed = jnp.concatenate([term_query, term_key, term_value, term_output], axis=0).astype(low)
    grad_shard = jnp.concatenate(
        [
            lax.psum_scatter(grad_packed, "fsdp", scatter_dimension=1, tiled=True),
            gain_shard.astype(low),
        ],
        axis=0,
    )
    totals = (
        ctx_sum(grad_shard),
        ffn_sums[:ffn_units],
        ffn_sums[ffn_units : 2 * ffn_units],
        ffn_sums[2 * ffn_units :],
    )
    grad_shard = totals[0].astype(f32)
    grows = grad_shard[o4:]
    return (
        outputs[None],
        in_grad[None],
        grad_shard[:o1].T,
        grad_shard[o1:o2].T,
        grad_shard[o2:o3].T,
        grad_shard[o3:o4],
        totals[1].astype(f32),
        totals[2].astype(f32),
        totals[3].astype(f32),
        grows[0],
        grows[4, :head_shard],
        grows[5, :head_shard],
        grows[1],
        grows[2],
        grows[3],
    )


def solution(mesh):
    placed = (
        P("fsdp", "ctx", None),
        P("fsdp", "ctx", None),
        P("fsdp", "ctx"),
        P(),
        P("fsdp", None),
        P("fsdp", None),
        P("fsdp", None),
        P(None, "fsdp"),
        P("fsdp", None),
        P("fsdp", None),
        P("fsdp", None),
        P("fsdp"),
        P("fsdp"),
        P("fsdp"),
        P("fsdp"),
        P("fsdp"),
        P("fsdp"),
    )
    return jax.shard_map(
        body,
        mesh=mesh,
        in_specs=placed,
        out_specs=(
            P("fsdp", "ctx", None),
            P("fsdp", "ctx", None),
            P("fsdp", None),
            P("fsdp", None),
            P("fsdp", None),
            P(None, "fsdp"),
            P("fsdp", None),
            P("fsdp", None),
            P("fsdp", None),
            P("fsdp"),
            P("fsdp"),
            P("fsdp"),
            P("fsdp"),
            P("fsdp"),
            P("fsdp"),
        ),
        check_vma=False,
    )
```
